32 devices in a mesh: dp: 32 (over z, y, x, core).
Axes of the slice: x: 2, y: 2, z: 4, core: 2. Of those that a mesh axis runs over, the one named last changes fastest.
Arguments:
- tokens: bfloat16 [5120, 2048], P('dp'), may hold values from -6 to 6
- cotangent: bfloat16 [5120, 2048], P('dp'), may hold values from -6 to 6
- seq_lengths: int32 [5], replicated, may hold values from 1 to 2048, 5120 in all
- block_deal: int32 [32], replicated, may hold values from 0 to 31, each once
- in_proj: float32 [2048, 2048], P('dp'), may hold values from -0.125 to 0.125
- forget_proj: float32 [1024, 2048], P('dp'), may hold values from -0.125 to 0.125
- gate_proj: float32 [2048, 2048], P('dp'), may hold values from -0.125 to 0.125
- out_proj: float32 [2048, 2048], P('dp'), may hold values from -0.125 to 0.125
- ffn_gate: float32 [5632, 2048], P('dp'), may hold values from -0.125 to 0.125
- ffn_up: float32 [5632, 2048], P('dp'), may hold values from -0.125 to 0.125
- ffn_down: float32 [5632, 2048], P('dp'), may hold values from -0.078125 to 0.078125
- gain_mix: float32 [2048], P('dp'), may hold values from 0.5 to 1.5
- gain_out: float32 [2048], P('dp'), may hold values from 0.5 to 1.5
- gain_ffn: float32 [2048], P('dp'), may hold values from 0.5 to 1.5
- lower_bound: float32 [1024], P('dp'), may hold values from 0.95 to 0.9999
- rotation: float32 [1024], P('dp'), may hold values from -3.140625 to 3.140625
Outputs:
- mixed_out: bfloat16 [5120, 2048], P('dp')
- tokens_grad: bfloat16 [5120, 2048], P('dp')
- in_proj_grad: float32 [2048, 2048], P('dp')
- forget_proj_grad: float32 [1024, 2048], P('dp')
- gate_proj_grad: float32 [2048, 2048], P('dp')
- out_proj_grad: float32 [2048, 2048], P('dp')
- ffn_gate_grad: float32 [5632, 2048], P('dp')
- ffn_up_grad: float32 [5632, 2048], P('dp')
- ffn_down_grad: float32 [5632, 2048], P('dp')
- gain_mix_grad: float32 [2048], P('dp')
- gain_out_grad: float32 [2048], P('dp')
- gain_ffn_grad: float32 [2048], P('dp')
- lower_bound_grad: float32 [1024], P('dp')
- rotation_grad: float32 [1024], P('dp')
The draws below stay inside these ranges and needn't reach their ends.
Inputs may be any that keep to these rules, and one draw needn't show every extreme that they name: `seq_lengths`: the lengths sum to 5120; the longest is exactly 2048. `block_deal`: every block of the stream is held by exactly one device.
All inputs are finite; a program needn't handle non-finite values.
Results may differ from the reference program's by a relative error of at most 0.011.
Values may be sent and summed in bfloat16 or wider, within the bound.
A program may use at most 448 MiB of HBM per device.

```python
import math
import jax
import jax.numpy as jnp
import numpy as np
from jax import lax

D = 2048
FF = 5632
HALF = 1024
TOK_DEV = 160
TOKENS = 5120
MOST = 2048
SEQS = 5
BLOCKS = 32
N_DP = 32


def draw_lower_bound(key, part):
    unit = jax.random.uniform(key, (HALF,), jnp.float32)
    rate = jnp.exp(jnp.log(0.0001) + unit * (jnp.log(0.05) - jnp.log(0.0001)))
    return (1.0 - rate).astype(jnp.float32)


def levels(rng, dims, pieces, least, high):
    level, own = 1.0, jax.random.fold_in(rng, 6)
    for axis_at, blocks in pieces:
        draws = jnp.exp(jax.random.uniform(jax.random.fold_in(own, axis_at), (blocks,), jnp.float32, least / len(pieces), high / len(pieces)))
        level = level * jnp.repeat(draws, dims[axis_at] // blocks).reshape([-1 if axis == axis_at else 1 for axis in range(len(dims))])
    return level


def profile(count, total, reach, slope):
    weights = [(1 << 20) // math.isqrt(rank ** slope) + 1 for rank in range(2, count + 1)]
    surplus, holding = total - reach - (count - 1), [1] * (count - 1)
    while surplus > 0:
        candidates = [i for i in range(count - 1) if holding[i] < reach]
        pool, budget = sum([weights[i] for i in candidates]), surplus
        for i in candidates:
            addition = min(reach - holding[i], max(1, budget * weights[i] // pool), surplus)
            holding[i] = holding[i] + addition
            surplus = surplus - addition
    return np.array([reach] + holding)


def ragged(rng, amount, total, limit, skew):
    if amount == 2:
        one = jax.random.randint(rng, (), max(1, total - limit), min(limit, total - 1) + 1)
        return jnp.stack([one, total - one])
    tallies = jnp.asarray(profile(amount, total, limit, skew), jnp.int32)
    couples = (amount - 1) // 2
    source_of, taker = tallies[1:1 + 2 * couples:2], tallies[2:2 + 2 * couples:2]
    room = jnp.minimum(source_of - 1, limit - taker)
    shifted = jax.random.randint(jax.random.fold_in(rng, 1), (couples,), 0, 1 << 20) % (room + 1)
    tallies = tallies.at[1:1 + 2 * couples:2].set(source_of - shifted).at[2:2 + 2 * couples:2].set(taker + shifted)
    return tallies[jax.random.permutation(jax.random.fold_in(rng, 2), amount)]


def bell_draw(key, shape, spread, reach, pieces=(), kind=jnp.bfloat16):
    values = spread * jax.random.normal(key, shape, jnp.float32)
    if pieces:
        values = values * levels(key, shape, pieces, -0.22, 0.18)
    return jnp.clip(values, -reach, reach).astype(kind)


def setup_inputs(seed: int = 0) -> dict:
    arg_keys = jax.random.split(jax.random.key(seed), 17)
    tokens = bell_draw(arg_keys[0], (TOKENS, D), 1.0, 6.0, ((0, 32),))
    cotangent = bell_draw(arg_keys[1], (TOKENS, D), 1.0, 6.0, ((0, 32),))
    seq_lengths = ragged(arg_keys[2], SEQS, TOKENS, MOST, 2).astype(jnp.int32)
    block_deal = jax.random.permutation(arg_keys[3], BLOCKS).astype(jnp.int32)
    in_proj = bell_draw(arg_keys[4], (D, D), D ** -0.5, 0.125, ((0, 32),), jnp.float32)
    forget_proj = bell_draw(arg_keys[5], (HALF, D), D ** -0.5, 0.125, ((0, 32),), jnp.float32)
    gate_proj = bell_draw(arg_keys[6], (D, D), D ** -0.5, 0.125, ((0, 32),), jnp.float32)
    out_proj = bell_draw(arg_keys[7], (D, D), D ** -0.5, 0.125, ((0, 32),), jnp.float32)
    ffn_gate = bell_draw(arg_keys[8], (FF, D), D ** -0.5, 0.125, ((0, 32),), jnp.float32)
    ffn_up = bell_draw(arg_keys[9], (FF, D), D ** -0.5, 0.125, ((0, 32),), jnp.float32)
    ffn_down = bell_draw(arg_keys[10], (FF, D), FF ** -0.5, 0.078125, ((0, 32),), jnp.float32)
    gain_mix = jnp.clip(1.0 + 0.1 * jax.random.normal(arg_keys[11], (D,), jnp.float32), 0.5, 1.5)
    gain_out = jnp.clip(1.0 + 0.1 * jax.random.normal(arg_keys[12], (D,), jnp.float32), 0.5, 1.5)
    gain_ffn = jnp.clip(1.0 + 0.1 * jax.random.normal(arg_keys[13], (D,), jnp.float32), 0.5, 1.5)
    lower_bound = draw_lower_bound(jax.random.fold_in(arg_keys[16], 71), 0)
    rotation = jnp.clip(jax.random.uniform(arg_keys[15], (HALF,), jnp.float32, -3.140625, 3.140625), -3.140625, 3.140625)
    return dict(tokens=tokens, cotangent=cotangent, seq_lengths=seq_lengths, block_deal=block_deal, in_proj=in_proj, forget_proj=forget_proj, gate_proj=gate_proj, out_proj=out_proj, ffn_gate=ffn_gate, ffn_up=ffn_up, ffn_down=ffn_down, gain_mix=gain_mix, gain_out=gain_out, gain_ffn=gain_ffn, lower_bound=lower_bound, rotation=rotation)


EPS = 1e-06
PRECISE = lax.Precision.HIGHEST

@jax.custom_vjp
def low(v):
    return lax.optimization_barrier(v.astype(jnp.bfloat16)).astype(jnp.float32)

@jax.custom_vjp
def low_back(v):
    return v

def low_keep(v):
    return (low(v), None)

def low_pass(kept, grad):
    return (grad,)

def back_keep(v):
    return (v, None)

def back_low(kept, grad):
    return (low(grad),)
low.defvjp(low_keep, low_pass)
low_back.defvjp(back_keep, back_low)

def rms_scale(tensor, gain_vec):
    return tensor * lax.rsqrt(lax.optimization_barrier(jnp.mean(tensor * tensor, axis=-1, keepdims=True)) + EPS) * gain_vec

def project(left_rows, right_rows):
    return lax.dot_general(left_rows, right_rows, (((1,), (1,)), ((), ())), precision=PRECISE, preferred_element_type=jnp.float32)

def block_scan(carry_in, block_items):

    def advance(state_in, token_in):
        state_re, state_im = state_in
        decay_re, decay_im, drive_re, drive_im = token_in
        next_re = decay_re * state_re - decay_im * state_im + drive_re
        next_im = decay_re * state_im + decay_im * state_re + drive_im
        return ((next_re, next_im), (next_re, next_im))
    return lax.scan(advance, carry_in, block_items)

def reference(tokens, cotangent, seq_lengths, block_deal, in_proj, forget_proj, gate_proj, out_proj, ffn_gate, ffn_up, ffn_down, gain_mix, gain_out, gain_ffn, lower_bound, rotation):
    block_ids = jnp.arange(N_DP, dtype=jnp.int32)
    block_order = jnp.zeros((N_DP,), jnp.int32).at[block_deal].set(block_ids)
    offsets = (jnp.cumsum(seq_lengths) - seq_lengths).astype(jnp.int32)
    start_flags = jnp.zeros((TOKENS,), jnp.float32).at[offsets].set(jnp.float32(1.0))
    keep_mask = (1.0 - start_flags).reshape(N_DP, TOK_DEV)[block_deal].reshape(TOKENS, 1)

    def to_stream(tensor):
        return tensor.reshape(N_DP, TOK_DEV, HALF)[block_order]

    def to_device(tensor):
        return tensor[block_deal].reshape(TOKENS, HALF)

    def forward(inputs, in_proj, forget_proj, gate_proj, out_proj, ffn_gate, ffn_up, ffn_down, gain_mix, gain_out, gain_ffn, lower_bound, rotation):
        normed_in = low(rms_scale(inputs, gain_mix))
        in_out = low_back(project(normed_in, low(in_proj)))
        forget_out = low_back(project(normed_in, low(forget_proj)))
        gate_out = low_back(project(normed_in, low(gate_proj)))
        magnitude = lower_bound + (1.0 - lower_bound) * jax.nn.sigmoid(forget_out)
        decay_re = keep_mask * magnitude * jnp.cos(rotation)
        decay_im = keep_mask * magnitude * jnp.sin(rotation)
        drive_re = jax.nn.silu(in_out[:, :HALF]) * (1.0 - magnitude)
        drive_im = jax.nn.silu(in_out[:, HALF:]) * (1.0 - magnitude)
        zero_state = jnp.zeros((HALF,), jnp.float32)
        _, (state_re, state_im) = lax.scan(jax.checkpoint(block_scan), (zero_state, zero_state), (to_stream(decay_re), to_stream(decay_im), to_stream(drive_re), to_stream(drive_im)))
        state = jnp.concatenate([to_device(state_re), to_device(state_im)], axis=1)
        normed_mid = low(rms_scale(state, gain_out) * jax.nn.silu(gate_out))
        residual = inputs + low_back(project(normed_mid, low(out_proj)))
        normed_ffn = low(rms_scale(residual, gain_ffn))
        gate_value = low_back(project(normed_ffn, low(ffn_gate)))
        up_value = low_back(project(normed_ffn, low(ffn_up)))
        hidden = low(jax.nn.silu(gate_value) * up_value)
        return residual + low_back(jnp.dot(hidden, low(ffn_down), precision=PRECISE, preferred_element_type=jnp.float32))
    inputs = tokens.astype(jnp.float32)
    result, pullback = jax.vjp(forward, inputs, in_proj, forget_proj, gate_proj, out_proj, ffn_gate, ffn_up, ffn_down, gain_mix, gain_out, gain_ffn, lower_bound, rotation)
    grads = pullback(cotangent.astype(jnp.float32))
    return (result.astype(jnp.bfloat16), grads[0].astype(jnp.bfloat16), grads[1], grads[2], grads[3], grads[4], grads[5], grads[6], grads[7], grads[8], grads[9], grads[10], grads[11], grads[12])
```

```python
from functools import partial

import jax
import jax.numpy as jnp
from jax import lax
from jax.experimental import pallas as pl
from jax.experimental.pallas import tpu as pltpu
from jax.sharding import PartitionSpec as P


EPS = 1e-06
LOW = jnp.bfloat16
F32 = jnp.float32
MESH = pl.DeviceIdType.MESH
ROWS = 32
LANES = 128


def contract(left_rows, right_rows):
    return lax.dot_general(
        left_rows, right_rows, (((1,), (1,)), ((), ())), preferred_element_type=F32
    )


def outer_rows(left_rows, right_rows):
    return lax.dot_general(
        left_rows, right_rows, (((0,), (0,)), ((), ())), preferred_element_type=F32
    )


class Layout:
    def __init__(self, n):
        self.n = n
        self.Y = n // 16
        self.C, self.X, self.ZL, self.ZH = 1, 2, 4 * self.Y, 8 * self.Y
        self.ybits = []
        bit = 4
        while bit < self.ZL:
            self.ybits.append(bit)
            bit *= 2
        self.wbits = [self.ZH] + self.ybits + [self.C]
        self.tmasks = [0, self.X, self.ZL, self.ZL | self.X]
        self.wmasks = [0]
        for bit in self.wbits:
            self.wmasks = self.wmasks + [m | bit for m in self.wmasks]
        self.bits = [1 << k for k in range(n.bit_length() - 1)]

    def flip(self, device, mask):
        for bit in self.bits:
            if mask & bit:
                device = device + bit * (1 - 2 * ((device // bit) % 2))
        return device

    def parts(self, device):
        c = device % 2
        x = (device // self.X) % 2
        y = (device // 4) % self.Y
        zlo = (device // self.ZL) % 2
        zhi = device // self.ZH
        return zhi, zlo, y, x, c

    def send(self, value, mask):
        return lax.ppermute(value, "dp", [(i, i ^ mask) for i in range(self.n)])

    def gather_t(self, value):
        return [value] + [self.send(value, m) for m in self.tmasks[1:]]

    def scatter_t(self, blocks):
        got = [self.send(b, m) for b, m in zip(blocks[1:], self.tmasks[1:])]
        total = blocks[0].astype(F32)
        for g in got:
            total = total + g.astype(F32)
        return total

    def gather_w(self, value):
        pieces = [value]
        for bit in self.wbits:
            pieces = pieces + [self.send(v, bit) for v in pieces]
        return pieces


def gather_kernel(lay, masks, slot_of, in_ref, out_ref, send_sems, recv_sems):
    me = lax.axis_index("dp")
    peers = [lay.flip(me, m) for m in masks]
    barrier = pltpu.get_barrier_semaphore()
    for peer in peers:
        pl.semaphore_signal(barrier, inc=1, device_id=(peer,), device_id_type=MESH)
    pl.semaphore_wait(barrier, len(peers))
    slot = slot_of(me)
    copies = []
    for i, peer in enumerate(peers):
        copy = pltpu.make_async_remote_copy(
            src_ref=in_ref,
            dst_ref=out_ref.at[slot],
            send_sem=send_sems.at[i],
            recv_sem=recv_sems.at[i],
            device_id=(peer,),
            device_id_type=MESH,
        )
        copy.start()
        copies.append(copy)
    out_ref[slot] = in_ref[...]
    for copy in copies:
        copy.wait()


def small_gather(lay, value, masks, slot_of, slots, collective_id):
    masks = [m for m in masks if m]
    vmem = pl.BlockSpec(memory_space=pltpu.VMEM)
    return pl.pallas_call(
        partial(gather_kernel, lay, masks, slot_of),
        out_shape=jax.ShapeDtypeStruct((slots,) + value.shape, value.dtype),
        in_specs=[vmem],
        out_specs=vmem,
        scratch_shapes=[
            pltpu.SemaphoreType.DMA((len(masks),)),
            pltpu.SemaphoreType.DMA((len(masks),)),
        ],
        compiler_params=pltpu.CompilerParams(collective_id=collective_id, has_side_effects=True),
    )(value)


def exchange_kernel(lay, masks, in_ref, out_ref, send_sems, recv_sems):
    me = lax.axis_index("dp")
    peers = [lay.flip(me, m) for m in masks]
    barrier = pltpu.get_barrier_semaphore()
    for peer in peers:
        pl.semaphore_signal(barrier, inc=1, device_id=(peer,), device_id_type=MESH)
    pl.semaphore_wait(barrier, len(peers))
    copies = []
    for i, peer in enumerate(peers):
        copy = pltpu.make_async_remote_copy(
            src_ref=in_ref.at[peer],
            dst_ref=out_ref.at[me],
            send_sem=send_sems.at[i],
            recv_sem=recv_sems.at[i],
            device_id=(peer,),
            device_id_type=MESH,
        )
        copy.start()
        copies.append(copy)
    out_ref[me] = in_ref[me]
    for copy in copies:
        copy.wait()


def small_exchange(lay, value, collective_id):
    masks = list(range(1, lay.n))
    vmem = pl.BlockSpec(memory_space=pltpu.VMEM)
    return pl.pallas_call(
        partial(exchange_kernel, lay, masks),
        out_shape=jax.ShapeDtypeStruct(value.shape, value.dtype),
        in_specs=[vmem],
        out_specs=vmem,
        scratch_shapes=[
            pltpu.SemaphoreType.DMA((len(masks),)),
            pltpu.SemaphoreType.DMA((len(masks),)),
        ],
        compiler_params=pltpu.CompilerParams(collective_id=collective_id, has_side_effects=True),
    )(value)


def sig(v):
    return 1.0 / (1.0 + jnp.exp(-v))


def lanes(base, h):
    return slice(base + h * LANES, base + (h + 1) * LANES)


def fold_rows(v):
    return jnp.sum(v.reshape(v.shape[0] // 8, 8, v.shape[1]), axis=0)


def forward_kernel(half, length, proj, keep, par, d_re, d_im, v_re, v_im, summ):
    total = d_re.shape[1]
    blocks = total // length
    tiles = half // LANES

    def terms(i, _):
        rows = pl.ds(pl.multiple_of(i * ROWS, ROWS), ROWS)
        kept = keep[rows, :]
        for h in range(tiles):
            at = slice(h * LANES, (h + 1) * LANES)
            lower = par[0:1, at]
            magnitude = lower + (1.0 - lower) * sig(proj[rows, lanes(4 * half, h)])
            rest = 1.0 - magnitude
            d_re[h, rows, :] = kept * magnitude * par[1:2, at]
            d_im[h, rows, :] = kept * magnitude * par[2:3, at]
            a = proj[rows, lanes(0, h)]
            b = proj[rows, lanes(half, h)]
            v_re[h, rows, :] = a * sig(a) * rest
            v_im[h, rows, :] = b * sig(b) * rest
        return 0

    lax.fori_loop(0, total // ROWS, terms, 0)

    def step(t, carry):
        rows = pl.ds(t, blocks, stride=length)
        out = []
        for h in range(tiles):
            p_re, p_im, s_re, s_im = carry[4 * h : 4 * h + 4]
            dr, di = d_re[h, rows, :], d_im[h, rows, :]
            out += [
                dr * p_re - di * p_im,
                dr * p_im + di * p_re,
                dr * s_re - di * s_im + v_re[h, rows, :],
                dr * s_im + di * s_re + v_im[h, rows, :],
            ]
        return tuple(out)

    zero = jnp.zeros((blocks, LANES), F32)
    ends = lax.fori_loop(0, length, step, (zero + 1.0, zero, zero, zero) * tiles, unroll=4)
    for j in range(blocks):
        summ[j, 4:8, :] = jnp.zeros((4, half), F32)
        for h in range(tiles):
            for k in range(4):
                summ[j, k : k + 1, lanes(0, h)] = ends[4 * h + k][j : j + 1, :]


def chain_blocks(half, n, blocks, ints, summ, back):
    tiles = half // LANES

    def chain(i, carry):
        p = i if back is None else n - 1 - i
        tile = summ[ints[p]]
        shift = tile[2:4, :] if back is None else back[ints[p]]
        out = []
        for h in range(tiles):
            at = slice(h * LANES, (h + 1) * LANES)
            old = carry[h * (2 + 2 * blocks) : (h + 1) * (2 + 2 * blocks)]
            c_re, c_im = old[0], old[1]
            a_re = tile[0:1, at]
            a_im = tile[1:2, at] if back is None else -tile[1:2, at]
            out.append(a_re * c_re - a_im * c_im + shift[0:1, at])
            out.append(a_re * c_im + a_im * c_re + shift[1:2, at])
            for j in range(blocks):
                here = ints[n + j] == p
                out.append(jnp.where(here, c_re, old[2 + 2 * j]))
                out.append(jnp.where(here, c_im, old[3 + 2 * j]))
        return tuple(out)

    first = summ[0]
    zero = first[0:1, 0:LANES] - first[0:1, 0:LANES]
    res = lax.fori_loop(0, n, chain, (zero,) * (tiles * (2 + 2 * blocks)))
    entry = []
    for h in range(tiles):
        old = res[h * (2 + 2 * blocks) : (h + 1) * (2 + 2 * blocks)]
        entry.append(jnp.concatenate([old[2 + 2 * j] for j in range(blocks)], axis=0))
        entry.append(jnp.concatenate([old[3 + 2 * j] for j in range(blocks)], axis=0))
    return tuple(entry)


def state_kernel(
    half, length, n, ints, summ, d_re, d_im, v_re, v_im, proj, gain,
    st_re, st_im, be_re, be_im, unit, squares,
):
    total = d_re.shape[1]
    blocks = total // length
    tiles = half // LANES

    def step(t, carry):
        rows = pl.ds(t, blocks, stride=length)
        out = []
        for h in range(tiles):
            s_re, s_im = carry[2 * h], carry[2 * h + 1]
            be_re[h, rows, :] = s_re
            be_im[h, rows, :] = s_im
            dr, di = d_re[h, rows, :], d_im[h, rows, :]
            n_re = dr * s_re - di * s_im + v_re[h, rows, :]
            n_im = dr * s_im + di * s_re + v_im[h, rows, :]
            st_re[h, rows, :] = n_re
            st_im[h, rows, :] = n_im
            out += [n_re, n_im]
        return tuple(out)

    entry = chain_blocks(half, n, blocks, ints, summ, None)
    lax.fori_loop(0, length, step, entry, unroll=4)

    def finish(i, _):
        rows = pl.ds(pl.multiple_of(i * ROWS, ROWS), ROWS)
        square = jnp.zeros((ROWS, 1), F32)
        for h in range(tiles):
            for part, st in ((0, st_re), (1, st_im)):
                v = st[h, rows, :]
                g = proj[rows, lanes((2 + part) * half, h)]
                at = lanes(part * half, h)
                unit[rows, at] = (v * gain[0:1, at] * (g * sig(g))).astype(LOW)
                square = square + jnp.sum(v * v, axis=1, keepdims=True)
        squares[rows, :] = square
        return 0

    lax.fori_loop(0, total // ROWS, finish, 0)


def back_kernel(
    half, length, grad_mid, st_re, st_im, proj, gain, scale, d_re, d_im,
    gs_re, gs_im, gate_low, mid, gain_grad, summ, acc,
):
    total = d_re.shape[1]
    blocks = total // length
    tiles = half // LANES
    acc[...] = jnp.zeros_like(acc)

    def terms(i, _):
        rows = pl.ds(pl.multiple_of(i * ROWS, ROWS), ROWS)
        r = scale[rows, 0:1]
        q = scale[rows, 1:2]
        for h in range(tiles):
            for part, st, gs in ((0, st_re, gs_re), (1, st_im, gs_im)):
                at = lanes(part * half, h)
                g = proj[rows, lanes((2 + part) * half, h)]
                v = st[h, rows, :]
                gv = gain[0:1, at]
                dm = grad_mid[rows, at]
                sg = sig(g)
                silu = g * sg
                du = dm * silu
                normed = v * r
                scaled = normed * gv
                mid[rows, at] = (scaled * silu).astype(LOW)
                gate_low[rows, at] = (dm * scaled * (sg * (1.0 + g * (1.0 - sg)))).astype(LOW)
                gs[h, rows, :] = du * gv * r - v * q
                acc[:, at] = acc[:, at] + fold_rows(du * normed)
        return 0

    lax.fori_loop(0, total // ROWS, terms, 0)
    gain_grad[...] = acc[...]

    def step(i, carry):
        rows = pl.ds(length - 1 - i, blocks, stride=length)
        out = []
        for h in range(tiles):
            a_re = gs_re[h, rows, :] + carry[2 * h]
            a_im = gs_im[h, rows, :] + carry[2 * h + 1]
            dr, di = d_re[h, rows, :], d_im[h, rows, :]
            out += [dr * a_re + di * a_im, dr * a_im - di * a_re]
        return tuple(out)

    zero = jnp.zeros((blocks, LANES), F32)
    ends = lax.fori_loop(0, length, step, (zero, zero) * tiles, unroll=4)
    for j in range(blocks):
        summ[j, 2:8, :] = jnp.zeros((6, half), F32)
        for h in range(tiles):
            for k in range(2):
                summ[j, k : k + 1, lanes(0, h)] = ends[2 * h + k][j : j + 1, :]


def adjoint_kernel(
    half, length, n, ints, summ, back, gs_re, gs_im, d_re, d_im, be_re, be_im, proj, keep, par, gate_low,
    grads, lower_grad, angle_grad, ad_re, ad_im, acc,
):
    total = d_re.shape[1]
    blocks = total // length
    tiles = half // LANES

    def step(i, carry):
        rows = pl.ds(length - 1 - i, blocks, stride=length)
        out = []
        for h in range(tiles):
            a_re = gs_re[h, rows, :] + carry[2 * h]
            a_im = gs_im[h, rows, :] + carry[2 * h + 1]
            ad_re[h, rows, :] = a_re
            ad_im[h, rows, :] = a_im
            dr, di = d_re[h, rows, :], d_im[h, rows, :]
            out += [dr * a_re + di * a_im, dr * a_im - di * a_re]
        return tuple(out)

    entry = chain_blocks(half, n, blocks, ints, summ, back)
    lax.fori_loop(0, length, step, entry, unroll=4)
    acc[...] = jnp.zeros_like(acc)

    def terms(i, _):
        rows = pl.ds(pl.multiple_of(i * ROWS, ROWS), ROWS)
        kept = keep[rows, :]
        for h in range(tiles):
            at = slice(h * LANES, (h + 1) * LANES)
            lower, cos, sin = par[0:1, at], par[1:2, at], par[2:3, at]
            sf = sig(proj[rows, lanes(4 * half, h)])
            magnitude = lower + (1.0 - lower) * sf
            rest = 1.0 - magnitude
            a = proj[rows, lanes(0, h)]
            b = proj[rows, lanes(half, h)]
            sa, sb = sig(a), sig(b)
            ar, ai = ad_re[h, rows, :], ad_im[h, rows, :]
            br, bi = be_re[h, rows, :], be_im[h, rows, :]
            g_re = ar * br + ai * bi
            g_im = ai * br - ar * bi
            g_mag = kept * (g_re * cos + g_im * sin) - (ar * (a * sa) + ai * (b * sb))
            acc[0:8, at] = acc[0:8, at] + fold_rows(g_mag * (1.0 - sf))
            acc[8:16, at] = acc[8:16, at] + fold_rows(kept * magnitude * (g_im * cos - g_re * sin))
            grads[rows, lanes(0, h)] = (ar * rest * (sa * (1.0 + a * (1.0 - sa)))).astype(LOW)
            grads[rows, lanes(half, h)] = (ai * rest * (sb * (1.0 + b * (1.0 - sb)))).astype(LOW)
            grads[rows, lanes(4 * half, h)] = (g_mag * (1.0 - lower) * sf * (1.0 - sf)).astype(LOW)
        grads[rows, 2 * half : 4 * half] = gate_low[rows, :]
        return 0

    lax.fori_loop(0, total // ROWS, terms, 0)
    lower_grad[...] = acc[0:8, :]
    angle_grad[...] = acc[8:16, :]


VMEM = pl.BlockSpec(memory_space=pltpu.VMEM)
SMEM = pl.BlockSpec(memory_space=pltpu.SMEM)


def plain_call(body, outs, n_in, smem=0, scratch=(), name=None):
    return pl.pallas_call(
        body,
        out_shape=tuple(jax.ShapeDtypeStruct(s, d) for s, d in outs),
        in_specs=[SMEM] * smem + [VMEM] * (n_in - smem),
        out_specs=tuple(VMEM for _ in outs),
        scratch_shapes=list(scratch),
        compiler_params=pltpu.CompilerParams(vmem_limit_bytes=48 << 20),
        cost_estimate=pl.CostEstimate(flops=20_000_000, bytes_accessed=12_000_000, transcendentals=0),
        name=name,
    )


def local(
    n,
    tokens,
    cotangent,
    seq_lengths,
    block_deal,
    in_proj,
    forget_proj,
    gate_proj,
    out_proj,
    ffn_gate,
    ffn_up,
    ffn_down,
    gain_mix,
    gain_out,
    gain_ffn,
    lower_bound,
    rotation,
):
    lay = Layout(n)
    Y = lay.Y
    W = n // 4
    me = lax.axis_index("dp")
    zhi, zlo, y, x, c = lay.parts(me)
    mine_t = zlo * 2 + x
    length, width = tokens.shape
    half = width // 8
    total = 4 * length
    r_in, r_f = in_proj.shape[0], forget_proj.shape[0]

    def w_slot(device):
        zh, _, yy, _, cc = lay.parts(device)
        return (zh * Y + yy) * 2 + cc

    indices = jnp.arange(n, dtype=jnp.int32)
    order = jnp.sum(jnp.where(block_deal[None, :] == indices[:, None], indices[None, :], 0), axis=1)
    t_devices = jnp.stack([lay.flip(me, m) for m in lay.tmasks])
    t_places = jnp.sum(
        jnp.where(t_devices[:, None] == indices[None, :], block_deal[None, :], 0), axis=1
    )
    o_parts = lay.parts(order)
    t_rel = ((o_parts[1] + zlo) % 2) * 2 + (o_parts[3] + x) % 2
    ints = jnp.concatenate([w_slot(order) * 4 + t_rel, t_places]).astype(jnp.int32)
    offsets = jnp.cumsum(seq_lengths) - seq_lengths
    positions = (
        t_places[:, None] * length + jnp.arange(length, dtype=jnp.int32)[None, :]
    ).reshape(-1)
    starts = jnp.any(positions[:, None] == offsets[None, :], axis=1)
    keep = jnp.where(starts, 0.0, 1.0).astype(F32)[:, None]

    packed = jnp.concatenate([gain_mix, gain_ffn, gain_out, lower_bound, rotation])
    pack_rows = -(-packed.shape[0] // 128)
    packed = jnp.pad(packed, (0, 8 * 128 - packed.shape[0])).reshape(8, 128)
    every = small_gather(lay, packed, list(range(n)), lambda d: d, n, 0)
    every = every[:, :pack_rows, :].reshape(n, pack_rows * 128)
    g_mix = every[:, 0:r_in].reshape(1, width)
    g_ffn = every[:, r_in : 2 * r_in].reshape(1, width)
    g_out = every[:, 2 * r_in : 3 * r_in].reshape(2, 2, Y, 2, 2 * r_in)
    g_out = lax.dynamic_index_in_dim(g_out, zlo, 1, keepdims=False)
    g_out = lax.dynamic_index_in_dim(g_out, x, 2, keepdims=False).reshape(1, 2 * half)

    def channels(vector):
        vector = vector.reshape(2, Y, 2, half // Y)
        vector = lax.dynamic_index_in_dim(vector, zlo, 0, keepdims=False)
        return lax.dynamic_index_in_dim(vector, x, 1, keepdims=False).reshape(1, half)

    lower = channels(every[:, 3 * r_in : 3 * r_in + r_f])
    angle = channels(every[:, 3 * r_in + r_f : 3 * r_in + 2 * r_f])
    par = jnp.concatenate(
        [lower, jnp.cos(angle), jnp.sin(angle), jnp.zeros((5, half), F32)], axis=0
    )

    forget_to = [(2 * e + b, b * (n // 2) + e) for e in range(n // 2) for b in range(2)]
    forget_from = [(d, s) for s, d in forget_to]
    forget_low = lax.ppermute(forget_proj.astype(LOW), "dp", forget_to)
    tok_all = jnp.concatenate(lay.gather_t(tokens), axis=0)
    out_cols = out_proj.astype(LOW).reshape(r_in, 2, 2, Y, 2, 2 * r_in)
    out_cols = out_cols.transpose(2, 4, 0, 1, 3, 5).reshape(4, r_in, 2 * half)

    def out_for(mask):
        slot = ((zlo + (1 if mask & lay.ZL else 0)) % 2) * 2 + (x + (1 if mask & lay.X else 0)) % 2
        return lax.dynamic_index_in_dim(out_cols, slot, 0, keepdims=False)

    out_low = jnp.stack(
        [out_for(0)] + [lay.send(out_for(m), m) for m in lay.tmasks[1:]]
    )
    mix_low = jnp.concatenate([in_proj.astype(LOW), gate_proj.astype(LOW), forget_low], axis=0)
    mix_pieces = lay.gather_w(mix_low)
    out_pieces = lay.gather_w(out_low)

    slots = [w_slot(lay.flip(me, m)) for m in lay.wmasks]
    mix_buf = jnp.zeros((W,) + mix_low.shape, LOW)
    for slot, piece in zip(slots, mix_pieces):
        mix_buf = lax.dynamic_update_slice(mix_buf, piece[None], (slot, 0, 0))
    w_in = mix_buf[:, :r_in].reshape(2 * half, width)
    w_gate = mix_buf[:, r_in : 2 * r_in].reshape(2 * half, width)
    w_forget = (
        mix_buf[:, 2 * r_in :]
        .reshape(2, W // 2, r_f, width)
        .transpose(1, 0, 2, 3)
        .reshape(half, width)
    )
    w_mix = jnp.concatenate([w_in, w_gate, w_forget], axis=0)
    out_buf = jnp.zeros((n, r_in, 2 * half), LOW)
    for mask, piece in zip(lay.wmasks, out_pieces):
        for j, t_mask in enumerate(lay.tmasks):
            out_buf = lax.dynamic_update_slice(
                out_buf, piece[j][None], (lay.flip(me, mask ^ t_mask), 0, 0)
            )
    w_out = out_buf.reshape(width, 2 * half)

    f_gate, f_up, f_down, cot_own, _, _ = lax.optimization_barrier(
        (ffn_gate.astype(LOW), ffn_up.astype(LOW), ffn_down.astype(LOW), cotangent, mix_pieces[1], tok_all)
    )
    gate_pieces = lay.gather_w(f_gate)
    f_up, _ = lax.optimization_barrier((f_up, gate_pieces[1]))
    up_pieces = lay.gather_w(f_up)
    f_down, _ = lax.optimization_barrier((f_down, up_pieces[1]))
    down_pieces = lay.gather_w(f_down)
    w_gu = jnp.concatenate(gate_pieces + up_pieces, axis=0)
    w_down = jnp.concatenate(down_pieces, axis=0)
    hid = w_down.shape[0]
    cot_all = jnp.concatenate(lay.gather_t(cot_own), axis=0)

    inputs = tokens.astype(F32)
    r_tok = lax.rsqrt(jnp.mean(inputs * inputs, axis=-1, keepdims=True) + EPS)
    all32 = tok_all.astype(F32)
    normed = (
        all32 * lax.rsqrt(jnp.mean(all32 * all32, axis=-1, keepdims=True) + EPS) * g_mix
    ).astype(LOW)
    proj = contract(normed, w_mix)
    wide = ((half // LANES, total, LANES), F32)
    d_re, d_im, v_re, v_im, summ = plain_call(
        partial(forward_kernel, half, length),
        [wide] * 4 + [((4, 8, half), F32)],
        3,
        name="gates",
    )(proj, keep, par)
    summ_all = small_gather(lay, summ, lay.wmasks, w_slot, W, 1).reshape(n, 8, half)
    st_re, st_im, be_re, be_im, unit, squares = plain_call(
        partial(state_kernel, half, length, n),
        [wide] * 4 + [((total, 2 * half), LOW), ((total, 1), F32)],
        8,
        smem=1,
        name="states",
    )(ints, summ_all, d_re, d_im, v_re, v_im, proj, g_out)
    branch_low = contract(unit, w_out).astype(LOW)

    def t_blocks(value):
        return [value[j * length : (j + 1) * length] for j in range(4)]

    square = lay.scatter_t(t_blocks(squares))
    branch = lay.scatter_t(t_blocks(branch_low))
    r_state = lax.rsqrt(square / width + EPS)
    residual = inputs + r_state * branch
    r_res = lax.rsqrt(jnp.mean(residual * residual, axis=-1, keepdims=True) + EPS)
    ffn_low = (residual * r_res * g_ffn).astype(LOW)

    ffn_all = jnp.concatenate(lay.gather_t(ffn_low), axis=0)
    gate_up = contract(ffn_all, w_gu)
    gate_value, up_value = gate_up[:, :hid], gate_up[:, hid:]
    s_gate = jax.nn.sigmoid(gate_value)
    silu_gate = gate_value * s_gate
    hidden_low = (silu_gate * up_value).astype(LOW)
    grad_hidden = contract(cot_all, w_down)
    grad_gu = jnp.concatenate(
        [
            (grad_hidden * up_value * s_gate * (1.0 + gate_value * (1.0 - s_gate))).astype(LOW),
            (grad_hidden * silu_gate).astype(LOW),
        ],
        axis=1,
    )
    du_low = jnp.dot(grad_gu, w_gu, preferred_element_type=F32).astype(LOW)
    du = lay.scatter_t(t_blocks(du_low))
    mixed_low = jnp.dot(hidden_low, w_down, preferred_element_type=F32).astype(LOW)
    mixed_out = (residual + lay.scatter_t(t_blocks(mixed_low))).astype(LOW)

    def scatter_w(partial_grad):
        for bit in reversed(lay.wbits):
            rows = partial_grad.shape[0] // 2
            got = lay.send(partial_grad[rows:], bit)
            partial_grad = partial_grad[:rows].astype(F32) + got.astype(F32)
            if bit != lay.wbits[0]:
                partial_grad = partial_grad.astype(LOW)
        return partial_grad

    grad_w_gu = outer_rows(grad_gu, ffn_all).astype(LOW)
    grad_w_down = outer_rows(hidden_low, cot_all).astype(LOW)
    ffn_gate_grad = scatter_w(grad_w_gu[:hid])
    ffn_up_grad = scatter_w(grad_w_gu[hid:])
    ffn_down_grad = scatter_w(grad_w_down)

    du_gain = du * g_ffn
    grad_residual = (
        cotangent.astype(F32)
        + r_res * du_gain
        - residual * (r_res * r_res * r_res) * jnp.mean(residual * du_gain, axis=-1, keepdims=True)
    )
    ffn_gain_part = jnp.sum(du * residual * r_res, axis=0)
    grad_low = grad_residual.astype(LOW)
    inner = jnp.sum(grad_low.astype(F32) * branch, axis=-1, keepdims=True) / width
    scale = jnp.concatenate([r_state, r_state * r_state * r_state * inner], axis=1)

    grad_all = jnp.concatenate(lay.gather_t(grad_low), axis=0)
    scale_all = jnp.concatenate(lay.gather_t(scale), axis=0)
    grad_mid = jnp.dot(grad_all, w_out, preferred_element_type=F32)
    gs_re, gs_im, gate_low, mid, out_gain_part, back = plain_call(
        partial(back_kernel, half, length),
        [wide] * 2
        + [((total, 2 * half), LOW)] * 2
        + [((8, 2 * half), F32), ((4, 8, half), F32)],
        8,
        scratch=[pltpu.VMEM((8, 2 * half), F32)],
        name="back_gates",
    )(grad_mid, st_re, st_im, proj, g_out, scale_all, d_re, d_im)
    back_all = small_gather(lay, back, lay.wmasks, w_slot, W, 2).reshape(n, 8, half)
    grads, lower_part, angle_part = plain_call(
        partial(adjoint_kernel, half, length, n),
        [((total, 5 * half), LOW), ((8, half), F32), ((8, half), F32)],
        13,
        smem=1,
        scratch=[pltpu.VMEM((half // LANES, total, LANES), F32)] * 2 + [pltpu.VMEM((16, half), F32)],
        name="adjoints",
    )(ints, summ_all, back_all, gs_re, gs_im, d_re, d_im, be_re, be_im, proj, keep, par, gate_low)
    du_mix_low = jnp.dot(grads, w_mix, preferred_element_type=F32).astype(LOW)
    du_mix = lay.scatter_t(t_blocks(du_mix_low))
    dg_mix = du_mix * g_mix
    tokens_grad = (
        grad_residual
        + r_tok * dg_mix
        - inputs * (r_tok * r_tok * r_tok) * jnp.mean(inputs * dg_mix, axis=-1, keepdims=True)
    ).astype(LOW)
    mix_gain_part = jnp.sum(du_mix * inputs * r_tok, axis=0)

    def scatter_abs(part):
        shape = part.shape
        axes = len(lay.wbits)
        bits = {0: zhi, axes - 1: c}
        for k, bit in enumerate(reversed(lay.ybits)):
            bits[1 + k] = (me // bit) % 2
        names = {0: lay.ZH, axes - 1: lay.C}
        for k, bit in enumerate(reversed(lay.ybits)):
            names[1 + k] = bit
        part = part.reshape((2,) * axes + shape[3:])
        for k in reversed(range(axes)):
            kept = lax.dynamic_index_in_dim(part, bits[k], k, keepdims=False)
            away = lax.dynamic_index_in_dim(part, 1 - bits[k], k, keepdims=False)
            got = lay.send(away, names[k])
            part = kept.astype(F32) + got.astype(F32)
            if k:
                part = part.astype(LOW)
        return part

    grad_w_out = outer_rows(grad_all, mid).astype(LOW)
    grad_w_out = grad_w_out.reshape(2, 2, Y, 2, 2, r_in, 2 * half).transpose(0, 2, 4, 1, 3, 5, 6)
    out_part = scatter_abs(grad_w_out).reshape(4, r_in, 2 * half)

    def out_back(mask):
        slot = ((zlo + (1 if mask & lay.ZL else 0)) % 2) * 2 + (x + (1 if mask & lay.X else 0)) % 2
        return lax.dynamic_index_in_dim(out_part, slot, 0, keepdims=False), slot

    out_grad = jnp.zeros((4, r_in, 2 * half), F32)
    for mask in lay.tmasks:
        value, slot = out_back(mask)
        if mask:
            value = lay.send(value, mask)
        out_grad = lax.dynamic_update_slice(out_grad, value[None], (slot, 0, 0))
    out_proj_grad = (
        out_grad.reshape(2, 2, r_in, 2, Y, 2 * r_in).transpose(2, 3, 0, 4, 1, 5).reshape(r_in, width)
    )

    grad_w_mix = outer_rows(grads, normed).astype(LOW)
    grad_w_mix = jnp.concatenate(
        [
            grad_w_mix[: 2 * half].reshape(W, r_in, width),
            grad_w_mix[2 * half : 4 * half].reshape(W, r_in, width),
            grad_w_mix[4 * half :]
            .reshape(W // 2, 2, r_f, width)
            .transpose(1, 0, 2, 3)
            .reshape(W, r_f, width),
        ],
        axis=1,
    ).reshape(2, Y, 2, 2 * r_in + r_f, width)
    mix_part = scatter_abs(grad_w_mix)
    in_proj_grad = mix_part[:r_in]
    gate_proj_grad = mix_part[r_in : 2 * r_in]
    forget_proj_grad = lax.ppermute(mix_part[2 * r_in :], "dp", forget_from)

    t_hot = ((jnp.arange(2)[:, None] == zlo) & (jnp.arange(2)[None, :] == x)).astype(F32)
    out_gain_part = jnp.sum(out_gain_part, axis=0).reshape(2, 1, Y, 1, 2 * r_in)
    out_gain_part = (out_gain_part * t_hot[None, :, None, :, None]).reshape(n, r_in)

    def spread(vector):
        vector = jnp.sum(vector, axis=0).reshape(1, Y, 1, half // Y)
        return (vector * t_hot[:, None, :, None]).reshape(n, r_f)

    to_owner = jnp.concatenate(
        [
            mix_gain_part.reshape(n, r_in),
            ffn_gain_part.reshape(n, r_in),
            out_gain_part,
            spread(lower_part),
            spread(angle_part),
        ],
        axis=1,
    )
    to_owner = jnp.pad(to_owner, ((0, 0), (0, 1024 - to_owner.shape[1]))).reshape(n, 8, 128)
    owned = jnp.sum(small_exchange(lay, to_owner, 3), axis=0).reshape(-1)
    return (
        mixed_out,
        tokens_grad,
        in_proj_grad,
        forget_proj_grad,
        gate_proj_grad,
        out_proj_grad,
        ffn_gate_grad,
        ffn_up_grad,
        ffn_down_grad,
        owned[0:r_in],
        owned[2 * r_in : 3 * r_in],
        owned[r_in : 2 * r_in],
        owned[3 * r_in : 3 * r_in + r_f],
        owned[3 * r_in + r_f : 3 * r_in + 2 * r_f],
    )


def solution(mesh):
    rows, vector = P("dp", None), P("dp")
    in_specs = (rows, rows, P(), P()) + (rows,) * 7 + (vector,) * 5
    out_specs = (rows,) * 9 + (vector,) * 5
    return jax.shard_map(
        partial(local, mesh.shape["dp"]),
        mesh=mesh,
        in_specs=in_specs,
        out_specs=out_specs,
        check_vma=False,
    )
```

```python
from functools import partial

import jax
import jax.numpy as jnp
from jax import lax
from jax.experimental import pallas as pl
from jax.experimental.pallas import tpu as pltpu
from jax.sharding import PartitionSpec as P


EPS = 1e-06
LOW = jnp.bfloat16
F32 = jnp.float32
MESH = pl.DeviceIdType.MESH
ROWS = 32
LANES = 128


def contract(left_rows, right_rows):
    return lax.dot_general(
        left_rows, right_rows, (((1,), (1,)), ((), ())), preferred_element_type=F32
    )


def outer_rows(left_rows, right_rows):
    return lax.dot_general(
        left_rows, right_rows, (((0,), (0,)), ((), ())), preferred_element_type=F32
    )


class Layout:
    def __init__(self, n):
        self.n = n
        self.Y = n // 16
        self.C, self.X, self.ZL, self.ZH = 1, 2, 4 * self.Y, 8 * self.Y
        self.ybits = []
        bit = 4
        while bit < self.ZL:
            self.ybits.append(bit)
            bit *= 2
        self.wbits = [self.ZH] + self.ybits + [self.C]
        self.rbits = [self.C] + self.ybits + [self.ZH]
        self.tmasks = [0, self.X, self.ZL, self.ZL | self.X]
        self.wmasks = [0]
        for bit in self.wbits:
            self.wmasks = self.wmasks + [m | bit for m in self.wmasks]
        self.bits = [1 << k for k in range(n.bit_length() - 1)]

    def flip(self, device, mask):
        for bit in self.bits:
            if mask & bit:
                device = device + bit * (1 - 2 * ((device // bit) % 2))
        return device

    def parts(self, device):
        c = device % 2
        x = (device // self.X) % 2
        y = (device // 4) % self.Y
        zlo = (device // self.ZL) % 2
        zhi = device // self.ZH
        return zhi, zlo, y, x, c

    def send(self, value, mask):
        return lax.ppermute(value, "dp", [(i, i ^ mask) for i in range(self.n)])

    def gather_t(self, value):
        return [value] + [self.send(value, m) for m in self.tmasks[1:]]

    def scatter_t(self, blocks):
        got = [self.send(b, m) for b, m in zip(blocks[1:], self.tmasks[1:])]
        total = blocks[0].astype(F32)
        for g in got:
            total = total + g.astype(F32)
        return total

    def gather_w(self, value):
        pieces = [value]
        for bit in self.wbits:
            pieces = pieces + [self.send(v, bit) for v in pieces]
        return pieces


def gather_kernel(lay, masks, slot_of, in_ref, out_ref, send_sems, recv_sems):
    me = lax.axis_index("dp")
    peers = [lay.flip(me, m) for m in masks]
    barrier = pltpu.get_barrier_semaphore()
    for peer in peers:
        pl.semaphore_signal(barrier, inc=1, device_id=(peer,), device_id_type=MESH)
    pl.semaphore_wait(barrier, len(peers))
    slot = slot_of(me)
    copies = []
    for i, peer in enumerate(peers):
        copy = pltpu.make_async_remote_copy(
            src_ref=in_ref,
            dst_ref=out_ref.at[slot],
            send_sem=send_sems.at[i],
            recv_sem=recv_sems.at[i],
            device_id=(peer,),
            device_id_type=MESH,
        )
        copy.start()
        copies.append(copy)
    out_ref[slot] = in_ref[...]
    for copy in copies:
        copy.wait()


def small_gather(lay, value, masks, slot_of, slots, collective_id):
    masks = [m for m in masks if m]
    vmem = pl.BlockSpec(memory_space=pltpu.VMEM)
    return pl.pallas_call(
        partial(gather_kernel, lay, masks, slot_of),
        out_shape=jax.ShapeDtypeStruct((slots,) + value.shape, value.dtype),
        in_specs=[vmem],
        out_specs=vmem,
        scratch_shapes=[
            pltpu.SemaphoreType.DMA((len(masks),)),
            pltpu.SemaphoreType.DMA((len(masks),)),
        ],
        compiler_params=pltpu.CompilerParams(collective_id=collective_id, has_side_effects=True),
    )(value)


class Net:
    def __init__(self, lay, peers, send_sems, recv_sems, local_sems):
        self.lay, self.send_sems, self.recv_sems, self.local_sems = lay, send_sems, recv_sems, local_sems
        self.me = lax.axis_index("dp")
        self.used, self.used_local, self.open, self.local = 0, 0, [], []
        barrier = pltpu.get_barrier_semaphore()
        for mask in peers:
            pl.semaphore_signal(
                barrier, inc=1, device_id=(lay.flip(self.me, mask),), device_id_type=MESH
            )
        pl.semaphore_wait(barrier, len(peers))

    def put(self, src, dst, mask):
        copy = pltpu.make_async_remote_copy(
            src_ref=src,
            dst_ref=dst,
            send_sem=self.send_sems.at[self.used],
            recv_sem=self.recv_sems.at[self.used],
            device_id=(self.lay.flip(self.me, mask),),
            device_id_type=MESH,
        )
        copy.start()
        self.used += 1
        self.open.append(copy)
        return copy

    def load(self, src, dst):
        copy = pltpu.make_async_copy(src, dst, self.local_sems.at[self.used_local])
        copy.start()
        self.used_local += 1
        return copy

    def keep(self, src, dst):
        self.local.append(self.load(src, dst))

    def finish(self):
        for copy in self.open:
            copy.wait_send()
        for copy in self.local:
            copy.wait()


class WeightGather:
    def __init__(self, net, own, place):
        self.net, self.own, self.place = net, own, place
        self.bits = net.lay.wbits
        self.pending = {}

    def start(self):
        for bit in self.bits:
            self.pending[bit] = self.net.put(self.own, self.place(self.net.me), bit)
        self.net.keep(self.own, self.place(self.net.me))

    def masks(self):
        out = [0]
        for bit in self.bits[:-1]:
            out = out + [m | bit for m in out]
        return sorted(out[1:], key=lambda m: (bin(m).count("1"), -m))

    def forward(self, mask):
        self.pending[mask].wait_recv()
        last = max(i for i, bit in enumerate(self.bits) if mask & bit)
        here = self.place(self.net.lay.flip(self.net.me, mask))
        for bit in self.bits[last + 1 :]:
            self.pending[mask | bit] = self.net.put(here, here, bit)

    def end(self):
        for mask, copy in self.pending.items():
            if mask & self.bits[-1]:
                copy.wait_recv()


def token_gather(net, own, out):
    lay = net.lay
    net.keep(own, out.at[0])
    return [net.put(own, out.at[j], m) for j, m in enumerate(lay.tmasks) if j]


def token_scatter(net, blocks, out):
    return [net.put(blocks.at[j], out.at[j - 1], m) for j, m in enumerate(net.lay.tmasks) if j]


def arrived(copies):
    for copy in copies:
        copy.wait_recv()


def net_call(body, lay, values, outs, copies, local, collective_id, name, scratch=()):
    hbm = pl.BlockSpec(memory_space=pl.ANY)
    return pl.pallas_call(
        body,
        out_shape=tuple(jax.ShapeDtypeStruct(s, d) for s, d in outs),
        in_specs=[hbm] * len(values),
        out_specs=tuple(hbm for _ in outs),
        scratch_shapes=[
            *scratch,
            pltpu.SemaphoreType.DMA((copies,)),
            pltpu.SemaphoreType.DMA((copies,)),
            pltpu.SemaphoreType.DMA((local,)),
        ],
        compiler_params=pltpu.CompilerParams(
            collective_id=collective_id,
            has_side_effects=True,
            vmem_limit_bytes=(56 << 20) if scratch else None,
        ),
        name=name,
    )(*values)


def w_slot(lay, device):
    zhi, _, y, _, c = lay.parts(device)
    return (zhi * lay.Y + y) * 2 + c


def f_slot(lay, device):
    zhi, _, y, _, c = lay.parts(device)
    return (y * 2 + c) * 2 + zhi


def t_slot(lay, device):
    _, zlo, _, x, _ = lay.parts(device)
    return zlo * 2 + x


def start_kernel(
    lay, units, tok, cot, w_in, w_gate, w_forget, w_out, f_gate, pack,
    tok_all, cot_all, mix_all, out_own, out_all, f_gate_all, every, send_sems, recv_sems, local_sems,
):
    n, W = lay.n, lay.n // 4
    net = Net(lay, list(range(1, n)), send_sems, recv_sems, local_sems)
    me = net.me

    def region(base):
        return lambda d: mix_all.at[pl.ds(base + w_slot(lay, d) * units, units)]

    g_in = WeightGather(net, w_in, region(0))
    g_gate = WeightGather(net, w_gate, region(W * units))
    g_forget = WeightGather(
        net, w_forget, lambda d: mix_all.at[pl.ds(2 * W * units + f_slot(lay, d), 1)]
    )
    g_out = WeightGather(net, out_own, lambda d: out_all.at[w_slot(lay, d)])
    g_ffn = WeightGather(net, f_gate, lambda d: f_gate_all.at[w_slot(lay, d)])
    g_in.start()
    g_gate.start()
    tok_in = token_gather(net, tok, tok_all)
    mine = t_slot(lay, me)
    own = net.load(w_out.at[mine], out_own.at[mine])
    out_in = [
        net.put(w_out.at[t_slot(lay, lay.flip(me, m))], out_own.at[mine], m) for m in lay.tmasks[1:]
    ]
    g_forget.start()
    all_in = [net.put(pack, every.at[me], m) for m in range(1, n)]
    net.keep(pack, every.at[me])
    for mask in g_in.masks():
        g_in.forward(mask)
        g_gate.forward(mask)
    for mask in g_forget.masks():
        g_forget.forward(mask)
    own.wait()
    arrived(out_in)
    g_out.start()
    g_ffn.start()
    arrived(tok_in)
    cot_in = token_gather(net, cot, cot_all)
    for mask in g_out.masks():
        g_out.forward(mask)
    for mask in g_ffn.masks():
        g_ffn.forward(mask)
    for gather in (g_in, g_gate, g_forget, g_out, g_ffn):
        gather.end()
    arrived(cot_in)
    arrived(all_in)
    net.finish()


def group_peers(lay):
    return lay.tmasks[1:] + lay.wbits


def scatter_kernel(lay, blocks, small, weight, got, got_small, weight_all, send_sems, recv_sems, local_sems):
    net = Net(lay, group_peers(lay), send_sems, recv_sems, local_sems)
    gather = WeightGather(net, weight, lambda d: weight_all.at[w_slot(lay, d)])
    waits = token_scatter(net, blocks, got) + token_scatter(net, small, got_small)
    gather.start()
    for mask in gather.masks():
        gather.forward(mask)
    gather.end()
    arrived(waits)
    net.finish()


def gather_both_kernel(lay, own, weight, own_all, weight_all, send_sems, recv_sems, local_sems):
    net = Net(lay, group_peers(lay), send_sems, recv_sems, local_sems)
    gather = WeightGather(net, weight, lambda d: weight_all.at[w_slot(lay, d)])
    waits = token_gather(net, own, own_all)
    gather.start()
    for mask in gather.masks():
        gather.forward(mask)
    gather.end()
    arrived(waits)
    net.finish()


def add_rows(out, left, right):
    rows = left.shape[0]
    tile = 16 if rows % 16 == 0 else rows

    def body(i, _):
        at = pl.ds(pl.multiple_of(i * tile, tile), tile)
        out[at, :] = (left[at, :].astype(F32) + right[at, :].astype(F32)).astype(out.dtype)
        return 0

    lax.fori_loop(0, rows // tile, body, 0)


class WeightReduce:
    def __init__(self, net, part, place, local, stages, total, out):
        self.net, self.part, self.place = net, part, place
        self.local, self.stages, self.total, self.out = local, stages, total, out
        self.bits = net.lay.rbits
        self.sent, self.waited = [], -1

    def side(self, k):
        return (self.net.me // self.bits[k]) % 2

    def start(self):
        at = self.side(0)
        count = self.stages[0].shape[0]
        self.sent = [
            self.net.put(self.part.at[self.place(2 * i + 1 - at)], self.stages[0].at[i], self.bits[0])
            for i in range(count)
        ]
        self.loads = [
            self.net.load(self.part.at[self.place(2 * i + at)], self.local.at[i]) for i in range(count)
        ]

    def wait(self, k):
        if self.waited < k:
            arrived(self.sent)
            self.waited = k

    def add(self, k):
        stage = self.stages[k]
        count = stage.shape[0]
        if k == 0:
            for copy in self.loads:
                copy.wait()
        at = self.side(k)
        mine = self.side(k + 1) if count > 1 else 0

        def one(i):
            old = self.local.at[i] if k == 0 else self.stages[k - 1].at[2 * i + at]
            if count == 1:
                add_rows(self.total, stage.at[i], old)
            else:
                add_rows(stage.at[i], stage.at[i], old)

        if count == 1:
            one(0)
        else:
            for i in range(count // 2):
                one(2 * i + 1 - mine)
            for i in range(count // 2):
                one(2 * i + mine)

    def send(self, k):
        at = self.side(k)
        self.sent = [
            self.net.put(self.stages[k - 1].at[2 * i + 1 - at], self.stages[k].at[i], self.bits[k])
            for i in range(self.stages[k].shape[0])
        ]

    def store(self):
        if self.out is not None:
            self.net.keep(self.total, self.out)


def reduce_kernel(lay, n_parts, *refs):
    W = lay.n // 4
    depth = len(lay.rbits)
    parts, refs = refs[:n_parts], refs[n_parts:]
    (du, mixed, vectors), refs = refs[:3], refs[3:]
    outs, refs = refs[: n_parts - 1], refs[n_parts - 1 :]
    (out_cols, got_du, got_mixed, all_vectors), refs = refs[:4], refs[4:]
    scratch, (send_sems, recv_sems, local_sems) = refs[:-3], refs[-3:]
    net = Net(lay, list(range(1, lay.n)), send_sems, recv_sems, local_sems)
    me = net.me
    jobs = []
    for i, part in enumerate(parts):
        local, *stages = scratch[i * (depth + 2) : i * (depth + 2) + depth + 1]
        total = scratch[i * (depth + 2) + depth + 1]
        place = (lambda k: k) if i else (lambda k: ((k // 2) % lay.Y * 2 + k % 2) * 2 + k // (2 * lay.Y))
        out = None if i == 1 else outs[i - (i > 1)]
        jobs.append(WeightReduce(net, part, place, local, stages, total, out))
    waits = token_scatter(net, du, got_du)
    for job in jobs:
        job.start()
    waits += [net.put(vectors.at[lay.flip(me, m)], all_vectors.at[me], m) for m in range(1, lay.n)]
    net.keep(vectors.at[me], all_vectors.at[me])

    def finish(job, i):
        job.store()
        if i == 1:
            rows = job.total.shape[0] // 4
            mine = t_slot(lay, me)

            def cut(slot):
                return job.total.at[pl.ds(pl.multiple_of(slot * rows, rows), rows)]

            net.keep(cut(mine), out_cols.at[mine])
            for m in lay.tmasks[1:]:
                waits.append(net.put(cut(t_slot(lay, lay.flip(me, m))), out_cols.at[mine], m))

    for tick in range(n_parts + depth - 1):
        for k in range(depth):
            i = tick - k
            valid = 0 <= i < n_parts
            if valid:
                jobs[i].wait(k)
                jobs[i].add(k)
            if k + 1 < depth:
                if 0 <= i - 1 < n_parts:
                    jobs[i - 1].wait(k + 1)
                if valid:
                    jobs[i].send(k + 1)
            elif valid:
                finish(jobs[i], i)
        if tick == 1:
            waits += token_scatter(net, mixed, got_mixed)
    arrived(waits)
    net.finish()


def sig(v):
    return 1.0 / (1.0 + jnp.exp(-v))


def lanes(base, h):
    return slice(base + h * LANES, base + (h + 1) * LANES)


def fold_rows(v):
    return jnp.sum(v.reshape(v.shape[0] // 8, 8, v.shape[1]), axis=0)


def forward_kernel(half, length, proj, keep, par, d_re, d_im, v_re, v_im, summ):
    total = d_re.shape[1]
    blocks = total // length
    tiles = half // LANES

    def terms(i, _):
        rows = pl.ds(pl.multiple_of(i * ROWS, ROWS), ROWS)
        kept = keep[rows, :]
        for h in range(tiles):
            at = slice(h * LANES, (h + 1) * LANES)
            lower = par[0:1, at]
            magnitude = lower + (1.0 - lower) * sig(proj[rows, lanes(4 * half, h)])
            rest = 1.0 - magnitude
            d_re[h, rows, :] = kept * magnitude * par[1:2, at]
            d_im[h, rows, :] = kept * magnitude * par[2:3, at]
            a = proj[rows, lanes(0, h)]
            b = proj[rows, lanes(half, h)]
            v_re[h, rows, :] = a * sig(a) * rest
            v_im[h, rows, :] = b * sig(b) * rest
        return 0

    lax.fori_loop(0, total // ROWS, terms, 0)

    def step(t, carry):
        rows = pl.ds(t, blocks, stride=length)
        out = []
        for h in range(tiles):
            p_re, p_im, s_re, s_im = carry[4 * h : 4 * h + 4]
            dr, di = d_re[h, rows, :], d_im[h, rows, :]
            out += [
                dr * p_re - di * p_im,
                dr * p_im + di * p_re,
                dr * s_re - di * s_im + v_re[h, rows, :],
                dr * s_im + di * s_re + v_im[h, rows, :],
            ]
        return tuple(out)

    zero = jnp.zeros((blocks, LANES), F32)
    ends = lax.fori_loop(0, length, step, (zero + 1.0, zero, zero, zero) * tiles, unroll=4)
    for j in range(blocks):
        summ[j, 4:8, :] = jnp.zeros((4, half), F32)
        for h in range(tiles):
            for k in range(4):
                summ[j, k : k + 1, lanes(0, h)] = ends[4 * h + k][j : j + 1, :]


def chain_blocks(half, n, blocks, ints, summ, back):
    tiles = half // LANES

    def chain(i, carry):
        p = i if back is None else n - 1 - i
        tile = summ[ints[p]]
        shift = tile[2:4, :] if back is None else back[ints[p]]
        out = []
        for h in range(tiles):
            at = slice(h * LANES, (h + 1) * LANES)
            old = carry[h * (2 + 2 * blocks) : (h + 1) * (2 + 2 * blocks)]
            c_re, c_im = old[0], old[1]
            a_re = tile[0:1, at]
            a_im = tile[1:2, at] if back is None else -tile[1:2, at]
            out.append(a_re * c_re - a_im * c_im + shift[0:1, at])
            out.append(a_re * c_im + a_im * c_re + shift[1:2, at])
            for j in range(blocks):
                here = ints[n + j] == p
                out.append(jnp.where(here, c_re, old[2 + 2 * j]))
                out.append(jnp.where(here, c_im, old[3 + 2 * j]))
        return tuple(out)

    first = summ[0]
    zero = first[0:1, 0:LANES] - first[0:1, 0:LANES]
    res = lax.fori_loop(0, n, chain, (zero,) * (tiles * (2 + 2 * blocks)))
    entry = []
    for h in range(tiles):
        old = res[h * (2 + 2 * blocks) : (h + 1) * (2 + 2 * blocks)]
        entry.append(jnp.concatenate([old[2 + 2 * j] for j in range(blocks)], axis=0))
        entry.append(jnp.concatenate([old[3 + 2 * j] for j in range(blocks)], axis=0))
    return tuple(entry)


def state_kernel(
    half, length, n, ints, summ, d_re, d_im, v_re, v_im, proj, gain,
    st_re, st_im, be_re, be_im, unit, squares,
):
    total = d_re.shape[1]
    blocks = total // length
    tiles = half // LANES

    def step(t, carry):
        rows = pl.ds(t, blocks, stride=length)
        out = []
        for h in range(tiles):
            s_re, s_im = carry[2 * h], carry[2 * h + 1]
            be_re[h, rows, :] = s_re
            be_im[h, rows, :] = s_im
            dr, di = d_re[h, rows, :], d_im[h, rows, :]
            n_re = dr * s_re - di * s_im + v_re[h, rows, :]
            n_im = dr * s_im + di * s_re + v_im[h, rows, :]
            st_re[h, rows, :] = n_re
            st_im[h, rows, :] = n_im
            out += [n_re, n_im]
        return tuple(out)

    entry = chain_blocks(half, n, blocks, ints, summ, None)
    lax.fori_loop(0, length, step, entry, unroll=4)

    def finish(i, _):
        rows = pl.ds(pl.multiple_of(i * ROWS, ROWS), ROWS)
        square = jnp.zeros((ROWS, 1), F32)
        for h in range(tiles):
            for part, st in ((0, st_re), (1, st_im)):
                v = st[h, rows, :]
                g = proj[rows, lanes((2 + part) * half, h)]
                at = lanes(part * half, h)
                unit[rows, at] = (v * gain[0:1, at] * (g * sig(g))).astype(LOW)
                square = square + jnp.sum(v * v, axis=1, keepdims=True)
        squares[rows, :] = jnp.broadcast_to(square, (ROWS, LANES))
        return 0

    lax.fori_loop(0, total // ROWS, finish, 0)


def back_kernel(
    half, length, grad_mid, st_re, st_im, proj, gain, scale, d_re, d_im,
    gs_re, gs_im, gate_low, mid, gain_grad, summ, acc,
):
    total = d_re.shape[1]
    blocks = total // length
    tiles = half // LANES
    acc[...] = jnp.zeros_like(acc)

    def terms(i, _):
        rows = pl.ds(pl.multiple_of(i * ROWS, ROWS), ROWS)
        r = scale[rows, 0:1]
        q = scale[rows, 1:2]
        for h in range(tiles):
            for part, st, gs in ((0, st_re, gs_re), (1, st_im, gs_im)):
                at = lanes(part * half, h)
                g = proj[rows, lanes((2 + part) * half, h)]
                v = st[h, rows, :]
                gv = gain[0:1, at]
                dm = grad_mid[rows, at]
                sg = sig(g)
                silu = g * sg
                du = dm * silu
                normed = v * r
                scaled = normed * gv
                mid[rows, at] = (scaled * silu).astype(LOW)
                gate_low[rows, at] = (dm * scaled * (sg * (1.0 + g * (1.0 - sg)))).astype(LOW)
                gs[h, rows, :] = du * gv * r - v * q
                acc[:, at] = acc[:, at] + fold_rows(du * normed)
        return 0

    lax.fori_loop(0, total // ROWS, terms, 0)
    gain_grad[...] = acc[...]

    def step(i, carry):
        rows = pl.ds(length - 1 - i, blocks, stride=length)
        out = []
        for h in range(tiles):
            a_re = gs_re[h, rows, :] + carry[2 * h]
            a_im = gs_im[h, rows, :] + carry[2 * h + 1]
            dr, di = d_re[h, rows, :], d_im[h, rows, :]
            out += [dr * a_re + di * a_im, dr * a_im - di * a_re]
        return tuple(out)

    zero = jnp.zeros((blocks, LANES), F32)
    ends = lax.fori_loop(0, length, step, (zero, zero) * tiles, unroll=4)
    for j in range(blocks):
        summ[j, 2:8, :] = jnp.zeros((6, half), F32)
        for h in range(tiles):
            for k in range(2):
                summ[j, k : k + 1, lanes(0, h)] = ends[2 * h + k][j : j + 1, :]


def adjoint_kernel(
    half, length, n, ints, summ, back, gs_re, gs_im, d_re, d_im, be_re, be_im, proj, keep, par, gate_low,
    grads, lower_grad, angle_grad, ad_re, ad_im, acc,
):
    total = d_re.shape[1]
    blocks = total // length
    tiles = half // LANES

    def step(i, carry):
        rows = pl.ds(length - 1 - i, blocks, stride=length)
        out = []
        for h in range(tiles):
            a_re = gs_re[h, rows, :] + carry[2 * h]
            a_im = gs_im[h, rows, :] + carry[2 * h + 1]
            ad_re[h, rows, :] = a_re
            ad_im[h, rows, :] = a_im
            dr, di = d_re[h, rows, :], d_im[h, rows, :]
            out += [dr * a_re + di * a_im, dr * a_im - di * a_re]
        return tuple(out)

    entry = chain_blocks(half, n, blocks, ints, summ, back)
    lax.fori_loop(0, length, step, entry, unroll=4)
    acc[...] = jnp.zeros_like(acc)

    def terms(i, _):
        rows = pl.ds(pl.multiple_of(i * ROWS, ROWS), ROWS)
        kept = keep[rows, :]
        for h in range(tiles):
            at = slice(h * LANES, (h + 1) * LANES)
            lower, cos, sin = par[0:1, at], par[1:2, at], par[2:3, at]
            sf = sig(proj[rows, lanes(4 * half, h)])
            magnitude = lower + (1.0 - lower) * sf
            rest = 1.0 - magnitude
            a = proj[rows, lanes(0, h)]
            b = proj[rows, lanes(half, h)]
            sa, sb = sig(a), sig(b)
            ar, ai = ad_re[h, rows, :], ad_im[h, rows, :]
            br, bi = be_re[h, rows, :], be_im[h, rows, :]
            g_re = ar * br + ai * bi
            g_im = ai * br - ar * bi
            g_mag = kept * (g_re * cos + g_im * sin) - (ar * (a * sa) + ai * (b * sb))
            acc[0:8, at] = acc[0:8, at] + fold_rows(g_mag * (1.0 - sf))
            acc[8:16, at] = acc[8:16, at] + fold_rows(kept * magnitude * (g_im * cos - g_re * sin))
            grads[rows, lanes(0, h)] = (ar * rest * (sa * (1.0 + a * (1.0 - sa)))).astype(LOW)
            grads[rows, lanes(half, h)] = (ai * rest * (sb * (1.0 + b * (1.0 - sb)))).astype(LOW)
            grads[rows, lanes(4 * half, h)] = (g_mag * (1.0 - lower) * sf * (1.0 - sf)).astype(LOW)
        grads[rows, 2 * half : 4 * half] = gate_low[rows, :]
        return 0

    lax.fori_loop(0, total // ROWS, terms, 0)
    lower_grad[...] = acc[0:8, :]
    angle_grad[...] = acc[8:16, :]


VMEM = pl.BlockSpec(memory_space=pltpu.VMEM)
SMEM = pl.BlockSpec(memory_space=pltpu.SMEM)


def plain_call(body, outs, n_in, smem=0, scratch=(), name=None):
    return pl.pallas_call(
        body,
        out_shape=tuple(jax.ShapeDtypeStruct(s, d) for s, d in outs),
        in_specs=[SMEM] * smem + [VMEM] * (n_in - smem),
        out_specs=tuple(VMEM for _ in outs),
        scratch_shapes=list(scratch),
        compiler_params=pltpu.CompilerParams(vmem_limit_bytes=48 << 20),
        cost_estimate=pl.CostEstimate(flops=20_000_000, bytes_accessed=12_000_000, transcendentals=0),
        name=name,
    )


def local(
    n,
    tokens,
    cotangent,
    seq_lengths,
    block_deal,
    in_proj,
    forget_proj,
    gate_proj,
    out_proj,
    ffn_gate,
    ffn_up,
    ffn_down,
    gain_mix,
    gain_out,
    gain_ffn,
    lower_bound,
    rotation,
):
    lay = Layout(n)
    Y = lay.Y
    W = n // 4
    me = lax.axis_index("dp")
    zhi, zlo, y, x, c = lay.parts(me)
    mine_t = zlo * 2 + x
    length, width = tokens.shape
    half = width // 8
    total = 4 * length
    r_in, r_f = in_proj.shape[0], forget_proj.shape[0]

    indices = jnp.arange(n, dtype=jnp.int32)
    order = jnp.sum(jnp.where(block_deal[None, :] == indices[:, None], indices[None, :], 0), axis=1)
    t_devices = jnp.stack([lay.flip(me, m) for m in lay.tmasks])
    t_places = jnp.sum(
        jnp.where(t_devices[:, None] == indices[None, :], block_deal[None, :], 0), axis=1
    )
    o_parts = lay.parts(order)
    t_rel = ((o_parts[1] + zlo) % 2) * 2 + (o_parts[3] + x) % 2
    ints = jnp.concatenate([w_slot(lay, order) * 4 + t_rel, t_places]).astype(jnp.int32)
    offsets = jnp.cumsum(seq_lengths) - seq_lengths
    positions = (
        t_places[:, None] * length + jnp.arange(length, dtype=jnp.int32)[None, :]
    ).reshape(-1)
    starts = jnp.any(positions[:, None] == offsets[None, :], axis=1)
    keep = jnp.where(starts, 0.0, 1.0).astype(F32)[:, None]

    packed = jnp.concatenate([gain_mix, gain_ffn, gain_out, lower_bound, rotation])
    pack_rows = -(-packed.shape[0] // 128)
    packed = jnp.pad(packed, (0, 8 * 128 - packed.shape[0])).reshape(8, 128)
    forget_to = [(2 * e + b, b * (n // 2) + e) for e in range(n // 2) for b in range(2)]
    forget_from = [(d, s) for s, d in forget_to]
    forget_low = lax.ppermute(forget_proj.astype(LOW), "dp", forget_to)
    out_cols = out_proj.astype(LOW).reshape(r_in, 2, 2, Y, 2, 2 * r_in)
    out_cols = out_cols.transpose(2, 4, 0, 1, 3, 5).reshape(4, r_in, 2 * half)
    units = r_in // r_f
    r_ffn = ffn_gate.shape[0]
    tok_all, cot_all, w_mix, _, w_out, w_ffn_gate, every = net_call(
        partial(start_kernel, lay, units),
        lay,
        (
            tokens,
            cotangent,
            in_proj.astype(LOW).reshape(units, r_f, width),
            gate_proj.astype(LOW).reshape(units, r_f, width),
            forget_low.reshape(1, r_f, width),
            out_cols,
            ffn_gate.astype(LOW),
            packed,
        ),
        [
            ((4, length, width), LOW),
            ((4, length, width), LOW),
            ((W * (2 * units + 1), r_f, width), LOW),
            ((4, r_in, 2 * half), LOW),
            ((W, 4, r_in, 2 * half), LOW),
            ((W, r_ffn, width), LOW),
            ((n, 8, 128), F32),
        ],
        5 * (W - 1) + 9 + n - 1,
        16,
        0,
        "start",
    )
    tok_all = tok_all.reshape(total, width)
    cot_all = cot_all.reshape(total, width)
    w_mix = w_mix.reshape(5 * half, width)
    w_out = w_out.reshape(2, Y, 2, 2, 2, r_in, 2 * half).transpose(0, 3, 1, 4, 2, 5, 6)
    w_out = w_out.reshape(width, 2 * half)
    w_ffn_gate = w_ffn_gate.reshape(W * r_ffn, width)
    every = every[:, :pack_rows, :].reshape(n, pack_rows * 128)
    g_mix = every[:, 0:r_in].reshape(1, width)
    g_ffn = every[:, r_in : 2 * r_in].reshape(1, width)
    g_out = every[:, 2 * r_in : 3 * r_in].reshape(2, 2, Y, 2, 2 * r_in)
    g_out = lax.dynamic_index_in_dim(g_out, zlo, 1, keepdims=False)
    g_out = lax.dynamic_index_in_dim(g_out, x, 2, keepdims=False).reshape(1, 2 * half)

    def channels(vector):
        vector = vector.reshape(2, Y, 2, half // Y)
        vector = lax.dynamic_index_in_dim(vector, zlo, 0, keepdims=False)
        return lax.dynamic_index_in_dim(vector, x, 1, keepdims=False).reshape(1, half)

    lower = channels(every[:, 3 * r_in : 3 * r_in + r_f])
    angle = channels(every[:, 3 * r_in + r_f : 3 * r_in + 2 * r_f])
    par = jnp.concatenate(
        [lower, jnp.cos(angle), jnp.sin(angle), jnp.zeros((5, half), F32)], axis=0
    )

    inputs = tokens.astype(F32)
    r_tok = lax.rsqrt(jnp.mean(inputs * inputs, axis=-1, keepdims=True) + EPS)
    all32 = tok_all.astype(F32)
    r_all = lax.rsqrt(jnp.mean(all32 * all32, axis=-1, keepdims=True) + EPS)
    normed = (all32 * r_all * g_mix).astype(LOW)
    proj = contract(normed, w_mix)
    wide = ((half // LANES, total, LANES), F32)
    d_re, d_im, v_re, v_im, summ = plain_call(
        partial(forward_kernel, half, length),
        [wide] * 4 + [((4, 8, half), F32)],
        3,
        name="gates",
    )(proj, keep, par)
    summ_all = small_gather(lay, summ, lay.wmasks, partial(w_slot, lay), W, 1).reshape(n, 8, half)
    st_re, st_im, be_re, be_im, unit, squares = plain_call(
        partial(state_kernel, half, length, n),
        [wide] * 4 + [((total, 2 * half), LOW), ((total, LANES), F32)],
        8,
        smem=1,
        name="states",
    )(ints, summ_all, d_re, d_im, v_re, v_im, proj, g_out)
    branch_low = contract(unit, w_out).astype(LOW)

    def t_blocks(value):
        return [value[j * length : (j + 1) * length] for j in range(4)]

    got, got_squares, w_ffn_up = net_call(
        partial(scatter_kernel, lay),
        lay,
        (branch_low.reshape(4, length, width), squares.reshape(4, length, LANES), ffn_up.astype(LOW)),
        [((3, length, width), LOW), ((3, length, LANES), F32), ((W, r_ffn, width), LOW)],
        W - 1 + 6,
        2,
        4,
        "branch",
    )
    w_ffn_up = w_ffn_up.reshape(W * r_ffn, width)

    def own_sum(whole, arrived_parts):
        value = whole[:length].astype(F32)
        for j in range(3):
            value = value + arrived_parts[j].astype(F32)
        return value

    square = own_sum(squares, got_squares)[:, 0:1]
    branch = own_sum(branch_low, got)
    r_state = lax.rsqrt(square / width + EPS)
    residual = inputs + r_state * branch
    r_res = lax.rsqrt(jnp.mean(residual * residual, axis=-1, keepdims=True) + EPS)
    ffn_low = (residual * r_res * g_ffn).astype(LOW)

    ffn_all, w_down = net_call(
        partial(gather_both_kernel, lay),
        lay,
        (ffn_low, ffn_down.astype(LOW)),
        [((4, length, width), LOW), ((W, r_ffn, width), LOW)],
        W - 1 + 3,
        2,
        5,
        "ffn_in",
    )
    ffn_all = ffn_all.reshape(total, width)
    w_down = w_down.reshape(W * r_ffn, width)
    gate_value = contract(ffn_all, w_ffn_gate)
    up_value = contract(ffn_all, w_ffn_up)
    s_gate = jax.nn.sigmoid(gate_value)
    silu_gate = gate_value * s_gate
    hidden_low = (silu_gate * up_value).astype(LOW)
    grad_hidden = contract(cot_all, w_down)
    grad_gate = (grad_hidden * up_value * s_gate * (1.0 + gate_value * (1.0 - s_gate))).astype(LOW)
    grad_up = (grad_hidden * silu_gate).astype(LOW)
    du_low = (
        jnp.dot(grad_gate, w_ffn_gate, preferred_element_type=F32)
        + jnp.dot(grad_up, w_ffn_up, preferred_element_type=F32)
    ).astype(LOW)
    du = lay.scatter_t(t_blocks(du_low))
    mixed_low = jnp.dot(hidden_low, w_down, preferred_element_type=F32).astype(LOW)

    du_gain = du * g_ffn
    grad_residual = (
        cotangent.astype(F32)
        + r_res * du_gain
        - residual * (r_res * r_res * r_res) * jnp.mean(residual * du_gain, axis=-1, keepdims=True)
    )
    ffn_gain_part = jnp.sum(du * residual * r_res, axis=0)
    grad_low = grad_residual.astype(LOW)
    inner = jnp.sum(grad_low.astype(F32) * branch, axis=-1, keepdims=True) / width
    scale = jnp.concatenate([r_state, r_state * r_state * r_state * inner], axis=1)

    grad_all = jnp.concatenate(lay.gather_t(grad_low), axis=0)
    scale_all = jnp.concatenate(lay.gather_t(scale), axis=0)
    grad_mid = jnp.dot(grad_all, w_out, preferred_element_type=F32)
    gs_re, gs_im, gate_low, mid, out_gain_part, back = plain_call(
        partial(back_kernel, half, length),
        [wide] * 2
        + [((total, 2 * half), LOW)] * 2
        + [((8, 2 * half), F32), ((4, 8, half), F32)],
        8,
        scratch=[pltpu.VMEM((8, 2 * half), F32)],
        name="back_gates",
    )(grad_mid, st_re, st_im, proj, g_out, scale_all, d_re, d_im)
    back_all = small_gather(lay, back, lay.wmasks, partial(w_slot, lay), W, 2).reshape(n, 8, half)
    grads, lower_part, angle_part = plain_call(
        partial(adjoint_kernel, half, length, n),
        [((total, 5 * half), LOW), ((8, half), F32), ((8, half), F32)],
        13,
        smem=1,
        scratch=[pltpu.VMEM((half // LANES, total, LANES), F32)] * 2 + [pltpu.VMEM((16, half), F32)],
        name="adjoints",
    )(ints, summ_all, back_all, gs_re, gs_im, d_re, d_im, be_re, be_im, proj, keep, par, gate_low)
    du_mix_low = jnp.dot(grads, w_mix, preferred_element_type=F32).astype(LOW)
    mix_gain_part = jnp.sum(
        du_mix_low.astype(F32) * (all32 * r_all), axis=0
    )

    t_hot = ((jnp.arange(2)[:, None] == zlo) & (jnp.arange(2)[None, :] == x)).astype(F32)
    out_gain_part = jnp.sum(out_gain_part, axis=0).reshape(2, 1, Y, 1, 2 * r_in)
    out_gain_part = (out_gain_part * t_hot[None, :, None, :, None]).reshape(n, r_in)

    def spread(vector):
        vector = jnp.sum(vector, axis=0).reshape(1, Y, 1, half // Y)
        return (vector * t_hot[:, None, :, None]).reshape(n, r_f)

    to_owner = jnp.concatenate(
        [
            mix_gain_part.reshape(n, r_in),
            ffn_gain_part.reshape(n, r_in),
            out_gain_part,
            spread(lower_part),
            spread(angle_part),
        ],
        axis=1,
    )
    to_owner = jnp.pad(to_owner, ((0, 0), (0, 1024 - to_owner.shape[1]))).reshape(n, 8, 128)

    grad_w_out = outer_rows(grad_all, mid).astype(LOW).reshape(2, 2, Y, 2, 2, r_in, 2 * half)
    grad_w_out = grad_w_out.transpose(0, 2, 4, 1, 3, 5, 6).reshape(W, 4 * r_in, 2 * half)
    grad_w_mix = outer_rows(grads, normed).astype(LOW)
    parts = [
        grad_w_mix[4 * half :].reshape(W, r_f, width),
        grad_w_out,
        outer_rows(grad_gate, ffn_all).astype(LOW).reshape(W, r_ffn, width),
        outer_rows(grad_up, ffn_all).astype(LOW).reshape(W, r_ffn, width),
        outer_rows(hidden_low, cot_all).astype(LOW).reshape(W, r_ffn, width),
        grad_w_mix[: 2 * half].reshape(W, r_in, width),
        grad_w_mix[2 * half : 4 * half].reshape(W, r_in, width),
    ]
    scratch, copies, local_copies = [], 6 + 3 + n - 1, 2
    for part in parts:
        blocks, shape = W // 2, part.shape[1:]
        scratch.append(pltpu.VMEM((blocks,) + shape, LOW))
        local_copies += blocks + 1
        for _ in lay.rbits:
            scratch.append(pltpu.VMEM((blocks,) + shape, LOW))
            copies += blocks
            blocks //= 2
        scratch.append(pltpu.VMEM(shape, F32))
    forget_part, *w_grads, out_cols_grad, got_du, got_mixed, owned = net_call(
        partial(reduce_kernel, lay, len(parts)),
        lay,
        (
            *parts,
            du_mix_low.reshape(4, length, width),
            mixed_low.reshape(4, length, width),
            to_owner,
        ),
        [(part.shape[1:], F32) for i, part in enumerate(parts) if i != 1]
        + [
            ((4, r_in, 2 * half), F32),
            ((3, length, width), LOW),
            ((3, length, width), LOW),
            ((n, 8, 128), F32),
        ],
        copies,
        local_copies,
        3,
        "reduce",
        scratch,
    )
    ffn_gate_grad, ffn_up_grad, ffn_down_grad, in_proj_grad, gate_proj_grad = w_grads
    forget_proj_grad = lax.ppermute(forget_part, "dp", forget_from)
    out_proj_grad = (
        out_cols_grad.reshape(2, 2, r_in, 2, Y, 2 * r_in)
        .transpose(2, 3, 0, 4, 1, 5)
        .reshape(r_in, width)
    )
    owned = jnp.sum(owned, axis=0).reshape(-1)
    mixed_out = (residual + own_sum(mixed_low, got_mixed)).astype(LOW)
    du_mix = own_sum(du_mix_low, got_du)
    dg_mix = du_mix * g_mix
    tokens_grad = (
        grad_residual
        + r_tok * dg_mix
        - inputs * (r_tok * r_tok * r_tok) * jnp.mean(inputs * dg_mix, axis=-1, keepdims=True)
    ).astype(LOW)
    return (
        mixed_out,
        tokens_grad,
        in_proj_grad,
        forget_proj_grad,
        gate_proj_grad,
        out_proj_grad,
        ffn_gate_grad,
        ffn_up_grad,
        ffn_down_grad,
        owned[0:r_in],
        owned[2 * r_in : 3 * r_in],
        owned[r_in : 2 * r_in],
        owned[3 * r_in : 3 * r_in + r_f],
        owned[3 * r_in + r_f : 3 * r_in + 2 * r_f],
    )


def solution(mesh):
    rows, vector = P("dp", None), P("dp")
    in_specs = (rows, rows, P(), P()) + (rows,) * 7 + (vector,) * 5
    out_specs = (rows,) * 9 + (vector,) * 5
    return jax.shard_map(
        partial(local, mesh.shape["dp"]),
        mesh=mesh,
        in_specs=in_specs,
        out_specs=out_specs,
        check_vma=False,
    )
```

```python
from functools import partial

import jax
import jax.numpy as jnp
from jax import lax
from jax.experimental import pallas as pl
from jax.experimental.pallas import tpu as pltpu
from jax.sharding import PartitionSpec as P


EPS = 1e-06
LOW = jnp.bfloat16
F32 = jnp.float32
MESH = pl.DeviceIdType.MESH
ROWS = 32
LANES = 128


def contract(left_rows, right_rows):
    return lax.dot_general(
        left_rows, right_rows, (((1,), (1,)), ((), ())), preferred_element_type=F32
    )


def outer_rows(left_rows, right_rows):
    return lax.dot_general(
        left_rows, right_rows, (((0,), (0,)), ((), ())), preferred_element_type=F32
    )


def tie(value, *others):
    return lax.optimization_barrier((value,) + others)[0]


class Layout:
    def __init__(self, n):
        self.n = n
        self.Y = n // 16
        self.C, self.X, self.ZL, self.ZH = 1, 2, 4 * self.Y, 8 * self.Y
        self.ybits = []
        bit = 4
        while bit < self.ZL:
            self.ybits.append(bit)
            bit *= 2
        self.wbits = [self.ZH] + self.ybits + [self.C]
        self.rbits = [self.C] + self.ybits + [self.ZH]
        self.tmasks = [0, self.X, self.ZL, self.ZL | self.X]
        self.wmasks = [0]
        for bit in self.wbits:
            self.wmasks = self.wmasks + [m | bit for m in self.wmasks]
        self.bits = [1 << k for k in range(n.bit_length() - 1)]

    def rel_slot(self, mask):
        return ((mask % 2) * self.Y + (mask // 4) % self.Y) * 2 + mask // self.ZH

    def flip(self, device, mask):
        for bit in self.bits:
            if mask & bit:
                device = device + bit * (1 - 2 * ((device // bit) % 2))
        return device

    def parts(self, device):
        c = device % 2
        x = (device // self.X) % 2
        y = (device // 4) % self.Y
        zlo = (device // self.ZL) % 2
        zhi = device // self.ZH
        return zhi, zlo, y, x, c

    def send(self, value, mask):
        return lax.ppermute(value, "dp", [(i, i ^ mask) for i in range(self.n)])

    def gather_t(self, value):
        return [value] + [self.send(value, m) for m in self.tmasks[1:]]

    def scatter_t(self, blocks):
        got = [self.send(b, m) for b, m in zip(blocks[1:], self.tmasks[1:])]
        total = blocks[0].astype(F32)
        for g in got:
            total = total + g.astype(F32)
        return total

    def gather_w(self, value):
        pieces = [value]
        for bit in self.wbits:
            pieces = pieces + [self.send(v, bit) for v in pieces]
        return pieces


def gather_kernel(lay, masks, slot_of, in_ref, out_ref, send_sems, recv_sems):
    me = lax.axis_index("dp")
    peers = [lay.flip(me, m) for m in masks]
    barrier = pltpu.get_barrier_semaphore()
    for peer in peers:
        pl.semaphore_signal(barrier, inc=1, device_id=(peer,), device_id_type=MESH)
    pl.semaphore_wait(barrier, len(peers))
    slot = slot_of(me)
    copies = []
    for i, peer in enumerate(peers):
        copy = pltpu.make_async_remote_copy(
            src_ref=in_ref,
            dst_ref=out_ref.at[slot],
            send_sem=send_sems.at[i],
            recv_sem=recv_sems.at[i],
            device_id=(peer,),
            device_id_type=MESH,
        )
        copy.start()
        copies.append(copy)
    out_ref[slot] = in_ref[...]
    for copy in copies:
        copy.wait()


def small_gather(lay, value, masks, slot_of, slots, collective_id):
    masks = [m for m in masks if m]
    vmem = pl.BlockSpec(memory_space=pltpu.VMEM)
    return pl.pallas_call(
        partial(gather_kernel, lay, masks, slot_of),
        out_shape=jax.ShapeDtypeStruct((slots,) + value.shape, value.dtype),
        in_specs=[vmem],
        out_specs=vmem,
        scratch_shapes=[
            pltpu.SemaphoreType.DMA((len(masks),)),
            pltpu.SemaphoreType.DMA((len(masks),)),
        ],
        compiler_params=pltpu.CompilerParams(collective_id=collective_id, has_side_effects=True),
        cost_estimate=estimate(10),
    )(value)


class Net:
    def __init__(self, lay, peers, send_sems, recv_sems, local_sems, rooms=()):
        self.lay, self.send_sems, self.recv_sems, self.local_sems = lay, send_sems, recv_sems, local_sems
        self.rooms, self.moving = list(rooms), []
        self.me = lax.axis_index("dp")
        self.used, self.used_local, self.open, self.local = 0, 0, [], []
        barrier = pltpu.get_barrier_semaphore()
        for mask in peers:
            pl.semaphore_signal(
                barrier, inc=1, device_id=(lay.flip(self.me, mask),), device_id_type=MESH
            )
        pl.semaphore_wait(barrier, len(peers))

    def put(self, src, dst, mask):
        copy = pltpu.make_async_remote_copy(
            src_ref=src,
            dst_ref=dst,
            send_sem=self.send_sems.at[self.used],
            recv_sem=self.recv_sems.at[self.used],
            device_id=(self.lay.flip(self.me, mask),),
            device_id_type=MESH,
        )
        copy.start()
        self.used += 1
        self.open.append(copy)
        return copy

    def load(self, src, dst):
        copy = pltpu.make_async_copy(src, dst, self.local_sems.at[self.used_local])
        copy.start()
        self.used_local += 1
        return copy

    def keep(self, src, dst):
        self.local.append(self.load(src, dst))

    def move(self, src, dst):
        room = self.rooms.pop(0)
        self.moving.append((self.load(src, room), room, dst))

    def settle(self):
        for copy, room, dst in self.moving:
            copy.wait()
            self.keep(room, dst)
        self.moving = []

    def finish(self):
        for copy in self.open:
            copy.wait_send()
        for copy in self.local:
            copy.wait()


class WeightGather:
    def __init__(self, net, own, place, ahead=None):
        self.net, self.own, self.place, self.ahead = net, own, place, ahead
        self.bits = net.lay.wbits
        self.pending = {}

    def start(self):
        me = self.net.me
        if self.ahead is None:
            self.pending[self.bits[0]] = self.net.put(
                self.own, self.place(me, self.bits[0]), self.bits[0]
            )
        for bit in self.bits[1:]:
            self.pending[bit] = self.net.put(self.own, self.place(me, bit), bit)
        self.net.move(self.own, self.place(me, 0))
        if self.ahead is not None:
            self.pass_on(self.bits[0], self.ahead)
            self.net.move(self.ahead, self.place(self.net.lay.flip(me, self.bits[0]), self.bits[0]))

    def masks(self):
        out = [0]
        for bit in self.bits[:-1]:
            out = out + [m | bit for m in out]
        out = sorted(out[1:], key=lambda m: (bin(m).count("1"), -m))
        return [m for m in out if self.ahead is None or m != self.bits[0]]

    def pass_on(self, mask, block):
        last = max(i for i, bit in enumerate(self.bits) if mask & bit)
        source = self.net.lay.flip(self.net.me, mask)
        for bit in self.bits[last + 1 :]:
            self.pending[mask | bit] = self.net.put(block, self.place(source, mask | bit), bit)

    def forward(self, mask):
        self.pending[mask].wait_recv()
        self.pass_on(mask, self.place(self.net.lay.flip(self.net.me, mask), mask))

    def end(self):
        for mask, copy in self.pending.items():
            if mask & self.bits[-1]:
                copy.wait_recv()


def token_start(net, own, out):
    lay = net.lay
    first = [net.put(own, out.at[1], lay.X), net.put(own, out.at[2], lay.ZL)]
    net.move(own, out.at[0])
    return first


def token_finish(net, first, out):
    lay, half = net.lay, out.shape[1] // 2
    top, low = pl.ds(0, half), pl.ds(half, half)
    arrived(first[:1])
    copies = [net.put(out.at[1, top], out.at[3, top], lay.ZL)]
    arrived(first[1:])
    return copies + [net.put(out.at[2, low], out.at[3, low], lay.X)]


def token_scatter(net, blocks, out):
    return [net.put(blocks.at[j], out.at[j - 1], m) for j, m in enumerate(net.lay.tmasks) if j]


def arrived(copies):
    for copy in copies:
        copy.wait_recv()


def estimate(micros):
    return pl.CostEstimate(flops=micros * 1_000_000_000, bytes_accessed=0, transcendentals=0)


def net_call(body, lay, values, outs, copies, local, collective_id, name, micros, scratch=(), limit=None):
    hbm = pl.BlockSpec(memory_space=pl.ANY)
    return pl.pallas_call(
        body,
        out_shape=tuple(jax.ShapeDtypeStruct(s, d) for s, d in outs),
        in_specs=[hbm] * len(values),
        out_specs=tuple(hbm for _ in outs),
        scratch_shapes=[
            *scratch,
            pltpu.SemaphoreType.DMA((copies,)),
            pltpu.SemaphoreType.DMA((copies,)),
            pltpu.SemaphoreType.DMA((local,)),
        ],
        compiler_params=pltpu.CompilerParams(
            collective_id=collective_id,
            has_side_effects=True,
            vmem_limit_bytes=limit,
        ),
        cost_estimate=estimate(micros),
        name=name,
    )(*values)


def w_slot(lay, device):
    zhi, _, y, _, c = lay.parts(device)
    return (zhi * lay.Y + y) * 2 + c


def f_slot(lay, device):
    zhi, _, y, _, c = lay.parts(device)
    return (y * 2 + c) * 2 + zhi


def t_slot(lay, device):
    _, zlo, _, x, _ = lay.parts(device)
    return zlo * 2 + x


class Turn:
    def __init__(self, net, target, src, dst):
        self.remote = target != net.me
        self.away = pltpu.make_async_remote_copy(
            src_ref=src,
            dst_ref=dst,
            send_sem=net.send_sems.at[net.used],
            recv_sem=net.recv_sems.at[net.used],
            device_id=(target,),
            device_id_type=MESH,
        )
        self.here = pltpu.make_async_copy(src, dst, net.local_sems.at[net.used_local])
        net.used += 1
        net.used_local += 1

        @pl.when(self.remote)
        def _():
            self.away.start()

        @pl.when(jnp.logical_not(self.remote))
        def _():
            self.here.start()

    def wait(self):
        @pl.when(self.remote)
        def _():
            self.away.wait()

        @pl.when(jnp.logical_not(self.remote))
        def _():
            self.here.wait()


def forget_to(lay, device):
    return (device % 2) * (lay.n // 2) + device // 2


def forget_from(lay, device):
    return 2 * (device % (lay.n // 2)) + device // (lay.n // 2)


def start_kernel(
    lay, units, tok, w_in, w_gate, w_forget, w_out, pack,
    tok_all, mix_all, forget_own, out_own, out_all, every, *rest,
):
    n, W = lay.n, lay.n // 4
    *rooms, send_sems, recv_sems, local_sems = rest
    net = Net(lay, list(range(1, n)), send_sems, recv_sems, local_sems, rooms)
    me = net.me

    def region(base):
        return lambda d, m: mix_all.at[pl.ds(base + w_slot(lay, d) * units, units)]

    g_in = WeightGather(net, w_in, region(0))
    g_gate = WeightGather(net, w_gate, region(W * units))
    g_forget = WeightGather(
        net, forget_own, lambda d, m: mix_all.at[pl.ds(2 * W * units + f_slot(lay, d), 1)]
    )
    g_out = WeightGather(net, out_own, lambda d, m: out_all.at[w_slot(lay, d)])
    turn = Turn(net, forget_to(lay, me), w_forget, forget_own)
    g_in.start()
    g_gate.start()
    mine = t_slot(lay, me)
    own = net.load(w_out.at[mine], out_own.at[mine])
    out_in = [
        net.put(w_out.at[t_slot(lay, lay.flip(me, m))], out_own.at[mine], m) for m in lay.tmasks[1:]
    ]
    first = token_start(net, tok, tok_all)
    all_in = [net.put(pack, every.at[me], m) for m in range(1, n)]
    net.keep(pack, every.at[me])
    turn.wait()
    g_forget.start()
    own.wait()
    arrived(out_in)
    g_out.start()
    net.settle()
    for mask in g_in.masks():
        g_in.forward(mask)
        g_gate.forward(mask)
    rest = token_finish(net, first, tok_all)
    for mask in g_forget.masks():
        g_forget.forward(mask)
        g_out.forward(mask)
    for gather in (g_in, g_gate, g_forget, g_out):
        gather.end()
    arrived(rest)
    arrived(all_in)
    net.finish()


def group_peers(lay):
    return lay.tmasks[1:] + lay.wbits


def rel_gather(net, own, ahead, out):
    return WeightGather(net, own, lambda d, m: out.at[net.lay.rel_slot(m)], ahead)


def scatter_kernel(lay, blocks, small, weight, ahead, other, got, got_small, weight_all, other_got, *rest):
    *rooms, send_sems, recv_sems, local_sems = rest
    net = Net(lay, group_peers(lay), send_sems, recv_sems, local_sems, rooms)
    gather = rel_gather(net, weight, ahead, weight_all)
    waits = token_scatter(net, blocks, got) + token_scatter(net, small, got_small)
    gather.start()
    net.settle()
    for mask in gather.masks():
        gather.forward(mask)
    waits.append(net.put(other, other_got, lay.ybits[0]))
    gather.end()
    arrived(waits)
    net.finish()


def gather_kernel_both(lay, own, weight, ahead, own_all, weight_all, *rest):
    *rooms, send_sems, recv_sems, local_sems = rest
    net = Net(lay, group_peers(lay), send_sems, recv_sems, local_sems, rooms)
    first = token_start(net, own, own_all)
    gather = rel_gather(net, weight, ahead, weight_all)
    gather.start()
    net.settle()
    rest = token_finish(net, first, own_all)
    for mask in gather.masks():
        gather.forward(mask)
    gather.end()
    arrived(rest)
    net.finish()


def gather_kernel_two(lay, own, small, own_all, small_all, *rest):
    *rooms, send_sems, recv_sems, local_sems = rest
    net = Net(lay, lay.tmasks[1:], send_sems, recv_sems, local_sems, rooms)
    first = token_start(net, own, own_all)
    net.move(small, small_all.at[0])
    waits = [net.put(small, small_all.at[j], m) for j, m in enumerate(lay.tmasks) if j]
    net.settle()
    rest = token_finish(net, first, own_all)
    arrived(waits + rest)
    net.finish()


def add_rows(out, left, right):
    rows = left.shape[0]
    tile = 16 if rows % 16 == 0 else rows

    def body(i, _):
        at = pl.ds(pl.multiple_of(i * tile, tile), tile)
        out[at, :] = (left[at, :].astype(F32) + right[at, :].astype(F32)).astype(out.dtype)
        return 0

    lax.fori_loop(0, rows // tile, body, 0)


class WeightReduce:
    def __init__(self, net, bits, part, place, local, stages, total, away=None):
        self.net, self.bits, self.part, self.place, self.away = net, bits, part, place, away
        self.local, self.stages, self.total = local, stages, total
        self.sent, self.waited = [], -1

    def pick(self, k, i, away):
        if self.away is not None:
            return i + (self.stages[k].shape[0] if away and k else 0)
        side = (self.net.me // self.bits[k]) % 2
        return 2 * i + (1 - side if away else side)

    def start(self):
        count = self.stages[0].shape[0]
        self.sent = [
            self.net.put(
                (self.part if self.away is None else self.away).at[self.place(self.pick(0, i, True))],
                self.stages[0].at[i],
                self.bits[0],
            )
            for i in range(count)
        ]
        self.loads = [
            self.net.load(self.part.at[self.place(self.pick(0, i, False))], self.local.at[i])
            for i in range(count)
        ]

    def wait(self, k):
        if self.waited < k:
            arrived(self.sent)
            self.waited = k

    def add(self, k):
        stage = self.stages[k]
        count = stage.shape[0]
        if k == 0:
            for copy in self.loads:
                copy.wait()

        def one(i):
            old = self.local.at[i] if k == 0 else self.stages[k - 1].at[self.pick(k, i, False)]
            add_rows(self.total if count == 1 else stage.at[i], stage.at[i], old)

        if count == 1:
            one(0)
        else:
            for away in (True, False):
                for i in range(count // 2):
                    one(self.pick(k + 1, i, away))

    def send(self, k):
        self.sent = [
            self.net.put(self.stages[k - 1].at[self.pick(k, i, True)], self.stages[k].at[i], self.bits[k])
            for i in range(self.stages[k].shape[0])
        ]


PARTS = (("forget", 0), ("out", 0), ("down", 1), ("gate", 0), ("in", 0))


def forget_place(lay, slot):
    return ((slot // 2) % lay.Y * 2 + slot % 2) * 2 + slot // (2 * lay.Y)


def reduce_kernel(lay, *refs):
    count = len(PARTS)
    parts, refs = refs[:count], refs[count:]
    (away, up, du, vectors), refs = refs[:4], refs[4:]
    outs, refs = refs[:count], refs[count:]
    (got_up, got_du, all_vectors), refs = refs[:3], refs[3:]
    scratch, (send_sems, recv_sems, local_sems) = list(refs[:-3]), refs[-3:]
    net = Net(lay, list(range(1, lay.n)), send_sems, recv_sems, local_sems)
    me = net.me
    jobs, turns, waits = [], [], []
    for (name, first), part in zip(PARTS, parts):
        bits = lay.rbits[first:]
        local = scratch.pop(0)
        stages = [scratch.pop(0) for _ in bits]
        place = partial(forget_place, lay) if name == "forget" else lambda k: k
        jobs.append(
            WeightReduce(
                net, bits, part, place, local, stages, scratch.pop(0), away if name == "down" else None
            )
        )
    jobs[0].start()
    jobs[1].start()
    jobs[2].start()
    waits += [net.put(up, got_up, lay.ZH)]
    waits += token_scatter(net, du, got_du)
    jobs[3].start()
    jobs[4].start()
    waits += [net.put(vectors.at[lay.flip(me, m)], all_vectors.at[me], m) for m in range(1, lay.n)]
    net.keep(vectors.at[me], all_vectors.at[me])

    def finish(i):
        total, out = jobs[i].total, outs[i]
        if PARTS[i][0] == "forget":
            turns.append(Turn(net, forget_from(lay, me), total, out))
        elif PARTS[i][0] == "out":
            rows = total.shape[0] // 4
            mine = t_slot(lay, me)

            def cut(slot):
                return total.at[pl.ds(pl.multiple_of(slot * rows, rows), rows)]

            net.keep(cut(mine), out.at[mine])
            for m in lay.tmasks[1:]:
                waits.append(net.put(cut(t_slot(lay, lay.flip(me, m))), out.at[mine], m))
        else:
            net.keep(total, out)

    depth = len(lay.rbits)
    for tick in range(count + depth - 1):
        for stage in range(depth):
            i = tick - stage
            valid = 0 <= i < count
            k = stage - PARTS[i][1] if valid else 0
            if valid and k >= 0:
                jobs[i].wait(k)
                jobs[i].add(k)
            if stage + 1 < depth:
                if 0 <= i - 1 < count:
                    ahead = stage + 1 - PARTS[i - 1][1]
                    if ahead >= 0:
                        jobs[i - 1].wait(ahead)
                if valid and k >= 0:
                    jobs[i].send(k + 1)
            elif valid:
                finish(i)
    arrived(waits)
    for turn in turns:
        turn.wait()
    net.finish()


def sig(v):
    return 1.0 / (1.0 + jnp.exp(-v))


def lanes(base, h):
    return slice(base + h * LANES, base + (h + 1) * LANES)


def fold_rows(v):
    return jnp.sum(v.reshape(v.shape[0] // 8, 8, v.shape[1]), axis=0)


def forward_kernel(half, length, proj, keep, par, d_re, d_im, v_re, v_im, summ):
    total = d_re.shape[1]
    blocks = total // length
    tiles = half // LANES

    def terms(i, _):
        rows = pl.ds(pl.multiple_of(i * ROWS, ROWS), ROWS)
        kept = keep[rows, :]
        for h in range(tiles):
            at = slice(h * LANES, (h + 1) * LANES)
            lower = par[0:1, at]
            magnitude = lower + (1.0 - lower) * sig(proj[rows, lanes(4 * half, h)])
            rest = 1.0 - magnitude
            d_re[h, rows, :] = kept * magnitude * par[1:2, at]
            d_im[h, rows, :] = kept * magnitude * par[2:3, at]
            a = proj[rows, lanes(0, h)]
            b = proj[rows, lanes(half, h)]
            v_re[h, rows, :] = a * sig(a) * rest
            v_im[h, rows, :] = b * sig(b) * rest
        return 0

    lax.fori_loop(0, total // ROWS, terms, 0)

    def step(t, carry):
        rows = pl.ds(t, blocks, stride=length)
        out = []
        for h in range(tiles):
            p_re, p_im, s_re, s_im = carry[4 * h : 4 * h + 4]
            dr, di = d_re[h, rows, :], d_im[h, rows, :]
            out += [
                dr * p_re - di * p_im,
                dr * p_im + di * p_re,
                dr * s_re - di * s_im + v_re[h, rows, :],
                dr * s_im + di * s_re + v_im[h, rows, :],
            ]
        return tuple(out)

    zero = jnp.zeros((blocks, LANES), F32)
    ends = lax.fori_loop(0, length, step, (zero + 1.0, zero, zero, zero) * tiles, unroll=4)
    for j in range(blocks):
        summ[j, 4:8, :] = jnp.zeros((4, half), F32)
        for h in range(tiles):
            for k in range(4):
                summ[j, k : k + 1, lanes(0, h)] = ends[4 * h + k][j : j + 1, :]


def chain_blocks(half, n, blocks, ints, summ, back):
    tiles = half // LANES

    def chain(i, carry):
        p = i if back is None else n - 1 - i
        tile = summ[ints[p]]
        shift = tile[2:4, :] if back is None else back[ints[p]]
        out = []
        for h in range(tiles):
            at = slice(h * LANES, (h + 1) * LANES)
            old = carry[h * (2 + 2 * blocks) : (h + 1) * (2 + 2 * blocks)]
            c_re, c_im = old[0], old[1]
            a_re = tile[0:1, at]
            a_im = tile[1:2, at] if back is None else -tile[1:2, at]
            out.append(a_re * c_re - a_im * c_im + shift[0:1, at])
            out.append(a_re * c_im + a_im * c_re + shift[1:2, at])
            for j in range(blocks):
                here = ints[n + j] == p
                out.append(jnp.where(here, c_re, old[2 + 2 * j]))
                out.append(jnp.where(here, c_im, old[3 + 2 * j]))
        return tuple(out)

    first = summ[0]
    zero = first[0:1, 0:LANES] - first[0:1, 0:LANES]
    res = lax.fori_loop(0, n, chain, (zero,) * (tiles * (2 + 2 * blocks)))
    entry = []
    for h in range(tiles):
        old = res[h * (2 + 2 * blocks) : (h + 1) * (2 + 2 * blocks)]
        entry.append(jnp.concatenate([old[2 + 2 * j] for j in range(blocks)], axis=0))
        entry.append(jnp.concatenate([old[3 + 2 * j] for j in range(blocks)], axis=0))
    return tuple(entry)


def state_kernel(
    half, length, n, ints, summ, d_re, d_im, v_re, v_im, proj, gain,
    st_re, st_im, be_re, be_im, unit, squares,
):
    total = d_re.shape[1]
    blocks = total // length
    tiles = half // LANES

    def step(t, carry):
        rows = pl.ds(t, blocks, stride=length)
        out = []
        for h in range(tiles):
            s_re, s_im = carry[2 * h], carry[2 * h + 1]
            be_re[h, rows, :] = s_re
            be_im[h, rows, :] = s_im
            dr, di = d_re[h, rows, :], d_im[h, rows, :]
            n_re = dr * s_re - di * s_im + v_re[h, rows, :]
            n_im = dr * s_im + di * s_re + v_im[h, rows, :]
            st_re[h, rows, :] = n_re
            st_im[h, rows, :] = n_im
            out += [n_re, n_im]
        return tuple(out)

    entry = chain_blocks(half, n, blocks, ints, summ, None)
    lax.fori_loop(0, length, step, entry, unroll=4)

    def finish(i, _):
        rows = pl.ds(pl.multiple_of(i * ROWS, ROWS), ROWS)
        square = jnp.zeros((ROWS, 1), F32)
        for h in range(tiles):
            for part, st in ((0, st_re), (1, st_im)):
                v = st[h, rows, :]
                g = proj[rows, lanes((2 + part) * half, h)]
                at = lanes(part * half, h)
                unit[rows, at] = (v * gain[0:1, at] * (g * sig(g))).astype(LOW)
                square = square + jnp.sum(v * v, axis=1, keepdims=True)
        squares[rows, :] = jnp.broadcast_to(square, (ROWS, LANES))
        return 0

    lax.fori_loop(0, total // ROWS, finish, 0)


def back_kernel(
    half, length, grad_mid, st_re, st_im, proj, gain, scale, d_re, d_im,
    gs_re, gs_im, gate_low, mid, gain_grad, summ, acc,
):
    total = d_re.shape[1]
    blocks = total // length
    tiles = half // LANES
    acc[...] = jnp.zeros_like(acc)

    def terms(i, _):
        rows = pl.ds(pl.multiple_of(i * ROWS, ROWS), ROWS)
        r = scale[rows, 0:1]
        q = scale[rows, 1:2]
        for h in range(tiles):
            for part, st, gs in ((0, st_re, gs_re), (1, st_im, gs_im)):
                at = lanes(part * half, h)
                g = proj[rows, lanes((2 + part) * half, h)]
                v = st[h, rows, :]
                gv = gain[0:1, at]
                dm = grad_mid[rows, at]
                sg = sig(g)
                silu = g * sg
                du = dm * silu
                normed = v * r
                scaled = normed * gv
                mid[rows, at] = (scaled * silu).astype(LOW)
                gate_low[rows, at] = (dm * scaled * (sg * (1.0 + g * (1.0 - sg)))).astype(LOW)
                gs[h, rows, :] = du * gv * r - v * q
                acc[:, at] = acc[:, at] + fold_rows(du * normed)
        return 0

    lax.fori_loop(0, total // ROWS, terms, 0)
    gain_grad[...] = acc[...]

    def step(i, carry):
        rows = pl.ds(length - 1 - i, blocks, stride=length)
        out = []
        for h in range(tiles):
            a_re = gs_re[h, rows, :] + carry[2 * h]
            a_im = gs_im[h, rows, :] + carry[2 * h + 1]
            dr, di = d_re[h, rows, :], d_im[h, rows, :]
            out += [dr * a_re + di * a_im, dr * a_im - di * a_re]
        return tuple(out)

    zero = jnp.zeros((blocks, LANES), F32)
    ends = lax.fori_loop(0, length, step, (zero, zero) * tiles, unroll=4)
    for j in range(blocks):
        summ[j, 2:8, :] = jnp.zeros((6, half), F32)
        for h in range(tiles):
            for k in range(2):
                summ[j, k : k + 1, lanes(0, h)] = ends[2 * h + k][j : j + 1, :]


def adjoint_kernel(
    half, length, n, ints, summ, back, gs_re, gs_im, d_re, d_im, be_re, be_im, proj, keep, par, gate_low,
    grads, lower_grad, angle_grad, ad_re, ad_im, acc,
):
    total = d_re.shape[1]
    blocks = total // length
    tiles = half // LANES

    def step(i, carry):
        rows = pl.ds(length - 1 - i, blocks, stride=length)
        out = []
        for h in range(tiles):
            a_re = gs_re[h, rows, :] + carry[2 * h]
            a_im = gs_im[h, rows, :] + carry[2 * h + 1]
            ad_re[h, rows, :] = a_re
            ad_im[h, rows, :] = a_im
            dr, di = d_re[h, rows, :], d_im[h, rows, :]
            out += [dr * a_re + di * a_im, dr * a_im - di * a_re]
        return tuple(out)

    entry = chain_blocks(half, n, blocks, ints, summ, back)
    lax.fori_loop(0, length, step, entry, unroll=4)
    acc[...] = jnp.zeros_like(acc)

    def terms(i, _):
        rows = pl.ds(pl.multiple_of(i * ROWS, ROWS), ROWS)
        kept = keep[rows, :]
        for h in range(tiles):
            at = slice(h * LANES, (h + 1) * LANES)
            lower, cos, sin = par[0:1, at], par[1:2, at], par[2:3, at]
            sf = sig(proj[rows, lanes(4 * half, h)])
            magnitude = lower + (1.0 - lower) * sf
            rest = 1.0 - magnitude
            a = proj[rows, lanes(0, h)]
            b = proj[rows, lanes(half, h)]
            sa, sb = sig(a), sig(b)
            ar, ai = ad_re[h, rows, :], ad_im[h, rows, :]
            br, bi = be_re[h, rows, :], be_im[h, rows, :]
            g_re = ar * br + ai * bi
            g_im = ai * br - ar * bi
            g_mag = kept * (g_re * cos + g_im * sin) - (ar * (a * sa) + ai * (b * sb))
            acc[0:8, at] = acc[0:8, at] + fold_rows(g_mag * (1.0 - sf))
            acc[8:16, at] = acc[8:16, at] + fold_rows(kept * magnitude * (g_im * cos - g_re * sin))
            grads[rows, lanes(0, h)] = (ar * rest * (sa * (1.0 + a * (1.0 - sa)))).astype(LOW)
            grads[rows, lanes(half, h)] = (ai * rest * (sb * (1.0 + b * (1.0 - sb)))).astype(LOW)
            grads[rows, lanes(4 * half, h)] = (g_mag * (1.0 - lower) * sf * (1.0 - sf)).astype(LOW)
        grads[rows, 2 * half : 4 * half] = gate_low[rows, :]
        return 0

    lax.fori_loop(0, total // ROWS, terms, 0)
    lower_grad[...] = acc[0:8, :]
    angle_grad[...] = acc[8:16, :]


VMEM = pl.BlockSpec(memory_space=pltpu.VMEM)
SMEM = pl.BlockSpec(memory_space=pltpu.SMEM)


def plain_call(body, outs, n_in, smem=0, scratch=(), name=None):
    return pl.pallas_call(
        body,
        out_shape=tuple(jax.ShapeDtypeStruct(s, d) for s, d in outs),
        in_specs=[SMEM] * smem + [VMEM] * (n_in - smem),
        out_specs=tuple(VMEM for _ in outs),
        scratch_shapes=list(scratch),
        compiler_params=pltpu.CompilerParams(vmem_limit_bytes=48 << 20),
        cost_estimate=estimate(7),
        name=name,
    )


def local(
    n,
    tokens,
    cotangent,
    seq_lengths,
    block_deal,
    in_proj,
    forget_proj,
    gate_proj,
    out_proj,
    ffn_gate,
    ffn_up,
    ffn_down,
    gain_mix,
    gain_out,
    gain_ffn,
    lower_bound,
    rotation,
):
    lay = Layout(n)
    Y = lay.Y
    W = n // 4
    me = lax.axis_index("dp")
    zhi, zlo, y, x, c = lay.parts(me)
    mine_t = zlo * 2 + x
    length, width = tokens.shape
    half = width // 8
    total = 4 * length
    r_in, r_f = in_proj.shape[0], forget_proj.shape[0]

    indices = jnp.arange(n, dtype=jnp.int32)
    order = jnp.sum(jnp.where(block_deal[None, :] == indices[:, None], indices[None, :], 0), axis=1)
    t_devices = jnp.stack([lay.flip(me, m) for m in lay.tmasks])
    t_places = jnp.sum(
        jnp.where(t_devices[:, None] == indices[None, :], block_deal[None, :], 0), axis=1
    )
    o_parts = lay.parts(order)
    t_rel = ((o_parts[1] + zlo) % 2) * 2 + (o_parts[3] + x) % 2
    ints = jnp.concatenate([w_slot(lay, order) * 4 + t_rel, t_places]).astype(jnp.int32)
    offsets = jnp.cumsum(seq_lengths) - seq_lengths
    positions = (
        t_places[:, None] * length + jnp.arange(length, dtype=jnp.int32)[None, :]
    ).reshape(-1)
    starts = jnp.any(positions[:, None] == offsets[None, :], axis=1)
    keep = jnp.where(starts, 0.0, 1.0).astype(F32)[:, None]

    packed = jnp.concatenate([gain_mix, gain_ffn, gain_out, lower_bound, rotation])
    pack_rows = -(-packed.shape[0] // 128)
    packed = jnp.pad(packed, (0, 8 * 128 - packed.shape[0])).reshape(8, 128)
    out_cols = out_proj.astype(LOW).reshape(r_in, 2, 2, Y, 2, 2 * r_in)
    out_cols = out_cols.transpose(2, 4, 0, 1, 3, 5).reshape(4, r_in, 2 * half)
    units = r_in // r_f
    r_ffn = ffn_gate.shape[0]
    tok_all, w_mix, _, _, w_out, every = net_call(
        partial(start_kernel, lay, units),
        lay,
        (
            tokens,
            in_proj.astype(LOW).reshape(units, r_f, width),
            gate_proj.astype(LOW).reshape(units, r_f, width),
            forget_proj.astype(LOW).reshape(1, r_f, width),
            out_cols,
            packed,
        ),
        [
            ((4, length, width), LOW),
            ((W * (2 * units + 1), r_f, width), LOW),
            ((1, r_f, width), LOW),
            ((4, r_in, 2 * half), LOW),
            ((W, 4, r_in, 2 * half), LOW),
            ((n, 8, 128), F32),
        ],
        4 * (W - 1) + 8 + n - 1,
        24,
        0,
        "start",
        60,
        [
            pltpu.VMEM((units, r_f, width), LOW),
            pltpu.VMEM((units, r_f, width), LOW),
            pltpu.VMEM((length, width), LOW),
            pltpu.VMEM((1, r_f, width), LOW),
            pltpu.VMEM((4, r_in, 2 * half), LOW),
        ],
    )
    f_gate, f_up, f_down = lax.optimization_barrier(
        (ffn_gate.astype(LOW), ffn_up.astype(LOW), ffn_down.astype(LOW), every)
    )[:3]
    gate_z = lay.send(f_gate, lay.ZH)
    tok_all = tok_all.reshape(total, width)
    w_mix = w_mix.reshape(5 * half, width)
    w_out = w_out.reshape(2, Y, 2, 2, 2, r_in, 2 * half).transpose(0, 3, 1, 4, 2, 5, 6)
    w_out = w_out.reshape(width, 2 * half)
    every = every[:, :pack_rows, :].reshape(n, pack_rows * 128)
    g_mix = every[:, 0:r_in].reshape(1, width)
    g_ffn = every[:, r_in : 2 * r_in].reshape(1, width)
    g_out = every[:, 2 * r_in : 3 * r_in].reshape(2, 2, Y, 2, 2 * r_in)
    g_out = lax.dynamic_index_in_dim(g_out, zlo, 1, keepdims=False)
    g_out = lax.dynamic_index_in_dim(g_out, x, 2, keepdims=False).reshape(1, 2 * half)

    def channels(vector):
        vector = vector.reshape(2, Y, 2, half // Y)
        vector = lax.dynamic_index_in_dim(vector, zlo, 0, keepdims=False)
        return lax.dynamic_index_in_dim(vector, x, 1, keepdims=False).reshape(1, half)

    lower = channels(every[:, 3 * r_in : 3 * r_in + r_f])
    angle = channels(every[:, 3 * r_in + r_f : 3 * r_in + 2 * r_f])
    par = jnp.concatenate(
        [lower, jnp.cos(angle), jnp.sin(angle), jnp.zeros((5, half), F32)], axis=0
    )

    inputs = tokens.astype(F32)
    r_tok = lax.rsqrt(jnp.mean(inputs * inputs, axis=-1, keepdims=True) + EPS)
    all32 = tok_all.astype(F32)
    r_all = lax.rsqrt(jnp.mean(all32 * all32, axis=-1, keepdims=True) + EPS)
    normed = (all32 * r_all * g_mix).astype(LOW)
    proj = contract(normed, w_mix)
    wide = ((half // LANES, total, LANES), F32)
    d_re, d_im, v_re, v_im, summ = plain_call(
        partial(forward_kernel, half, length),
        [wide] * 4 + [((4, 8, half), F32)],
        3,
        name="gates",
    )(proj, keep, par)
    summ_all = small_gather(lay, summ, lay.wmasks, partial(w_slot, lay), W, 1).reshape(n, 8, half)
    cot_blocks = lay.gather_t(tie(cotangent, summ_all))
    up_z = lay.send(tie(f_up, gate_z, summ_all), lay.ZH)
    st_re, st_im, be_re, be_im, unit, squares = plain_call(
        partial(state_kernel, half, length, n),
        [wide] * 4 + [((total, 2 * half), LOW), ((total, LANES), F32)],
        8,
        smem=1,
        name="states",
    )(ints, summ_all, d_re, d_im, v_re, v_im, proj, g_out)
    branch_low = contract(unit, w_out).astype(LOW)

    def t_blocks(value):
        return [value[j * length : (j + 1) * length] for j in range(4)]

    got, got_squares, w_ffn_gate, down_y = net_call(
        partial(scatter_kernel, lay),
        lay,
        (branch_low.reshape(4, length, width), squares.reshape(4, length, LANES), f_gate, gate_z, f_down),
        [
            ((3, length, width), LOW),
            ((3, length, LANES), F32),
            ((W, r_ffn, width), LOW),
            ((r_ffn, width), LOW),
        ],
        W - 1 + 7,
        4,
        4,
        "branch",
        40,
        [pltpu.VMEM((r_ffn, width), LOW)] * 2,
    )
    w_ffn_gate = w_ffn_gate.reshape(W * r_ffn, width)
    down_z = lay.send(tie(f_down, up_z, got), lay.ZH)

    def own_sum(whole, arrived_parts):
        value = whole[:length].astype(F32)
        for j in range(3):
            value = value + arrived_parts[j].astype(F32)
        return value

    square = own_sum(squares, got_squares)[:, 0:1]
    branch = own_sum(branch_low, got)
    r_state = lax.rsqrt(square / width + EPS)
    residual = inputs + r_state * branch
    r_res = lax.rsqrt(jnp.mean(residual * residual, axis=-1, keepdims=True) + EPS)
    ffn_low = (residual * r_res * g_ffn).astype(LOW)

    ffn_all, w_ffn_up = net_call(
        partial(gather_kernel_both, lay),
        lay,
        (ffn_low, f_up, up_z),
        [((4, length, width), LOW), ((W, r_ffn, width), LOW)],
        W - 1 + 4,
        6,
        5,
        "ffn_in",
        40,
        [pltpu.VMEM((length, width), LOW)] + [pltpu.VMEM((r_ffn, width), LOW)] * 2,
    )
    ffn_all = ffn_all.reshape(total, width)
    w_ffn_up = w_ffn_up.reshape(W * r_ffn, width)
    down_pieces = [f_down, down_z]
    for bit in lay.ybits:
        first = [down_y] if bit == lay.ybits[0] else []
        down_pieces = down_pieces + first + [lay.send(v, bit) for v in down_pieces[len(first) :]]
    down_pieces[0] = tie(f_down, down_z)
    cot_all = jnp.concatenate(cot_blocks, axis=0)
    w_down = jnp.concatenate(down_pieces + [lay.send(v, lay.C) for v in down_pieces], axis=0)
    gate_value = contract(ffn_all, w_ffn_gate)
    up_value = contract(ffn_all, w_ffn_up)
    s_gate = jax.nn.sigmoid(gate_value)
    silu_gate = gate_value * s_gate
    hidden_low = (silu_gate * up_value).astype(LOW)
    grad_hidden = contract(cot_all, w_down)
    grad_gate = (grad_hidden * up_value * s_gate * (1.0 + gate_value * (1.0 - s_gate))).astype(LOW)
    grad_up = (grad_hidden * silu_gate).astype(LOW)
    du_low = (
        jnp.dot(grad_gate, w_ffn_gate, preferred_element_type=F32)
        + jnp.dot(grad_up, w_ffn_up, preferred_element_type=F32)
    ).astype(LOW)
    du = lay.scatter_t(t_blocks(du_low))

    def join(kept, got):
        return kept.astype(F32) + got.astype(F32)

    def split_sum(kept, got):
        rows = kept.shape[0] // 2
        return join(kept[:rows], got[:rows]).astype(LOW), join(kept[rows:], got[rows:]).astype(LOW)

    def over_core(part):
        rows = part.shape[0] // 2
        return split_sum(part[:rows], lay.send(part[rows:], lay.C))

    def over_y(kept, away):
        for bit in lay.ybits:
            kept, away = split_sum(kept, lay.send(away, bit))
        return kept, away

    left_gate, left_up, left_hidden, _ = lax.optimization_barrier(
        (grad_gate, grad_up, hidden_low, du_low)
    )
    gate_kept, gate_away = over_core(outer_rows(left_gate, ffn_all).astype(LOW))
    up_kept, up_away = over_core(outer_rows(left_up, ffn_all).astype(LOW))
    down_part = outer_rows(left_hidden, cot_all).astype(LOW)
    mixed_low = jnp.dot(left_hidden, w_down, preferred_element_type=F32).astype(LOW)

    du_gain = du * g_ffn
    grad_residual = (
        cotangent.astype(F32)
        + r_res * du_gain
        - residual * (r_res * r_res * r_res) * jnp.mean(residual * du_gain, axis=-1, keepdims=True)
    )
    ffn_gain_part = jnp.sum(du * residual * r_res, axis=0)
    grad_low = tie(grad_residual.astype(LOW), gate_away)
    inner = jnp.sum(grad_low.astype(F32) * branch, axis=-1, keepdims=True) / width
    scale = jnp.where(
        jnp.arange(LANES)[None, :] == 0, r_state, r_state * r_state * r_state * inner
    )

    grad_all, scale_all = net_call(
        partial(gather_kernel_two, lay),
        lay,
        (grad_low, scale),
        [((4, length, width), LOW), ((4, length, LANES), F32)],
        7,
        4,
        6,
        "grad_in",
        27,
        [pltpu.VMEM((length, width), LOW), pltpu.VMEM((length, LANES), F32)],
    )
    gate_kept, gate_away = over_y(gate_kept, gate_away)
    mixed_blocks = t_blocks(tie(mixed_low, grad_all))
    mixed = lay.scatter_t(mixed_blocks)
    mixed_out = (residual + mixed).astype(LOW)
    grad_all = grad_all.reshape(total, width)
    scale_all = scale_all.reshape(total, LANES)
    grad_mid = jnp.dot(grad_all, w_out, preferred_element_type=F32)
    gs_re, gs_im, gate_low, mid, out_gain_part, back = plain_call(
        partial(back_kernel, half, length),
        [wide] * 2
        + [((total, 2 * half), LOW)] * 2
        + [((8, 2 * half), F32), ((4, 8, half), F32)],
        8,
        scratch=[pltpu.VMEM((8, 2 * half), F32)],
        name="back_gates",
    )(grad_mid, st_re, st_im, proj, g_out, scale_all, d_re, d_im)
    back = tie(back, gate_away)
    back_all = small_gather(lay, back, lay.wmasks, partial(w_slot, lay), W, 2).reshape(n, 8, half)
    grads, lower_part, angle_part = plain_call(
        partial(adjoint_kernel, half, length, n),
        [((total, 5 * half), LOW), ((8, half), F32), ((8, half), F32)],
        13,
        smem=1,
        scratch=[pltpu.VMEM((half // LANES, total, LANES), F32)] * 2 + [pltpu.VMEM((16, half), F32)],
        name="adjoints",
    )(ints, summ_all, back_all, gs_re, gs_im, d_re, d_im, be_re, be_im, proj, keep, par, gate_low)
    du_mix_low = jnp.dot(grads, w_mix, preferred_element_type=F32).astype(LOW)
    mix_gain_part = jnp.sum(
        du_mix_low.astype(F32) * (all32 * r_all), axis=0
    )

    t_hot = ((jnp.arange(2)[:, None] == zlo) & (jnp.arange(2)[None, :] == x)).astype(F32)
    out_gain_part = jnp.sum(out_gain_part, axis=0).reshape(2, 1, Y, 1, 2 * r_in)
    out_gain_part = (out_gain_part * t_hot[None, :, None, :, None]).reshape(n, r_in)

    def spread(vector):
        vector = jnp.sum(vector, axis=0).reshape(1, Y, 1, half // Y)
        return (vector * t_hot[:, None, :, None]).reshape(n, r_f)

    to_owner = jnp.concatenate(
        [
            mix_gain_part.reshape(n, r_in),
            ffn_gain_part.reshape(n, r_in),
            out_gain_part,
            spread(lower_part),
            spread(angle_part),
        ],
        axis=1,
    )
    to_owner = jnp.pad(to_owner, ((0, 0), (0, 1024 - to_owner.shape[1]))).reshape(n, 8, 128)

    grad_w_out = outer_rows(grad_all, mid).astype(LOW).reshape(2, 2, Y, 2, 2, r_in, 2 * half)
    grad_w_out = grad_w_out.transpose(0, 2, 4, 1, 3, 5, 6).reshape(W, 4 * r_in, 2 * half)
    grad_w_mix = outer_rows(grads, normed).astype(LOW)
    down_kept, down_away = over_core(down_part)
    up_kept, up_away = over_y(up_kept, tie(up_away, back_all))
    gate_got = lay.send(tie(gate_away, back_all), lay.ZH)
    du_mix_low = tie(du_mix_low, mixed_out, gate_got)
    parts = [
        grad_w_mix[4 * half :].reshape(W, r_f, width),
        grad_w_out,
        down_kept.reshape(W // 4, r_ffn, width),
        grad_w_mix[2 * half : 4 * half].reshape(W, r_in, width),
        grad_w_mix[: 2 * half].reshape(W, r_in, width),
    ]
    scratch, copies, local_copies = [], 6 + 3 + n + 2, 4
    for (_, first), part in zip(PARTS, parts):
        blocks, shape = W // 2 >> first, part.shape[1:]
        scratch.append(pltpu.VMEM((blocks,) + shape, LOW))
        local_copies += blocks + 1
        for _ in lay.rbits[first:]:
            scratch.append(pltpu.VMEM((blocks,) + shape, LOW))
            copies += blocks
            blocks //= 2
        scratch.append(pltpu.VMEM(shape, F32))
    forget_proj_grad, out_cols_grad, ffn_down_grad, gate_proj_grad, in_proj_grad, got_up, got_du, owned = net_call(
        partial(reduce_kernel, lay),
        lay,
        (
            *parts,
            down_away.reshape(W // 4, r_ffn, width),
            up_away,
            du_mix_low.reshape(4, length, width),
            to_owner,
        ),
        [
            ((r_f, width), F32),
            ((4, r_in, 2 * half), F32),
            ((r_ffn, width), F32),
            ((r_in, width), F32),
            ((r_in, width), F32),
            ((r_ffn, width), LOW),
            ((3, length, width), LOW),
            ((n, 8, 128), F32),
        ],
        copies,
        local_copies,
        3,
        "reduce",
        120,
        scratch,
        56 << 20,
    )
    ffn_gate_grad = join(gate_kept, gate_got)
    ffn_up_grad = join(up_kept, got_up)
    out_proj_grad = (
        out_cols_grad.reshape(2, 2, r_in, 2, Y, 2 * r_in)
        .transpose(2, 3, 0, 4, 1, 5)
        .reshape(r_in, width)
    )
    owned = jnp.sum(owned, axis=0).reshape(-1)
    du_mix = own_sum(du_mix_low, got_du)
    dg_mix = du_mix * g_mix
    tokens_grad = (
        grad_residual
        + r_tok * dg_mix
        - inputs * (r_tok * r_tok * r_tok) * jnp.mean(inputs * dg_mix, axis=-1, keepdims=True)
    ).astype(LOW)
    return (
        mixed_out,
        tokens_grad,
        in_proj_grad,
        forget_proj_grad,
        gate_proj_grad,
        out_proj_grad,
        ffn_gate_grad,
        ffn_up_grad,
        ffn_down_grad,
        owned[0:r_in],
        owned[2 * r_in : 3 * r_in],
        owned[r_in : 2 * r_in],
        owned[3 * r_in : 3 * r_in + r_f],
        owned[3 * r_in + r_f : 3 * r_in + 2 * r_f],
    )


def solution(mesh):
    rows, vector = P("dp", None), P("dp")
    in_specs = (rows, rows, P(), P()) + (rows,) * 7 + (vector,) * 5
    out_specs = (rows,) * 9 + (vector,) * 5
    return jax.shard_map(
        partial(local, mesh.shape["dp"]),
        mesh=mesh,
        in_specs=in_specs,
        out_specs=out_specs,
        check_vma=False,
    )
```

```python
from functools import partial

import jax
import jax.numpy as jnp
from jax import lax
from jax.experimental import pallas as pl
from jax.experimental.pallas import tpu as pltpu
from jax.sharding import PartitionSpec as P


EPS = 1e-06
LOW = jnp.bfloat16
F32 = jnp.float32
MESH = pl.DeviceIdType.MESH
ROWS = 32
LANES = 128


def contract(left_rows, right_rows):
    return lax.dot_general(
        left_rows, right_rows, (((1,), (1,)), ((), ())), preferred_element_type=F32
    )


def outer_rows(left_rows, right_rows):
    return lax.dot_general(
        left_rows, right_rows, (((0,), (0,)), ((), ())), preferred_element_type=F32
    )


def tie(value, *others):
    return lax.optimization_barrier((value,) + others)[0]


class Layout:
    def __init__(self, n):
        self.n = n
        self.Y = n // 16
        self.C, self.X, self.ZL, self.ZH = 1, 2, 4 * self.Y, 8 * self.Y
        self.ybits = []
        bit = 4
        while bit < self.ZL:
            self.ybits.append(bit)
            bit *= 2
        self.wbits = [self.ZH] + self.ybits + [self.C]
        self.rbits = [self.C] + self.ybits + [self.ZH]
        self.tmasks = [0, self.X, self.ZL, self.ZL | self.X]
        self.wmasks = [0]
        for bit in self.wbits:
            self.wmasks = self.wmasks + [m | bit for m in self.wmasks]
        self.bits = [1 << k for k in range(n.bit_length() - 1)]

    def rel_slot(self, mask):
        return ((mask % 2) * self.Y + (mask // 4) % self.Y) * 2 + mask // self.ZH

    def flip(self, device, mask):
        for bit in self.bits:
            if mask & bit:
                device = device + bit * (1 - 2 * ((device // bit) % 2))
        return device

    def parts(self, device):
        c = device % 2
        x = (device // self.X) % 2
        y = (device // 4) % self.Y
        zlo = (device // self.ZL) % 2
        zhi = device // self.ZH
        return zhi, zlo, y, x, c

    def send(self, value, mask):
        return lax.ppermute(value, "dp", [(i, i ^ mask) for i in range(self.n)])

    def gather_t(self, value):
        return [value] + [self.send(value, m) for m in self.tmasks[1:]]

    def scatter_t(self, blocks):
        got = [self.send(b, m) for b, m in zip(blocks[1:], self.tmasks[1:])]
        total = blocks[0].astype(F32)
        for g in got:
            total = total + g.astype(F32)
        return total

    def gather_w(self, value):
        pieces = [value]
        for bit in self.wbits:
            pieces = pieces + [self.send(v, bit) for v in pieces]
        return pieces


def gather_kernel(lay, masks, slot_of, in_ref, out_ref, send_sems, recv_sems):
    me = lax.axis_index("dp")
    peers = [lay.flip(me, m) for m in masks]
    barrier = pltpu.get_barrier_semaphore()
    for peer in peers:
        pl.semaphore_signal(barrier, inc=1, device_id=(peer,), device_id_type=MESH)
    pl.semaphore_wait(barrier, len(peers))
    slot = slot_of(me)
    copies = []
    for i, peer in enumerate(peers):
        copy = pltpu.make_async_remote_copy(
            src_ref=in_ref,
            dst_ref=out_ref.at[pl.ds(slot * in_ref.shape[0], in_ref.shape[0])],
            send_sem=send_sems.at[i],
            recv_sem=recv_sems.at[i],
            device_id=(peer,),
            device_id_type=MESH,
        )
        copy.start()
        copies.append(copy)
    out_ref[pl.ds(slot * in_ref.shape[0], in_ref.shape[0])] = in_ref[...]
    for copy in copies:
        copy.wait()


def small_gather(lay, value, masks, slot_of, slots, collective_id):
    masks = [m for m in masks if m]
    vmem = pl.BlockSpec(memory_space=pltpu.VMEM)
    return pl.pallas_call(
        partial(gather_kernel, lay, masks, slot_of),
        out_shape=jax.ShapeDtypeStruct((slots * value.shape[0],) + value.shape[1:], value.dtype),
        in_specs=[vmem],
        out_specs=vmem,
        scratch_shapes=[
            pltpu.SemaphoreType.DMA((len(masks),)),
            pltpu.SemaphoreType.DMA((len(masks),)),
        ],
        compiler_params=pltpu.CompilerParams(collective_id=collective_id, has_side_effects=True),
        cost_estimate=estimate(10),
    )(value)


class Net:
    def __init__(self, lay, peers, send_sems, recv_sems, local_sems, rooms=()):
        self.lay, self.send_sems, self.recv_sems, self.local_sems = lay, send_sems, recv_sems, local_sems
        self.rooms, self.moving = list(rooms), []
        self.me = lax.axis_index("dp")
        self.used, self.used_local, self.open, self.local = 0, 0, [], []
        barrier = pltpu.get_barrier_semaphore()
        for mask in peers:
            pl.semaphore_signal(
                barrier, inc=1, device_id=(lay.flip(self.me, mask),), device_id_type=MESH
            )
        pl.semaphore_wait(barrier, len(peers))

    def put(self, src, dst, mask):
        copy = pltpu.make_async_remote_copy(
            src_ref=src,
            dst_ref=dst,
            send_sem=self.send_sems.at[self.used],
            recv_sem=self.recv_sems.at[self.used],
            device_id=(self.lay.flip(self.me, mask),),
            device_id_type=MESH,
        )
        copy.start()
        self.used += 1
        self.open.append(copy)
        return copy

    def load(self, src, dst):
        copy = pltpu.make_async_copy(src, dst, self.local_sems.at[self.used_local])
        copy.start()
        self.used_local += 1
        return copy

    def keep(self, src, dst):
        self.local.append(self.load(src, dst))

    def move(self, src, dst):
        room = self.rooms.pop(0)
        self.moving.append((self.load(src, room), room, dst))

    def settle(self):
        for copy, room, dst in self.moving:
            copy.wait()
            self.keep(room, dst)
        self.moving = []

    def finish(self):
        for copy in self.open:
            copy.wait_send()
        for copy in self.local:
            copy.wait()


class WeightGather:
    def __init__(self, net, own, place, early=None):
        self.net, self.own, self.place, self.early = net, own, place, early or {}
        self.bits = net.lay.wbits
        self.pending = {}

    def start(self):
        me = self.net.me
        for bit in self.bits:
            if bit not in self.early:
                self.pending[bit] = self.net.put(self.own, self.place(me, bit), bit)
        self.net.move(self.own, self.place(me, 0))
        for bit, block in self.early.items():
            self.pass_on(bit, block)
            self.net.move(block, self.place(self.net.lay.flip(me, bit), bit))

    def masks(self):
        out = [0]
        for bit in self.bits[:-1]:
            out = out + [m | bit for m in out]
        out = sorted(out[1:], key=lambda m: (bin(m).count("1"), -m))
        return [m for m in out if m not in self.early]

    def pass_on(self, mask, block):
        last = max(i for i, bit in enumerate(self.bits) if mask & bit)
        source = self.net.lay.flip(self.net.me, mask)
        for bit in self.bits[last + 1 :]:
            self.pending[mask | bit] = self.net.put(block, self.place(source, mask | bit), bit)

    def forward(self, mask):
        self.pending[mask].wait_recv()
        self.pass_on(mask, self.place(self.net.lay.flip(self.net.me, mask), mask))

    def end(self):
        for mask, copy in self.pending.items():
            if mask & self.bits[-1]:
                copy.wait_recv()


def token_start(net, own, out):
    lay = net.lay
    first = [net.put(own, out.at[1], lay.X), net.put(own, out.at[2], lay.ZL)]
    net.move(own, out.at[0])
    return first


def token_finish(net, first, out):
    lay, half = net.lay, out.shape[1] // 2
    top, low = pl.ds(0, half), pl.ds(half, half)
    arrived(first[:1])
    copies = [net.put(out.at[1, top], out.at[3, top], lay.ZL)]
    arrived(first[1:])
    return copies + [net.put(out.at[2, low], out.at[3, low], lay.X)]


def token_scatter(net, blocks, out):
    return [net.put(blocks.at[j], out.at[j - 1], m) for j, m in enumerate(net.lay.tmasks) if j]


def arrived(copies):
    for copy in copies:
        copy.wait_recv()


SCALE = 10_000_000


def estimate(micros):
    return pl.CostEstimate(flops=micros * SCALE, bytes_accessed=0, transcendentals=0)


def net_call(body, lay, values, outs, copies, local, collective_id, name, micros, scratch=()):
    hbm = pl.BlockSpec(memory_space=pl.ANY)
    return pl.pallas_call(
        body,
        out_shape=tuple(jax.ShapeDtypeStruct(s, d) for s, d in outs),
        in_specs=[hbm] * len(values),
        out_specs=tuple(hbm for _ in outs),
        scratch_shapes=[
            *scratch,
            pltpu.SemaphoreType.DMA((copies,)),
            pltpu.SemaphoreType.DMA((copies,)),
            pltpu.SemaphoreType.DMA((local,)),
        ],
        compiler_params=pltpu.CompilerParams(
            collective_id=collective_id,
            has_side_effects=True,
            vmem_limit_bytes=60 << 20,
        ),
        cost_estimate=estimate(micros),
        name=name,
    )(*values)


def w_slot(lay, device):
    zhi, _, y, _, c = lay.parts(device)
    return (zhi * lay.Y + y) * 2 + c


def f_slot(lay, device):
    zhi, _, y, _, c = lay.parts(device)
    return (y * 2 + c) * 2 + zhi


def t_slot(lay, device):
    _, zlo, _, x, _ = lay.parts(device)
    return zlo * 2 + x


class Turn:
    def __init__(self, net, target, src, dst):
        self.remote = target != net.me
        self.away = pltpu.make_async_remote_copy(
            src_ref=src,
            dst_ref=dst,
            send_sem=net.send_sems.at[net.used],
            recv_sem=net.recv_sems.at[net.used],
            device_id=(target,),
            device_id_type=MESH,
        )
        self.here = pltpu.make_async_copy(src, dst, net.local_sems.at[net.used_local])
        net.used += 1
        net.used_local += 1

        @pl.when(self.remote)
        def _():
            self.away.start()

        @pl.when(jnp.logical_not(self.remote))
        def _():
            self.here.start()

    def wait(self):
        @pl.when(self.remote)
        def _():
            self.away.wait()

        @pl.when(jnp.logical_not(self.remote))
        def _():
            self.here.wait()


def forget_to(lay, device):
    return (device % 2) * (lay.n // 2) + device // 2


def forget_from(lay, device):
    return 2 * (device % (lay.n // 2)) + device // (lay.n // 2)


def start_kernel(
    lay, units, tok, w_in, w_gate, w_forget, w_out, f_gate, pack,
    tok_all, mix_all, forget_own, out_own, out_all, f_gate_z, every, *rest,
):
    n, W = lay.n, lay.n // 4
    *rooms, send_sems, recv_sems, local_sems = rest
    net = Net(lay, list(range(1, n)), send_sems, recv_sems, local_sems, rooms)
    me = net.me

    def region(base):
        return lambda d, m: mix_all.at[pl.ds(base + w_slot(lay, d) * units, units)]

    g_in = WeightGather(net, w_in, region(0))
    g_gate = WeightGather(net, w_gate, region(W * units))
    g_forget = WeightGather(
        net, forget_own, lambda d, m: mix_all.at[pl.ds(2 * W * units + f_slot(lay, d), 1)]
    )
    g_out = WeightGather(net, out_own, lambda d, m: out_all.at[w_slot(lay, d)])
    turn = Turn(net, forget_to(lay, me), w_forget, forget_own)
    g_in.start()
    g_gate.start()
    mine = t_slot(lay, me)
    own = net.load(w_out.at[mine], out_own.at[mine])
    out_in = [
        net.put(w_out.at[t_slot(lay, lay.flip(me, m))], out_own.at[mine], m) for m in lay.tmasks[1:]
    ]
    first = token_start(net, tok, tok_all)
    all_in = [net.put(pack, every.at[me], m) for m in range(1, n)]
    net.keep(pack, every.at[me])
    turn.wait()
    g_forget.start()
    own.wait()
    arrived(out_in)
    g_out.start()
    gate_in = net.put(f_gate, f_gate_z, lay.ZH)
    net.settle()
    for mask in g_in.masks():
        g_in.forward(mask)
        g_gate.forward(mask)
    rest = token_finish(net, first, tok_all)
    for mask in g_forget.masks():
        g_forget.forward(mask)
        g_out.forward(mask)
    for gather in (g_in, g_gate, g_forget, g_out):
        gather.end()
    arrived(rest + [gate_in])
    arrived(all_in)
    net.finish()


def group_peers(lay):
    return lay.tmasks[1:] + lay.wbits


def rel_gather(net, own, early, out):
    return WeightGather(net, own, lambda d, m: out.at[net.lay.rel_slot(m)], early)


def branch_kernel(lay, blocks, small, gate, gate_z, down, got_x, got_z, got_small, gate_all, down_y, down_z, *rest):
    token_rooms, rest = rest[:2], rest[2:]
    *rooms, send_sems, recv_sems, local_sems = rest
    net = Net(lay, group_peers(lay), send_sems, recv_sems, local_sems, rooms)
    gather = rel_gather(net, gate, {lay.ZH: gate_z}, gate_all)
    gather.start()
    waits = [net.put(down, down_z, lay.ZH)]
    tokens = TokenReduce(net, blocks, got_x, got_z, *token_rooms)
    waits += token_scatter(net, small, got_small)
    net.settle()
    for mask in gather.masks():
        gather.forward(mask)
    waits.append(net.put(down, down_y, lay.ybits[0]))
    tokens.pass_on()
    gather.end()
    tokens.end()
    arrived(waits)
    net.finish()


def ffn_kernel(lay, own, up, up_z, down, down_y, down_z, *rest):
    cot_blocks, (own_all, up_all, down_all, cot_all), rest = rest[:4], rest[4:8], rest[8:]
    *rooms, send_sems, recv_sems, local_sems = rest
    net = Net(lay, group_peers(lay), send_sems, recv_sems, local_sems, rooms)
    first = token_start(net, own, own_all)
    g_up = rel_gather(net, up, {lay.ZH: up_z}, up_all)
    g_down = rel_gather(net, down, {lay.ZH: down_z, lay.ybits[0]: down_y}, down_all)
    g_up.start()
    g_down.start()
    for j, block in enumerate(cot_blocks):
        net.move(block, cot_all.at[j])
    net.settle()
    rest = token_finish(net, first, own_all)
    for mask in g_up.masks():
        g_up.forward(mask)
    for mask in g_down.masks():
        g_down.forward(mask)
    g_up.end()
    g_down.end()
    arrived(rest)
    net.finish()


def add_rows(out, left, right):
    rows = left.shape[0]
    tile = 16 if rows % 16 == 0 else rows

    def body(i, _):
        at = pl.ds(pl.multiple_of(i * tile, tile), tile)
        out[at, :] = (left[at, :].astype(F32) + right[at, :].astype(F32)).astype(out.dtype)
        return 0

    lax.fori_loop(0, rows // tile, body, 0)


class WeightReduce:
    def __init__(self, net, part, rows, dims, local, stages, total, relative, leaves=None, came=None):
        self.net, self.part, self.rows, self.relative = net, part, rows, relative
        self.local, self.stages, self.total = local, stages, total
        self.leaves, self.came = leaves, came
        self.first = 0 if leaves is None and came is None else 1
        self.bits = net.lay.rbits[self.first :]
        self.dims = [[d for d in dims if d in self.bits]]
        for bit in self.bits:
            self.dims.append([d for d in self.dims[-1] if d != bit])
        self.copy, self.waited = None, -1

    def side(self, k):
        return 0 if self.relative else (self.net.me // self.bits[k]) % 2

    def cut(self, k, away):
        index = [slice(None)] * len(self.dims[k])
        index[self.dims[k].index(self.bits[k])] = 1 - self.side(k) if away else self.side(k)
        if k:
            return self.stages[k - 1].at[tuple(index)]
        return self.part.at[tuple(index) + self.rows]

    def start(self):
        if self.first == 0:
            self.copy = self.net.put(self.cut(0, True), self.stages[0], self.bits[0])
            self.loaded = self.net.load(self.cut(0, False), self.local)
            return
        index = (slice(None),) * len(self.dims[1]) + self.rows
        self.loaded = self.net.load(self.part.at[index] if self.rows else self.part, self.local)
        if self.came is None:
            block = self.leaves.at[index] if self.rows else self.leaves
            self.copy = self.net.put(block, self.stages[0], self.bits[0])
        else:
            block = self.came.at[index] if self.rows else self.came
            self.copy = self.net.load(block, self.stages[0])

    def wait(self, k):
        if self.waited < k:
            if k == 0 and self.came is not None:
                self.copy.wait()
            else:
                self.copy.wait_recv()
            self.waited = k

    def add(self, k, away):
        if k == 0 and away:
            self.loaded.wait()
        stage = self.stages[k]
        old = self.cut(k, False) if k else self.local
        if k + 1 == len(self.bits):
            if away:
                add_rows(self.total, stage, old)
            return
        dims = self.dims[k + 1]
        place = dims.index(self.bits[k + 1])
        side = 1 - self.side(k + 1) if away else self.side(k + 1)
        for number in range(1 << (len(dims) - 1)):
            index = [(number >> j) & 1 for j in range(len(dims) - 1)]
            index = tuple(index[:place] + [side] + index[place:])
            add_rows(stage.at[index], stage.at[index], old.at[index])

    def send(self, k):
        self.copy = self.net.put(self.cut(k, True), self.stages[k], self.bits[k])


def grad_kernel(lay, own, small, gate, up, down, own_all, small_all, *rest):
    outs, (room, small_room, *scratch), (send_sems, recv_sems, local_sems) = rest[:6], rest[6:-3], rest[-3:]
    net = Net(lay, lay.tmasks[1:] + [lay.C], send_sems, recv_sems, local_sems, [room, small_room])
    first = token_start(net, own, own_all)
    waits = [net.put(small, small_all.at[j], m) for j, m in enumerate(lay.tmasks) if j]
    net.move(small, small_all.at[0])
    dims = part_dims(lay, "up")
    jobs = []
    for j, part in enumerate((gate, up, down)):
        local, stage = scratch[2 * j : 2 * j + 2]
        jobs.append(WeightReduce(net, part, (), dims, local, [stage], None, True))
        jobs[-1].start()
    net.settle()
    for j, job in enumerate(jobs):
        job.wait(0)
        job.add(0, True)
        net.keep(job.cut(1, True), outs[2 * j + 1])
        job.add(0, False)
        net.keep(job.cut(1, False), outs[2 * j])
        if j == 0:
            waits += token_finish(net, first, own_all)
    arrived(waits)
    net.finish()


def row_cuts(name, rows):
    if name not in ("up", "down") or rows % 16 or rows < 128:
        return [(0, rows)]
    first = -(-rows // 32) * 16
    return [(0, first), (first, rows - first)]


PARTS = ("up", "forget", "out", "down", "gate", "in")


class TokenReduce:
    def __init__(self, net, blocks, got_x, got_z, room, other):
        lay = net.lay
        self.net, self.room, self.other, self.got_z = net, room, other, got_z
        self.first = [net.put(blocks.at[3], other, lay.X), net.put(blocks.at[1], got_x, lay.X)]
        self.loaded = net.load(blocks.at[2], room)

    def pass_on(self):
        self.first[0].wait_recv()
        self.loaded.wait()
        add_rows(self.room, self.room, self.other)
        self.last = self.net.put(self.room, self.got_z, self.net.lay.ZL)

    def end(self):
        arrived([self.first[1], self.last])


def first_stage(name):
    return 1 if name in ("up", "down") else 0


def part_dims(lay, name):
    y_bits = list(reversed(lay.ybits))
    if name == "forget":
        return y_bits + [lay.C, lay.ZH]
    if name in ("up", "down"):
        return [lay.C] + y_bits + [lay.ZH]
    return [lay.ZH] + y_bits + [lay.C]


LAG = 2


def reduce_kernel(lay, *refs):
    count = len(PARTS)
    parts, refs = refs[:count], refs[count:]
    (up_came, down_leaves, du, mixed, vectors), refs = refs[:5], refs[5:]
    outs, refs = refs[:count], refs[count:]
    (du_x, du_z, mixed_x, mixed_z, all_vectors), refs = refs[:5], refs[5:]
    token_rooms, refs = refs[:4], refs[4:]
    scratch, (send_sems, recv_sems, local_sems) = list(refs[:-3]), refs[-3:]
    net = Net(lay, list(range(1, lay.n)), send_sems, recv_sems, local_sems)
    me = net.me
    jobs, places, turns, waits = [], [], [], []
    for name, part, out in zip(PARTS, parts, outs):
        for first, rows in row_cuts(name, part.shape[-2]):
            local = scratch.pop(0)
            stages = [scratch.pop(0) for _ in lay.rbits[first_stage(name) :]]
            whole = rows == part.shape[-2]
            at = () if whole else (pl.ds(first, rows),)
            relative = name in ("up", "down")
            dims = part_dims(lay, name)
            jobs.append(
                WeightReduce(
                    net,
                    part,
                    at,
                    dims,
                    local,
                    stages,
                    scratch.pop(0),
                    relative,
                    down_leaves if name == "down" else None,
                    up_came if name == "up" else None,
                )
            )
            places.append((name, out if whole else out.at[pl.ds(first, rows)]))
    flows = [[] for _ in lay.rbits]
    late = []
    for job, (name, _) in zip(jobs, places):
        if name in ("gate", "in"):
            late.append(job)
        else:
            job.start()
            if name == "down":
                flows[1].append(job)
    du_sum = TokenReduce(net, du, du_x, du_z, *token_rooms[:2])

    def finish(i):
        total = jobs[i].total
        name, out = places[i]
        if name == "forget":
            turns.append(Turn(net, forget_from(lay, me), total, out))
        elif name == "out":
            rows = total.shape[0] // 4
            mine = t_slot(lay, me)

            def cut(slot):
                return total.at[pl.ds(pl.multiple_of(slot * rows, rows), rows)]

            net.keep(cut(mine), out.at[mine])
            for m in lay.tmasks[1:]:
                waits.append(net.put(cut(t_slot(lay, lay.flip(me, m))), out.at[mine], m))
        else:
            net.keep(total, out)

    depth = len(lay.rbits)
    for tick in range(len(jobs) + depth - 1):
        for k in range(depth):
            i = tick - k
            if not 0 <= i < len(jobs) or k + jobs[i].first >= depth:
                continue
            job = jobs[i]
            job.wait(k)
            job.add(k, True)
            flow = k + 1 + job.first
            if flow == depth:
                finish(i)
                continue
            if len(flows[flow]) >= LAG:
                behind = flows[flow][-LAG]
                behind.wait(flow - behind.first)
            job.send(k + 1)
            flows[flow].append(job)
            job.add(k, False)
        if tick == 0:
            for job in late:
                job.start()
        if tick == 1:
            waits += [
                net.put(vectors.at[lay.flip(me, m)], all_vectors.at[me], m) for m in range(1, lay.n)
            ]
            net.keep(vectors.at[me], all_vectors.at[me])
            mixed_sum = TokenReduce(net, mixed, mixed_x, mixed_z, *token_rooms[2:])
        if tick == 3:
            du_sum.pass_on()
        if tick == 5:
            mixed_sum.pass_on()
    du_sum.end()
    mixed_sum.end()
    arrived(waits)
    for turn in turns:
        turn.wait()
    net.finish()


def sig(v):
    return 1.0 / (1.0 + jnp.exp(-v))


def lanes(base, h):
    return slice(base + h * LANES, base + (h + 1) * LANES)


def fold_rows(v):
    return jnp.sum(v.reshape(v.shape[0] // 8, 8, v.shape[1]), axis=0)


def forward_kernel(half, length, proj, keep, par, d_re, d_im, v_re, v_im, summ):
    total = d_re.shape[1]
    blocks = total // length
    tiles = half // LANES

    def terms(i, _):
        rows = pl.ds(pl.multiple_of(i * ROWS, ROWS), ROWS)
        kept = keep[rows, :]
        for h in range(tiles):
            at = slice(h * LANES, (h + 1) * LANES)
            lower = par[0:1, at]
            magnitude = lower + (1.0 - lower) * sig(proj[rows, lanes(4 * half, h)])
            rest = 1.0 - magnitude
            d_re[h, rows, :] = kept * magnitude * par[1:2, at]
            d_im[h, rows, :] = kept * magnitude * par[2:3, at]
            a = proj[rows, lanes(0, h)]
            b = proj[rows, lanes(half, h)]
            v_re[h, rows, :] = a * sig(a) * rest
            v_im[h, rows, :] = b * sig(b) * rest
        return 0

    lax.fori_loop(0, total // ROWS, terms, 0)

    def step(t, carry):
        rows = pl.ds(t, blocks, stride=length)
        out = []
        for h in range(tiles):
            p_re, p_im, s_re, s_im = carry[4 * h : 4 * h + 4]
            dr, di = d_re[h, rows, :], d_im[h, rows, :]
            out += [
                dr * p_re - di * p_im,
                dr * p_im + di * p_re,
                dr * s_re - di * s_im + v_re[h, rows, :],
                dr * s_im + di * s_re + v_im[h, rows, :],
            ]
        return tuple(out)

    zero = jnp.zeros((blocks, LANES), F32)
    ends = lax.fori_loop(0, length, step, (zero + 1.0, zero, zero, zero) * tiles, unroll=4)
    for j in range(blocks):
        summ[j, 4:8, :] = jnp.zeros((4, half), F32)
        for h in range(tiles):
            for k in range(4):
                summ[j, k : k + 1, lanes(0, h)] = ends[4 * h + k][j : j + 1, :]


def chain_blocks(half, n, blocks, ints, summ, back):
    tiles = half // LANES

    def chain(i, carry):
        p = i if back is None else n - 1 - i
        tile = summ[ints[p]]
        shift = tile[2:4, :] if back is None else back[ints[p]]
        out = []
        for h in range(tiles):
            at = slice(h * LANES, (h + 1) * LANES)
            old = carry[h * (2 + 2 * blocks) : (h + 1) * (2 + 2 * blocks)]
            c_re, c_im = old[0], old[1]
            a_re = tile[0:1, at]
            a_im = tile[1:2, at] if back is None else -tile[1:2, at]
            out.append(a_re * c_re - a_im * c_im + shift[0:1, at])
            out.append(a_re * c_im + a_im * c_re + shift[1:2, at])
            for j in range(blocks):
                here = ints[n + j] == p
                out.append(jnp.where(here, c_re, old[2 + 2 * j]))
                out.append(jnp.where(here, c_im, old[3 + 2 * j]))
        return tuple(out)

    first = summ[0]
    zero = first[0:1, 0:LANES] - first[0:1, 0:LANES]
    res = lax.fori_loop(0, n, chain, (zero,) * (tiles * (2 + 2 * blocks)))
    entry = []
    for h in range(tiles):
        old = res[h * (2 + 2 * blocks) : (h + 1) * (2 + 2 * blocks)]
        entry.append(jnp.concatenate([old[2 + 2 * j] for j in range(blocks)], axis=0))
        entry.append(jnp.concatenate([old[3 + 2 * j] for j in range(blocks)], axis=0))
    return tuple(entry)


def state_kernel(
    half, length, n, ints, summ, d_re, d_im, v_re, v_im, proj, gain,
    st_re, st_im, be_re, be_im, unit, squares,
):
    total = d_re.shape[1]
    blocks = total // length
    tiles = half // LANES

    def step(t, carry):
        rows = pl.ds(t, blocks, stride=length)
        out = []
        for h in range(tiles):
            s_re, s_im = carry[2 * h], carry[2 * h + 1]
            be_re[h, rows, :] = s_re
            be_im[h, rows, :] = s_im
            dr, di = d_re[h, rows, :], d_im[h, rows, :]
            n_re = dr * s_re - di * s_im + v_re[h, rows, :]
            n_im = dr * s_im + di * s_re + v_im[h, rows, :]
            st_re[h, rows, :] = n_re
            st_im[h, rows, :] = n_im
            out += [n_re, n_im]
        return tuple(out)

    entry = chain_blocks(half, n, blocks, ints, summ, None)
    lax.fori_loop(0, length, step, entry, unroll=4)

    def finish(i, _):
        rows = pl.ds(pl.multiple_of(i * ROWS, ROWS), ROWS)
        square = jnp.zeros((ROWS, 1), F32)
        for h in range(tiles):
            for part, st in ((0, st_re), (1, st_im)):
                v = st[h, rows, :]
                g = proj[rows, lanes((2 + part) * half, h)]
                at = lanes(part * half, h)
                unit[rows, at] = (v * gain[0:1, at] * (g * sig(g))).astype(LOW)
                square = square + jnp.sum(v * v, axis=1, keepdims=True)
        squares[rows, :] = jnp.broadcast_to(square, (ROWS, LANES))
        return 0

    lax.fori_loop(0, total // ROWS, finish, 0)


def back_kernel(
    half, length, grad_mid, st_re, st_im, proj, gain, scale, d_re, d_im,
    gs_re, gs_im, gate_low, mid, gain_grad, summ, acc,
):
    total = d_re.shape[1]
    blocks = total // length
    tiles = half // LANES
    acc[...] = jnp.zeros_like(acc)

    def terms(i, _):
        rows = pl.ds(pl.multiple_of(i * ROWS, ROWS), ROWS)
        r = scale[rows, 0:1]
        q = scale[rows, 1:2]
        for h in range(tiles):
            for part, st, gs in ((0, st_re, gs_re), (1, st_im, gs_im)):
                at = lanes(part * half, h)
                g = proj[rows, lanes((2 + part) * half, h)]
                v = st[h, rows, :]
                gv = gain[0:1, at]
                dm = grad_mid[rows, at]
                sg = sig(g)
                silu = g * sg
                du = dm * silu
                normed = v * r
                scaled = normed * gv
                mid[rows, at] = (scaled * silu).astype(LOW)
                gate_low[rows, at] = (dm * scaled * (sg * (1.0 + g * (1.0 - sg)))).astype(LOW)
                gs[h, rows, :] = du * gv * r - v * q
                acc[:, at] = acc[:, at] + fold_rows(du * normed)
        return 0

    lax.fori_loop(0, total // ROWS, terms, 0)
    gain_grad[...] = acc[...]

    def step(i, carry):
        rows = pl.ds(length - 1 - i, blocks, stride=length)
        out = []
        for h in range(tiles):
            a_re = gs_re[h, rows, :] + carry[2 * h]
            a_im = gs_im[h, rows, :] + carry[2 * h + 1]
            dr, di = d_re[h, rows, :], d_im[h, rows, :]
            out += [dr * a_re + di * a_im, dr * a_im - di * a_re]
        return tuple(out)

    zero = jnp.zeros((blocks, LANES), F32)
    ends = lax.fori_loop(0, length, step, (zero, zero) * tiles, unroll=4)
    for j in range(blocks):
        summ[j, 2:8, :] = jnp.zeros((6, half), F32)
        for h in range(tiles):
            for k in range(2):
                summ[j, k : k + 1, lanes(0, h)] = ends[2 * h + k][j : j + 1, :]


def adjoint_kernel(
    half, length, n, ints, summ, back, gs_re, gs_im, d_re, d_im, be_re, be_im, proj, keep, par, gate_low,
    grads, lower_grad, angle_grad, ad_re, ad_im, acc,
):
    total = d_re.shape[1]
    blocks = total // length
    tiles = half // LANES

    def step(i, carry):
        rows = pl.ds(length - 1 - i, blocks, stride=length)
        out = []
        for h in range(tiles):
            a_re = gs_re[h, rows, :] + carry[2 * h]
            a_im = gs_im[h, rows, :] + carry[2 * h + 1]
            ad_re[h, rows, :] = a_re
            ad_im[h, rows, :] = a_im
            dr, di = d_re[h, rows, :], d_im[h, rows, :]
            out += [dr * a_re + di * a_im, dr * a_im - di * a_re]
        return tuple(out)

    entry = chain_blocks(half, n, blocks, ints, summ, back)
    lax.fori_loop(0, length, step, entry, unroll=4)
    acc[...] = jnp.zeros_like(acc)

    def terms(i, _):
        rows = pl.ds(pl.multiple_of(i * ROWS, ROWS), ROWS)
        kept = keep[rows, :]
        for h in range(tiles):
            at = slice(h * LANES, (h + 1) * LANES)
            lower, cos, sin = par[0:1, at], par[1:2, at], par[2:3, at]
            sf = sig(proj[rows, lanes(4 * half, h)])
            magnitude = lower + (1.0 - lower) * sf
            rest = 1.0 - magnitude
            a = proj[rows, lanes(0, h)]
            b = proj[rows, lanes(half, h)]
            sa, sb = sig(a), sig(b)
            ar, ai = ad_re[h, rows, :], ad_im[h, rows, :]
            br, bi = be_re[h, rows, :], be_im[h, rows, :]
            g_re = ar * br + ai * bi
            g_im = ai * br - ar * bi
            g_mag = kept * (g_re * cos + g_im * sin) - (ar * (a * sa) + ai * (b * sb))
            acc[0:8, at] = acc[0:8, at] + fold_rows(g_mag * (1.0 - sf))
            acc[8:16, at] = acc[8:16, at] + fold_rows(kept * magnitude * (g_im * cos - g_re * sin))
            grads[rows, lanes(0, h)] = (ar * rest * (sa * (1.0 + a * (1.0 - sa)))).astype(LOW)
            grads[rows, lanes(half, h)] = (ai * rest * (sb * (1.0 + b * (1.0 - sb)))).astype(LOW)
            grads[rows, lanes(4 * half, h)] = (g_mag * (1.0 - lower) * sf * (1.0 - sf)).astype(LOW)
        grads[rows, 2 * half : 4 * half] = gate_low[rows, :]
        return 0

    lax.fori_loop(0, total // ROWS, terms, 0)
    lower_grad[...] = acc[0:8, :]
    angle_grad[...] = acc[8:16, :]


VMEM = pl.BlockSpec(memory_space=pltpu.VMEM)
SMEM = pl.BlockSpec(memory_space=pltpu.SMEM)


def plain_call(body, outs, n_in, smem=0, scratch=(), name=None):
    return pl.pallas_call(
        body,
        out_shape=tuple(jax.ShapeDtypeStruct(s, d) for s, d in outs),
        in_specs=[SMEM] * smem + [VMEM] * (n_in - smem),
        out_specs=tuple(VMEM for _ in outs),
        scratch_shapes=list(scratch),
        compiler_params=pltpu.CompilerParams(vmem_limit_bytes=48 << 20),
        cost_estimate=estimate(7),
        name=name,
    )


def local(
    n,
    tokens,
    cotangent,
    seq_lengths,
    block_deal,
    in_proj,
    forget_proj,
    gate_proj,
    out_proj,
    ffn_gate,
    ffn_up,
    ffn_down,
    gain_mix,
    gain_out,
    gain_ffn,
    lower_bound,
    rotation,
):
    lay = Layout(n)
    Y = lay.Y
    W = n // 4
    me = lax.axis_index("dp")
    zhi, zlo, y, x, c = lay.parts(me)
    mine_t = zlo * 2 + x
    length, width = tokens.shape
    half = width // 8
    total = 4 * length
    r_in, r_f = in_proj.shape[0], forget_proj.shape[0]

    indices = jnp.arange(n, dtype=jnp.int32)
    order = jnp.sum(jnp.where(block_deal[None, :] == indices[:, None], indices[None, :], 0), axis=1)
    t_devices = jnp.stack([lay.flip(me, m) for m in lay.tmasks])
    t_places = jnp.sum(
        jnp.where(t_devices[:, None] == indices[None, :], block_deal[None, :], 0), axis=1
    )
    o_parts = lay.parts(order)
    t_rel = ((o_parts[1] + zlo) % 2) * 2 + (o_parts[3] + x) % 2
    ints = jnp.concatenate([w_slot(lay, order) * 4 + t_rel, t_places]).astype(jnp.int32)
    offsets = jnp.cumsum(seq_lengths) - seq_lengths
    positions = (
        t_places[:, None] * length + jnp.arange(length, dtype=jnp.int32)[None, :]
    ).reshape(-1)
    starts = jnp.any(positions[:, None] == offsets[None, :], axis=1)
    keep = jnp.where(starts, 0.0, 1.0).astype(F32)[:, None]

    packed = jnp.concatenate([gain_mix, gain_ffn, gain_out, lower_bound, rotation])
    pack_rows = -(-packed.shape[0] // 128)
    packed = jnp.pad(packed, (0, 8 * 128 - packed.shape[0])).reshape(8, 128)
    out_cols = out_proj.astype(LOW).reshape(r_in, 2, 2, Y, 2, 2 * r_in)
    out_cols = out_cols.transpose(2, 4, 0, 1, 3, 5).reshape(4, r_in, 2 * half)
    units = r_in // r_f
    r_ffn = ffn_gate.shape[0]
    f_gate = ffn_gate.astype(LOW)
    tok_all, w_mix, _, _, w_out, gate_z, every = net_call(
        partial(start_kernel, lay, units),
        lay,
        (
            tokens,
            in_proj.astype(LOW).reshape(units, r_f, width),
            gate_proj.astype(LOW).reshape(units, r_f, width),
            forget_proj.astype(LOW).reshape(1, r_f, width),
            out_cols,
            f_gate,
            packed,
        ),
        [
            ((4, length, width), LOW),
            ((W * (2 * units + 1), r_f, width), LOW),
            ((1, r_f, width), LOW),
            ((4, r_in, 2 * half), LOW),
            ((W, 4, r_in, 2 * half), LOW),
            ((r_ffn, width), LOW),
            ((n, 8, 128), F32),
        ],
        4 * (W - 1) + 9 + n - 1,
        24,
        0,
        "start",
        60,
        [
            pltpu.VMEM((units, r_f, width), LOW),
            pltpu.VMEM((units, r_f, width), LOW),
            pltpu.VMEM((length, width), LOW),
            pltpu.VMEM((1, r_f, width), LOW),
            pltpu.VMEM((4, r_in, 2 * half), LOW),
        ],
    )
    f_up, f_down = ffn_up.astype(LOW), ffn_down.astype(LOW)
    tok_all = tok_all.reshape(total, width)
    w_mix = w_mix.reshape(5 * half, width)
    w_out = w_out.reshape(2, Y, 2, 2, 2, r_in, 2 * half).transpose(0, 3, 1, 4, 2, 5, 6)
    w_out = w_out.reshape(width, 2 * half)
    every = every[:, :pack_rows, :].reshape(n, pack_rows * 128)
    g_mix = every[:, 0:r_in].reshape(1, width)
    g_ffn = every[:, r_in : 2 * r_in].reshape(1, width)
    g_out = every[:, 2 * r_in : 3 * r_in].reshape(2, 2, Y, 2, 2 * r_in)
    g_out = lax.dynamic_index_in_dim(g_out, zlo, 1, keepdims=False)
    g_out = lax.dynamic_index_in_dim(g_out, x, 2, keepdims=False).reshape(1, 2 * half)

    def channels(vector):
        vector = vector.reshape(2, Y, 2, half // Y)
        vector = lax.dynamic_index_in_dim(vector, zlo, 0, keepdims=False)
        return lax.dynamic_index_in_dim(vector, x, 1, keepdims=False).reshape(1, half)

    lower = channels(every[:, 3 * r_in : 3 * r_in + r_f])
    angle = channels(every[:, 3 * r_in + r_f : 3 * r_in + 2 * r_f])
    par = jnp.concatenate(
        [lower, jnp.cos(angle), jnp.sin(angle), jnp.zeros((5, half), F32)], axis=0
    )

    inputs = tokens.astype(F32)
    r_tok = lax.rsqrt(jnp.mean(inputs * inputs, axis=-1, keepdims=True) + EPS)
    all32 = tok_all.astype(F32)
    r_all = lax.rsqrt(jnp.mean(all32 * all32, axis=-1, keepdims=True) + EPS)
    normed = (all32 * r_all * g_mix).astype(LOW)
    proj = contract(normed, w_mix)
    wide = ((half // LANES, total, LANES), F32)
    d_re, d_im, v_re, v_im, summ = plain_call(
        partial(forward_kernel, half, length),
        [wide] * 4 + [((4, 8, half), F32)],
        3,
        name="gates",
    )(proj, keep, par)
    summ_all = small_gather(lay, summ, lay.wmasks, partial(w_slot, lay), W, 1)
    cot_blocks = lay.gather_t(tie(cotangent, summ_all))
    up_z = lay.send(tie(f_up, summ_all), lay.ZH)
    st_re, st_im, be_re, be_im, unit, squares = plain_call(
        partial(state_kernel, half, length, n),
        [wide] * 4 + [((total, 2 * half), LOW), ((total, LANES), F32)],
        8,
        smem=1,
        name="states",
    )(ints, summ_all, d_re, d_im, v_re, v_im, proj, g_out)
    branch_low = contract(unit, w_out).astype(LOW)

    def t_blocks(value):
        return [value[j * length : (j + 1) * length] for j in range(4)]

    branch_x, branch_z, got_squares, w_ffn_gate, down_y, down_z = net_call(
        partial(branch_kernel, lay),
        lay,
        (branch_low.reshape(4, length, width), squares.reshape(4, length, LANES), f_gate, gate_z, f_down),
        [
            ((length, width), LOW),
            ((length, width), LOW),
            ((3, length, LANES), F32),
            ((W, r_ffn, width), LOW),
            ((r_ffn, width), LOW),
            ((r_ffn, width), LOW),
        ],
        W + 7,
        6,
        4,
        "branch",
        40,
        [pltpu.VMEM((length, width), LOW)] * 2 + [pltpu.VMEM((r_ffn, width), LOW)] * 2,
    )
    w_ffn_gate = w_ffn_gate.reshape(W * r_ffn, width)

    def own_sum(whole, arrived_parts):
        value = whole[:length].astype(F32)
        for part in arrived_parts:
            value = value + part.astype(F32)
        return value

    square = own_sum(squares, [got_squares[j] for j in range(3)])[:, 0:1]
    branch = own_sum(branch_low, (branch_x, branch_z))
    r_state = lax.rsqrt(square / width + EPS)
    residual = inputs + r_state * branch
    r_res = lax.rsqrt(jnp.mean(residual * residual, axis=-1, keepdims=True) + EPS)
    ffn_low = (residual * r_res * g_ffn).astype(LOW)

    ffn_all, w_ffn_up, w_down, cot_all = net_call(
        partial(ffn_kernel, lay),
        lay,
        (ffn_low, f_up, up_z, f_down, down_y, down_z, *cot_blocks),
        [
            ((4, length, width), LOW),
            ((W, r_ffn, width), LOW),
            ((W, r_ffn, width), LOW),
            ((4, length, width), LOW),
        ],
        2 * W + 4,
        20,
        5,
        "ffn_in",
        40,
        [pltpu.VMEM((length, width), LOW)]
        + [pltpu.VMEM((r_ffn, width), LOW)] * 5
        + [pltpu.VMEM((length, width), LOW)] * 4,
    )
    ffn_all = ffn_all.reshape(total, width)
    w_ffn_up = w_ffn_up.reshape(W * r_ffn, width)
    w_down = w_down.reshape(W * r_ffn, width)
    cot_all = cot_all.reshape(total, width)
    gate_value = contract(ffn_all, w_ffn_gate)
    up_value = contract(ffn_all, w_ffn_up)
    s_gate = jax.nn.sigmoid(gate_value)
    silu_gate = gate_value * s_gate
    hidden_low = (silu_gate * up_value).astype(LOW)
    grad_hidden = contract(cot_all, w_down)
    grad_gate = (grad_hidden * up_value * s_gate * (1.0 + gate_value * (1.0 - s_gate))).astype(LOW)
    grad_up = (grad_hidden * silu_gate).astype(LOW)
    du_low = (
        jnp.dot(grad_gate, w_ffn_gate, preferred_element_type=F32)
        + jnp.dot(grad_up, w_ffn_up, preferred_element_type=F32)
    ).astype(LOW)
    du_blocks = t_blocks(du_low)
    du_got = [lay.send(b, m) for b, m in zip(du_blocks[1:], lay.tmasks[1:])]
    du = du_blocks[0].astype(F32)
    for got in du_got:
        du = du + got.astype(F32)

    def join(kept, got):
        return kept.astype(F32) + got.astype(F32)

    def split_sum(kept, got):
        rows = kept.shape[0] // 2
        return join(kept[:rows], got[:rows]).astype(LOW), join(kept[rows:], got[rows:]).astype(LOW)

    def over_y(kept, away):
        for bit in lay.ybits:
            kept, away = split_sum(kept, lay.send(away, bit))
        return kept, away

    left_gate, left_up, left_hidden, *_ = lax.optimization_barrier(
        (grad_gate, grad_up, hidden_low, *du_blocks)
    )
    gate_part = outer_rows(left_gate, ffn_all).astype(LOW)
    up_part = outer_rows(left_up, ffn_all).astype(LOW)
    down_part = outer_rows(left_hidden, cot_all).astype(LOW)
    mixed_low = jnp.dot(tie(left_hidden, du_got[0]), w_down, preferred_element_type=F32).astype(LOW)

    du_gain = du * g_ffn
    grad_residual = (
        cotangent.astype(F32)
        + r_res * du_gain
        - residual * (r_res * r_res * r_res) * jnp.mean(residual * du_gain, axis=-1, keepdims=True)
    )
    ffn_gain_part = jnp.sum(du * residual * r_res, axis=0)
    grad_low = tie(grad_residual.astype(LOW), mixed_low)
    inner = jnp.sum(grad_low.astype(F32) * branch, axis=-1, keepdims=True) / width
    scale = jnp.where(
        jnp.arange(LANES)[None, :] == 0, r_state, r_state * r_state * r_state * inner
    )

    split = (2,) * len(lay.wbits)
    block = (r_ffn, width)
    grad_all, scale_all, gate_kept, gate_away, up_kept, up_away, down_kept, down_away = net_call(
        partial(grad_kernel, lay),
        lay,
        (grad_low, scale, *[part.reshape(split + block) for part in (gate_part, up_part, down_part)]),
        [((4, length, width), LOW), ((4, length, LANES), F32)] + [(split[2:] + block, LOW)] * 6,
        10,
        13,
        6,
        "grad_in",
        27,
        [pltpu.VMEM((length, width), LOW), pltpu.VMEM((length, LANES), F32)]
        + [pltpu.VMEM(split[1:] + block, LOW)] * 6,
    )
    gate_kept, gate_away = over_y(gate_kept.reshape(-1, width), gate_away.reshape(-1, width))
    grad_all = grad_all.reshape(total, width)
    scale_all = scale_all.reshape(total, LANES)
    grad_mid = jnp.dot(grad_all, w_out, preferred_element_type=F32)
    gs_re, gs_im, gate_low, mid, out_gain_part, back = plain_call(
        partial(back_kernel, half, length),
        [wide] * 2
        + [((total, 2 * half), LOW)] * 2
        + [((8, 2 * half), F32), ((4, 8, half), F32)],
        8,
        scratch=[pltpu.VMEM((8, 2 * half), F32)],
        name="back_gates",
    )(grad_mid, st_re, st_im, proj, g_out, scale_all, d_re, d_im)
    back_all = tie(small_gather(lay, back, lay.wmasks, partial(w_slot, lay), W, 2), gate_away)
    grads, lower_part, angle_part = plain_call(
        partial(adjoint_kernel, half, length, n),
        [((total, 5 * half), LOW), ((8, half), F32), ((8, half), F32)],
        13,
        smem=1,
        scratch=[pltpu.VMEM((half // LANES, total, LANES), F32)] * 2 + [pltpu.VMEM((16, half), F32)],
        name="adjoints",
    )(ints, summ_all, back_all, gs_re, gs_im, d_re, d_im, be_re, be_im, proj, keep, par, gate_low)
    du_mix_low = jnp.dot(grads, w_mix, preferred_element_type=F32).astype(LOW)
    mix_gain_part = jnp.sum(
        du_mix_low.astype(F32) * (all32 * r_all), axis=0
    )

    t_hot = ((jnp.arange(2)[:, None] == zlo) & (jnp.arange(2)[None, :] == x)).astype(F32)
    out_gain_part = jnp.sum(out_gain_part, axis=0).reshape(2, 1, Y, 1, 2 * r_in)
    out_gain_part = (out_gain_part * t_hot[None, :, None, :, None]).reshape(n, r_in)

    def spread(vector):
        vector = jnp.sum(vector, axis=0).reshape(1, Y, 1, half // Y)
        return (vector * t_hot[:, None, :, None]).reshape(n, r_f)

    to_owner = jnp.concatenate(
        [
            mix_gain_part.reshape(n, r_in),
            ffn_gain_part.reshape(n, r_in),
            out_gain_part,
            spread(lower_part),
            spread(angle_part),
        ],
        axis=1,
    )
    to_owner = jnp.pad(to_owner, ((0, 0), (0, 1024 - to_owner.shape[1]))).reshape(n, 8, 128)

    grad_w_out = outer_rows(grad_all, mid).astype(LOW).reshape(2, 2, Y, 2, 2, r_in, 2 * half)
    grad_w_out = grad_w_out.transpose(0, 2, 4, 1, 3, 5, 6).reshape(W, 4 * r_in, 2 * half)
    gate_got = lay.send(tie(gate_away, back_all), lay.ZH)
    up_came = lay.send(tie(up_away, gate_away, back_all), lay.ybits[0])
    du_mix_low = tie(du_mix_low, gate_got)
    part_of = {
        "forget": outer_rows(grads[:, 4 * half :], normed).astype(LOW).reshape(split + (r_f, width)),
        "out": grad_w_out.reshape(split + (4 * r_in, 2 * half)),
        "up": up_kept,
        "down": down_kept,
        "gate": outer_rows(tie(gate_low, up_came), normed).astype(LOW).reshape(split + (r_in, width)),
        "in": outer_rows(grads[:, : 2 * half], normed).astype(LOW).reshape(split + (r_in, width)),
    }
    out_of = {name: (part.shape[-2:], F32) for name, part in part_of.items()}
    out_of["out"] = ((4, r_in, 2 * half), F32)
    parts = [part_of[name] for name in PARTS]
    scratch, copies, local_copies = [pltpu.VMEM((length, width), LOW)] * 4, 6 + 3 + n, 8
    for name, part in zip(PARTS, parts):
        for _, rows in row_cuts(name, part.shape[-2]):
            shape, skip = (rows, part.shape[-1]), first_stage(name)
            scratch.append(pltpu.VMEM(split[1 + skip :] + shape, LOW))
            for k in range(skip, len(split)):
                scratch.append(pltpu.VMEM(split[1 + k :] + shape, LOW))
            scratch.append(pltpu.VMEM(shape, F32))
            copies += len(split)
            local_copies += 3
    *sums, du_x, du_z, mixed_x, mixed_z, owned = net_call(
        partial(reduce_kernel, lay),
        lay,
        (
            *parts,
            up_came,
            down_away,
            du_mix_low.reshape(4, length, width),
            mixed_low.reshape(4, length, width),
            to_owner,
        ),
        [
            *[out_of[name] for name in PARTS],
            *[((length, width), LOW)] * 4,
            ((n, 8, 128), F32),
        ],
        copies,
        local_copies,
        3,
        "reduce",
        120,
        scratch,
    )
    ffn_gate_grad = join(gate_kept, gate_got)
    sum_of = dict(zip(PARTS, sums))
    out_proj_grad = (
        sum_of["out"].reshape(2, 2, r_in, 2, Y, 2 * r_in)
        .transpose(2, 3, 0, 4, 1, 5)
        .reshape(r_in, width)
    )
    owned = jnp.sum(owned, axis=0).reshape(-1)
    mixed_out = (residual + own_sum(mixed_low, (mixed_x, mixed_z))).astype(LOW)
    du_mix = own_sum(du_mix_low, (du_x, du_z))
    dg_mix = du_mix * g_mix
    tokens_grad = (
        grad_residual
        + r_tok * dg_mix
        - inputs * (r_tok * r_tok * r_tok) * jnp.mean(inputs * dg_mix, axis=-1, keepdims=True)
    ).astype(LOW)
    return (
        mixed_out,
        tokens_grad,
        sum_of["in"],
        sum_of["forget"],
        sum_of["gate"],
        out_proj_grad,
        ffn_gate_grad,
        sum_of["up"],
        sum_of["down"],
        owned[0:r_in],
        owned[2 * r_in : 3 * r_in],
        owned[r_in : 2 * r_in],
        owned[3 * r_in : 3 * r_in + r_f],
        owned[3 * r_in + r_f : 3 * r_in + 2 * r_f],
    )


def solution(mesh):
    rows, vector = P("dp", None), P("dp")
    in_specs = (rows, rows, P(), P()) + (rows,) * 7 + (vector,) * 5
    out_specs = (rows,) * 9 + (vector,) * 5
    return jax.shard_map(
        partial(local, mesh.shape["dp"]),
        mesh=mesh,
        in_specs=in_specs,
        out_specs=out_specs,
        check_vma=False,
    )
```

```python
from functools import partial

import jax
import jax.numpy as jnp
from jax import lax
from jax.experimental import pallas as pl
from jax.experimental.pallas import tpu as pltpu
from jax.sharding import PartitionSpec as P


EPS = 1e-06
LOW = jnp.bfloat16
F32 = jnp.float32
MESH = pl.DeviceIdType.MESH
ROWS = 32
LANES = 128


def contract(left_rows, right_rows):
    return lax.dot_general(
        left_rows, right_rows, (((1,), (1,)), ((), ())), preferred_element_type=F32
    )


def outer_rows(left_rows, right_rows):
    return lax.dot_general(
        left_rows, right_rows, (((0,), (0,)), ((), ())), preferred_element_type=F32
    )


def tie(value, *others):
    return lax.optimization_barrier((value,) + others)[0]


class Layout:
    def __init__(self, n):
        self.n = n
        self.Y = n // 16
        self.C, self.X, self.ZL, self.ZH = 1, 2, 4 * self.Y, 8 * self.Y
        self.ybits = []
        bit = 4
        while bit < self.ZL:
            self.ybits.append(bit)
            bit *= 2
        self.wbits = [self.ZH] + self.ybits + [self.C]
        self.rbits = [self.C] + self.ybits + [self.ZH]
        self.tmasks = [0, self.X, self.ZL, self.ZL | self.X]
        self.wmasks = [0]
        for bit in self.wbits:
            self.wmasks = self.wmasks + [m | bit for m in self.wmasks]
        self.bits = [1 << k for k in range(n.bit_length() - 1)]

    def rel_slot(self, mask):
        return ((mask % 2) * self.Y + (mask // 4) % self.Y) * 2 + mask // self.ZH

    def flip(self, device, mask):
        for bit in self.bits:
            if mask & bit:
                device = device + bit * (1 - 2 * ((device // bit) % 2))
        return device

    def parts(self, device):
        c = device % 2
        x = (device // self.X) % 2
        y = (device // 4) % self.Y
        zlo = (device // self.ZL) % 2
        zhi = device // self.ZH
        return zhi, zlo, y, x, c

    def send(self, value, mask):
        return lax.ppermute(value, "dp", [(i, i ^ mask) for i in range(self.n)])

    def gather_t(self, value):
        return [value] + [self.send(value, m) for m in self.tmasks[1:]]

    def scatter_t(self, blocks):
        got = [self.send(b, m) for b, m in zip(blocks[1:], self.tmasks[1:])]
        total = blocks[0].astype(F32)
        for g in got:
            total = total + g.astype(F32)
        return total

    def gather_w(self, value):
        pieces = [value]
        for bit in self.wbits:
            pieces = pieces + [self.send(v, bit) for v in pieces]
        return pieces


def gather_kernel(lay, masks, slot_of, in_ref, out_ref, send_sems, recv_sems):
    me = lax.axis_index("dp")
    peers = [lay.flip(me, m) for m in masks]
    barrier = pltpu.get_barrier_semaphore()
    for peer in peers:
        pl.semaphore_signal(barrier, inc=1, device_id=(peer,), device_id_type=MESH)
    pl.semaphore_wait(barrier, len(peers))
    slot = slot_of(me)
    copies = []
    for i, peer in enumerate(peers):
        copy = pltpu.make_async_remote_copy(
            src_ref=in_ref,
            dst_ref=out_ref.at[pl.ds(slot * in_ref.shape[0], in_ref.shape[0])],
            send_sem=send_sems.at[i],
            recv_sem=recv_sems.at[i],
            device_id=(peer,),
            device_id_type=MESH,
        )
        copy.start()
        copies.append(copy)
    out_ref[pl.ds(slot * in_ref.shape[0], in_ref.shape[0])] = in_ref[...]
    for copy in copies:
        copy.wait()


def small_gather(lay, value, masks, slot_of, slots, collective_id):
    masks = [m for m in masks if m]
    vmem = pl.BlockSpec(memory_space=pltpu.VMEM)
    return pl.pallas_call(
        partial(gather_kernel, lay, masks, slot_of),
        out_shape=jax.ShapeDtypeStruct((slots * value.shape[0],) + value.shape[1:], value.dtype),
        in_specs=[vmem],
        out_specs=vmem,
        scratch_shapes=[
            pltpu.SemaphoreType.DMA((len(masks),)),
            pltpu.SemaphoreType.DMA((len(masks),)),
        ],
        compiler_params=pltpu.CompilerParams(collective_id=collective_id, has_side_effects=True),
        cost_estimate=estimate(10),
    )(value)


class Net:
    def __init__(self, lay, peers, send_sems, recv_sems, local_sems, rooms=()):
        self.lay, self.send_sems, self.recv_sems, self.local_sems = lay, send_sems, recv_sems, local_sems
        self.rooms, self.moving = list(rooms), []
        self.me = lax.axis_index("dp")
        self.used, self.used_local, self.open, self.local = 0, 0, [], []
        barrier = pltpu.get_barrier_semaphore()
        for mask in peers:
            pl.semaphore_signal(
                barrier, inc=1, device_id=(lay.flip(self.me, mask),), device_id_type=MESH
            )
        pl.semaphore_wait(barrier, len(peers))

    def put(self, src, dst, mask):
        copy = pltpu.make_async_remote_copy(
            src_ref=src,
            dst_ref=dst,
            send_sem=self.send_sems.at[self.used],
            recv_sem=self.recv_sems.at[self.used],
            device_id=(self.lay.flip(self.me, mask),),
            device_id_type=MESH,
        )
        copy.start()
        self.used += 1
        self.open.append(copy)
        return copy

    def load(self, src, dst):
        copy = pltpu.make_async_copy(src, dst, self.local_sems.at[self.used_local])
        copy.start()
        self.used_local += 1
        return copy

    def keep(self, src, dst):
        self.local.append(self.load(src, dst))

    def move(self, src, dst):
        room = self.rooms.pop(0)
        self.moving.append((self.load(src, room), room, dst))

    def settle(self):
        for copy, room, dst in self.moving:
            copy.wait()
            self.keep(room, dst)
        self.moving = []

    def finish(self):
        for copy in self.open:
            copy.wait_send()
        for copy in self.local:
            copy.wait()


class WeightGather:
    def __init__(self, net, own, place, early=None):
        self.net, self.own, self.place, self.early = net, own, place, early or {}
        self.bits = net.lay.wbits
        self.pending = {}

    def start(self):
        me = self.net.me
        for bit in self.bits:
            if bit not in self.early:
                self.pending[bit] = self.net.put(self.own, self.place(me, bit), bit)
        self.net.move(self.own, self.place(me, 0))
        for bit, block in self.early.items():
            self.pass_on(bit, block)
            self.net.move(block, self.place(self.net.lay.flip(me, bit), bit))

    def masks(self):
        out = [0]
        for bit in self.bits[:-1]:
            out = out + [m | bit for m in out]
        out = sorted(out[1:], key=lambda m: (bin(m).count("1"), -m))
        return [m for m in out if m not in self.early]

    def pass_on(self, mask, block):
        last = max(i for i, bit in enumerate(self.bits) if mask & bit)
        source = self.net.lay.flip(self.net.me, mask)
        for bit in self.bits[last + 1 :]:
            self.pending[mask | bit] = self.net.put(block, self.place(source, mask | bit), bit)

    def forward(self, mask):
        self.pending[mask].wait_recv()
        self.pass_on(mask, self.place(self.net.lay.flip(self.net.me, mask), mask))

    def end(self):
        for mask, copy in self.pending.items():
            if mask & self.bits[-1]:
                copy.wait_recv()


def token_start(net, own, out):
    lay = net.lay
    first = [net.put(own, out.at[1], lay.X), net.put(own, out.at[2], lay.ZL)]
    net.move(own, out.at[0])
    return first


def token_finish(net, first, out):
    lay, half = net.lay, out.shape[1] // 2
    top, low = pl.ds(0, half), pl.ds(half, half)
    arrived(first[:1])
    copies = [net.put(out.at[1, top], out.at[3, top], lay.ZL)]
    arrived(first[1:])
    return copies + [net.put(out.at[2, low], out.at[3, low], lay.X)]


def token_scatter(net, blocks, out):
    return [net.put(blocks.at[j], out.at[j - 1], m) for j, m in enumerate(net.lay.tmasks) if j]


def arrived(copies):
    for copy in copies:
        copy.wait_recv()


SCALE = 10_000_000


def estimate(micros):
    return pl.CostEstimate(flops=micros * SCALE, bytes_accessed=0, transcendentals=0)


def net_call(body, lay, values, outs, copies, local, collective_id, name, micros, scratch=()):
    hbm = pl.BlockSpec(memory_space=pl.ANY)
    return pl.pallas_call(
        body,
        out_shape=tuple(jax.ShapeDtypeStruct(s, d) for s, d in outs),
        in_specs=[hbm] * len(values),
        out_specs=tuple(hbm for _ in outs),
        scratch_shapes=[
            *scratch,
            pltpu.SemaphoreType.DMA((copies,)),
            pltpu.SemaphoreType.DMA((copies,)),
            pltpu.SemaphoreType.DMA((local,)),
        ],
        compiler_params=pltpu.CompilerParams(
            collective_id=collective_id,
            has_side_effects=True,
            vmem_limit_bytes=60 << 20,
        ),
        cost_estimate=estimate(micros),
        name=name,
    )(*values)


def w_slot(lay, device):
    zhi, _, y, _, c = lay.parts(device)
    return (zhi * lay.Y + y) * 2 + c


def f_slot(lay, device):
    zhi, _, y, _, c = lay.parts(device)
    return (y * 2 + c) * 2 + zhi


def t_slot(lay, device):
    _, zlo, _, x, _ = lay.parts(device)
    return zlo * 2 + x


class Turn:
    def __init__(self, net, target, src, dst):
        self.remote = target != net.me
        self.away = pltpu.make_async_remote_copy(
            src_ref=src,
            dst_ref=dst,
            send_sem=net.send_sems.at[net.used],
            recv_sem=net.recv_sems.at[net.used],
            device_id=(target,),
            device_id_type=MESH,
        )
        self.here = pltpu.make_async_copy(src, dst, net.local_sems.at[net.used_local])
        net.used += 1
        net.used_local += 1

        @pl.when(self.remote)
        def _():
            self.away.start()

        @pl.when(jnp.logical_not(self.remote))
        def _():
            self.here.start()

    def wait(self):
        @pl.when(self.remote)
        def _():
            self.away.wait()

        @pl.when(jnp.logical_not(self.remote))
        def _():
            self.here.wait()


def forget_to(lay, device):
    return (device % 2) * (lay.n // 2) + device // 2


def forget_from(lay, device):
    return 2 * (device % (lay.n // 2)) + device // (lay.n // 2)


def start_kernel(
    lay, units, tok, w_in, w_gate, w_forget, w_out, f_gate, pack,
    tok_all, mix_all, forget_own, out_own, out_all, f_gate_z, every, *rest,
):
    n, W = lay.n, lay.n // 4
    *rooms, send_sems, recv_sems, local_sems = rest
    net = Net(lay, list(range(1, n)), send_sems, recv_sems, local_sems, rooms)
    me = net.me

    def region(base):
        return lambda d, m: mix_all.at[pl.ds(base + w_slot(lay, d) * units, units)]

    g_in = WeightGather(net, w_in, region(0))
    g_gate = WeightGather(net, w_gate, region(W * units))
    g_forget = WeightGather(
        net, forget_own, lambda d, m: mix_all.at[pl.ds(2 * W * units + f_slot(lay, d), 1)]
    )
    g_out = WeightGather(net, out_own, lambda d, m: out_all.at[w_slot(lay, d)])
    turn = Turn(net, forget_to(lay, me), w_forget, forget_own)
    g_in.start()
    g_gate.start()
    mine = t_slot(lay, me)
    own = net.load(w_out.at[mine], out_own.at[mine])
    out_in = [
        net.put(w_out.at[t_slot(lay, lay.flip(me, m))], out_own.at[mine], m) for m in lay.tmasks[1:]
    ]
    first = token_start(net, tok, tok_all)
    all_in = [net.put(pack, every.at[me], m) for m in range(1, n)]
    net.keep(pack, every.at[me])
    turn.wait()
    g_forget.start()
    own.wait()
    arrived(out_in)
    g_out.start()
    gate_in = net.put(f_gate.at[pl.ds(0, f_gate_z.shape[0])], f_gate_z, lay.ZH)
    net.settle()
    for mask in g_in.masks():
        g_in.forward(mask)
        g_gate.forward(mask)
    rest = token_finish(net, first, tok_all)
    for mask in g_forget.masks():
        g_forget.forward(mask)
        g_out.forward(mask)
    for gather in (g_in, g_gate, g_forget, g_out):
        gather.end()
    arrived(rest + [gate_in])
    arrived(all_in)
    net.finish()


def group_peers(lay):
    return lay.tmasks[1:] + lay.wbits


def rel_gather(net, own, early, out, cut):
    rows = pl.ds(*cut)
    early = {bit: block if block.shape[0] == cut[1] else block.at[rows] for bit, block in early.items()}
    return WeightGather(net, own.at[rows], lambda d, m: out.at[net.lay.rel_slot(m), rows], early)


def branch_kernel(lay, cuts, blocks, small, gate, up, down, *rest):
    pieces = len(cuts)
    gate_z, rest = rest[:pieces], rest[pieces:]
    (got_x, got_z, got_small, gate_all, down_y, down_z), rest = rest[:6], rest[6:]
    up_z, rest = rest[: pieces - 1], rest[pieces - 1 :]
    token_rooms, rest = rest[:2], rest[2:]
    *rooms, send_sems, recv_sems, local_sems = rest
    net = Net(lay, group_peers(lay), send_sems, recv_sems, local_sems, rooms)
    gathers = [rel_gather(net, gate, {lay.ZH: z}, gate_all, cut) for cut, z in zip(cuts, gate_z)]
    for gather in gathers:
        gather.start()
    tokens = TokenReduce(net, blocks, got_x, got_z, *token_rooms)
    waits = [net.put(up.at[pl.ds(*cut)], z, lay.ZH) for cut, z in zip(cuts[1:], up_z)]
    waits += token_scatter(net, small, got_small)
    net.settle()
    arrived(waits[: pieces - 1])
    waits = waits[pieces - 1 :]
    waits.append(net.put(down.at[pl.ds(*cuts[0])], down_z, lay.ZH))
    for gather in gathers:
        for mask in gather.masks():
            gather.forward(mask)
    waits.append(net.put(down, down_y, lay.ybits[0]))
    tokens.pass_on()
    for gather in gathers:
        gather.end()
    tokens.end()
    arrived(waits)
    net.finish()


def ffn_kernel(lay, cuts, own, up, down, down_y, down_z, *rest):
    pieces = len(cuts)
    up_z, rest = rest[:pieces], rest[pieces:]
    cot_blocks, (own_all, up_all, down_all, cot_all), rest = rest[:4], rest[4:8], rest[8:]
    *rooms, send_sems, recv_sems, local_sems = rest
    net = Net(lay, group_peers(lay), send_sems, recv_sems, local_sems, rooms)
    gathers = []
    for i, cut in enumerate(cuts):
        early = {lay.ybits[0]: down_y}
        if i == 0:
            early[lay.ZH] = down_z
        gathers.append(rel_gather(net, down, early, down_all, cut))
    for cut, z in zip(cuts, up_z):
        gathers.append(rel_gather(net, up, {lay.ZH: z}, up_all, cut))
    gathers[pieces - 1].start()
    first = token_start(net, own, own_all)
    for i, gather in enumerate(gathers):
        if i != pieces - 1:
            gather.start()
    for j, block in enumerate(cot_blocks):
        net.move(block, cot_all.at[j])
    net.settle()
    rest = token_finish(net, first, own_all)
    for gather in gathers[pieces:] + gathers[:pieces]:
        for mask in gather.masks():
            gather.forward(mask)
    for gather in gathers:
        gather.end()
    arrived(rest)
    net.finish()


def add_rows(out, left, right):
    rows = left.shape[0]
    tile = 16 if rows % 16 == 0 else rows

    def body(i, _):
        at = pl.ds(pl.multiple_of(i * tile, tile), tile)
        out[at, :] = (left[at, :].astype(F32) + right[at, :].astype(F32)).astype(out.dtype)
        return 0

    lax.fori_loop(0, rows // tile, body, 0)


class WeightReduce:
    def __init__(self, net, part, rows, dims, local, stages, total, relative, leaves=None, came=None):
        self.net, self.part, self.rows, self.relative = net, part, rows, relative
        self.local, self.stages, self.total = local, stages, total
        self.leaves, self.came = leaves, came
        self.first = 0 if leaves is None and came is None else 1
        self.bits = net.lay.rbits[self.first :]
        self.dims = [[d for d in dims if d in self.bits]]
        for bit in self.bits:
            self.dims.append([d for d in self.dims[-1] if d != bit])
        self.copy, self.waited = None, -1

    def side(self, k):
        return 0 if self.relative else (self.net.me // self.bits[k]) % 2

    def cut(self, k, away):
        index = [slice(None)] * len(self.dims[k])
        index[self.dims[k].index(self.bits[k])] = 1 - self.side(k) if away else self.side(k)
        if k:
            return self.stages[k - 1].at[tuple(index)]
        return self.part.at[tuple(index) + self.rows]

    def start(self):
        if self.first == 0:
            self.copy = self.net.put(self.cut(0, True), self.stages[0], self.bits[0])
            self.loaded = self.net.load(self.cut(0, False), self.local)
            return
        index = (slice(None),) * len(self.dims[1]) + self.rows
        self.loaded = self.net.load(self.part.at[index] if self.rows else self.part, self.local)
        if self.came is None:
            block = self.leaves.at[index] if self.rows else self.leaves
            self.copy = self.net.put(block, self.stages[0], self.bits[0])
        else:
            block = self.came.at[index] if self.rows else self.came
            self.copy = self.net.load(block, self.stages[0])

    def wait(self, k):
        if self.waited < k:
            if k == 0 and self.came is not None:
                self.copy.wait()
            else:
                self.copy.wait_recv()
            self.waited = k

    def add(self, k, away):
        if k == 0 and away:
            self.loaded.wait()
        stage = self.stages[k]
        old = self.cut(k, False) if k else self.local
        if k + 1 == len(self.bits):
            if away:
                add_rows(self.total, stage, old)
            return
        dims = self.dims[k + 1]
        place = dims.index(self.bits[k + 1])
        side = 1 - self.side(k + 1) if away else self.side(k + 1)
        for number in range(1 << (len(dims) - 1)):
            index = [(number >> j) & 1 for j in range(len(dims) - 1)]
            index = tuple(index[:place] + [side] + index[place:])
            add_rows(stage.at[index], stage.at[index], old.at[index])

    def send(self, k):
        self.copy = self.net.put(self.cut(k, True), self.stages[k], self.bits[k])


def grad_kernel(lay, own, small, gate, up, down, own_all, small_all, *rest):
    outs, (room, small_room, *scratch), (send_sems, recv_sems, local_sems) = rest[:6], rest[6:-3], rest[-3:]
    net = Net(lay, lay.tmasks[1:] + [lay.C], send_sems, recv_sems, local_sems, [room, small_room])
    first = token_start(net, own, own_all)
    waits = [net.put(small, small_all.at[j], m) for j, m in enumerate(lay.tmasks) if j]
    net.move(small, small_all.at[0])
    dims = part_dims(lay, "up")
    jobs = []
    for j, part in enumerate((gate, up, down)):
        local, stage = scratch[2 * j : 2 * j + 2]
        jobs.append(WeightReduce(net, part, (), dims, local, [stage], None, True))
        jobs[-1].start()
    net.settle()
    for j, job in enumerate(jobs):
        job.wait(0)
        job.add(0, True)
        net.keep(job.cut(1, True), outs[2 * j + 1])
        job.add(0, False)
        net.keep(job.cut(1, False), outs[2 * j])
        if j == 0:
            waits += token_finish(net, first, own_all)
    arrived(waits)
    net.finish()


def row_cuts(name, rows):
    if name not in ("up", "down") or rows % 16 or rows < 128:
        return [(0, rows)]
    first = -(-rows // 32) * 16
    return [(0, first), (first, rows - first)]


PARTS = ("up", "forget", "out", "down", "gate", "in")


class TokenReduce:
    def __init__(self, net, blocks, got_x, got_z, room, other):
        lay = net.lay
        self.net, self.room, self.other, self.got_z = net, room, other, got_z
        self.first = [net.put(blocks.at[3], other, lay.X), net.put(blocks.at[1], got_x, lay.X)]
        self.loaded = net.load(blocks.at[2], room)

    def pass_on(self):
        self.first[0].wait_recv()
        self.loaded.wait()
        add_rows(self.room, self.room, self.other)
        self.last = self.net.put(self.room, self.got_z, self.net.lay.ZL)

    def end(self):
        arrived([self.first[1], self.last])


def first_stage(name):
    return 1 if name in ("up", "down") else 0


def part_dims(lay, name):
    y_bits = list(reversed(lay.ybits))
    if name == "forget":
        return y_bits + [lay.C, lay.ZH]
    if name in ("up", "down"):
        return [lay.C] + y_bits + [lay.ZH]
    return [lay.ZH] + y_bits + [lay.C]


LAG = 2


def reduce_kernel(lay, *refs):
    count = len(PARTS)
    parts, refs = refs[:count], refs[count:]
    (up_came, down_leaves, du, mixed, vectors), refs = refs[:5], refs[5:]
    outs, refs = refs[:count], refs[count:]
    (du_x, du_z, mixed_x, mixed_z, all_vectors), refs = refs[:5], refs[5:]
    token_rooms, refs = refs[:4], refs[4:]
    scratch, (send_sems, recv_sems, local_sems) = list(refs[:-3]), refs[-3:]
    net = Net(lay, list(range(1, lay.n)), send_sems, recv_sems, local_sems)
    me = net.me
    jobs, places, turns, waits = [], [], [], []
    for name, part, out in zip(PARTS, parts, outs):
        for first, rows in row_cuts(name, part.shape[-2]):
            local = scratch.pop(0)
            stages = [scratch.pop(0) for _ in lay.rbits[first_stage(name) :]]
            whole = rows == part.shape[-2]
            at = () if whole else (pl.ds(first, rows),)
            relative = name in ("up", "down")
            dims = part_dims(lay, name)
            jobs.append(
                WeightReduce(
                    net,
                    part,
                    at,
                    dims,
                    local,
                    stages,
                    scratch.pop(0),
                    relative,
                    down_leaves if name == "down" else None,
                    up_came if name == "up" else None,
                )
            )
            places.append((name, out if whole else out.at[pl.ds(first, rows)]))
    flows = [[] for _ in lay.rbits]
    late = []
    for job, (name, _) in zip(jobs, places):
        if name in ("gate", "in"):
            late.append(job)
        else:
            job.start()
            if name == "down":
                flows[1].append(job)
    du_sum = TokenReduce(net, du, du_x, du_z, *token_rooms[:2])

    def finish(i):
        total = jobs[i].total
        name, out = places[i]
        if name == "forget":
            turns.append(Turn(net, forget_from(lay, me), total, out))
        elif name == "out":
            rows = total.shape[0] // 4
            mine = t_slot(lay, me)

            def cut(slot):
                return total.at[pl.ds(pl.multiple_of(slot * rows, rows), rows)]

            net.keep(cut(mine), out.at[mine])
            for m in lay.tmasks[1:]:
                waits.append(net.put(cut(t_slot(lay, lay.flip(me, m))), out.at[mine], m))
        else:
            net.keep(total, out)

    depth = len(lay.rbits)
    for tick in range(len(jobs) + depth - 1):
        for k in range(depth):
            i = tick - k
            if not 0 <= i < len(jobs) or k + jobs[i].first >= depth:
                continue
            job = jobs[i]
            job.wait(k)
            job.add(k, True)
            flow = k + 1 + job.first
            if flow == depth:
                finish(i)
                continue
            if len(flows[flow]) >= LAG:
                behind = flows[flow][-LAG]
                behind.wait(flow - behind.first)
            job.send(k + 1)
            flows[flow].append(job)
            job.add(k, False)
        if tick == 0:
            for job in late:
                job.start()
        if tick == 1:
            waits += [
                net.put(vectors.at[lay.flip(me, m)], all_vectors.at[me], m) for m in range(1, lay.n)
            ]
            net.keep(vectors.at[me], all_vectors.at[me])
            mixed_sum = TokenReduce(net, mixed, mixed_x, mixed_z, *token_rooms[2:])
        if tick == 3:
            du_sum.pass_on()
        if tick == 5:
            mixed_sum.pass_on()
    du_sum.end()
    mixed_sum.end()
    arrived(waits)
    for turn in turns:
        turn.wait()
    net.finish()


def sig(v):
    return 1.0 / (1.0 + jnp.exp(-v))


def lanes(base, h):
    return slice(base + h * LANES, base + (h + 1) * LANES)


def fold_rows(v):
    return jnp.sum(v.reshape(v.shape[0] // 8, 8, v.shape[1]), axis=0)


def forward_kernel(half, length, proj, keep, par, d_re, d_im, v_re, v_im, summ):
    total = d_re.shape[1]
    blocks = total // length
    tiles = half // LANES

    def terms(i, _):
        rows = pl.ds(pl.multiple_of(i * ROWS, ROWS), ROWS)
        kept = keep[rows, :]
        for h in range(tiles):
            at = slice(h * LANES, (h + 1) * LANES)
            lower = par[0:1, at]
            magnitude = lower + (1.0 - lower) * sig(proj[rows, lanes(4 * half, h)])
            rest = 1.0 - magnitude
            d_re[h, rows, :] = kept * magnitude * par[1:2, at]
            d_im[h, rows, :] = kept * magnitude * par[2:3, at]
            a = proj[rows, lanes(0, h)]
            b = proj[rows, lanes(half, h)]
            v_re[h, rows, :] = a * sig(a) * rest
            v_im[h, rows, :] = b * sig(b) * rest
        return 0

    lax.fori_loop(0, total // ROWS, terms, 0)

    def step(t, carry):
        rows = pl.ds(t, blocks, stride=length)
        out = []
        for h in range(tiles):
            p_re, p_im, s_re, s_im = carry[4 * h : 4 * h + 4]
            dr, di = d_re[h, rows, :], d_im[h, rows, :]
            out += [
                dr * p_re - di * p_im,
                dr * p_im + di * p_re,
                dr * s_re - di * s_im + v_re[h, rows, :],
                dr * s_im + di * s_re + v_im[h, rows, :],
            ]
        return tuple(out)

    zero = jnp.zeros((blocks, LANES), F32)
    ends = lax.fori_loop(0, length, step, (zero + 1.0, zero, zero, zero) * tiles, unroll=4)
    for j in range(blocks):
        summ[j, 4:8, :] = jnp.zeros((4, half), F32)
        for h in range(tiles):
            for k in range(4):
                summ[j, k : k + 1, lanes(0, h)] = ends[4 * h + k][j : j + 1, :]


def chain_blocks(half, n, blocks, ints, summ, back):
    tiles = half // LANES

    def chain(i, carry):
        p = i if back is None else n - 1 - i
        tile = summ[ints[p]]
        shift = tile[2:4, :] if back is None else back[ints[p]]
        out = []
        for h in range(tiles):
            at = slice(h * LANES, (h + 1) * LANES)
            old = carry[h * (2 + 2 * blocks) : (h + 1) * (2 + 2 * blocks)]
            c_re, c_im = old[0], old[1]
            a_re = tile[0:1, at]
            a_im = tile[1:2, at] if back is None else -tile[1:2, at]
            out.append(a_re * c_re - a_im * c_im + shift[0:1, at])
            out.append(a_re * c_im + a_im * c_re + shift[1:2, at])
            for j in range(blocks):
                here = ints[n + j] == p
                out.append(jnp.where(here, c_re, old[2 + 2 * j]))
                out.append(jnp.where(here, c_im, old[3 + 2 * j]))
        return tuple(out)

    first = summ[0]
    zero = first[0:1, 0:LANES] - first[0:1, 0:LANES]
    res = lax.fori_loop(0, n, chain, (zero,) * (tiles * (2 + 2 * blocks)))
    entry = []
    for h in range(tiles):
        old = res[h * (2 + 2 * blocks) : (h + 1) * (2 + 2 * blocks)]
        entry.append(jnp.concatenate([old[2 + 2 * j] for j in range(blocks)], axis=0))
        entry.append(jnp.concatenate([old[3 + 2 * j] for j in range(blocks)], axis=0))
    return tuple(entry)


def state_kernel(
    half, length, n, ints, summ, d_re, d_im, v_re, v_im, proj, gain,
    st_re, st_im, be_re, be_im, unit, squares,
):
    total = d_re.shape[1]
    blocks = total // length
    tiles = half // LANES

    def step(t, carry):
        rows = pl.ds(t, blocks, stride=length)
        out = []
        for h in range(tiles):
            s_re, s_im = carry[2 * h], carry[2 * h + 1]
            be_re[h, rows, :] = s_re
            be_im[h, rows, :] = s_im
            dr, di = d_re[h, rows, :], d_im[h, rows, :]
            n_re = dr * s_re - di * s_im + v_re[h, rows, :]
            n_im = dr * s_im + di * s_re + v_im[h, rows, :]
            st_re[h, rows, :] = n_re
            st_im[h, rows, :] = n_im
            out += [n_re, n_im]
        return tuple(out)

    entry = chain_blocks(half, n, blocks, ints, summ, None)
    lax.fori_loop(0, length, step, entry, unroll=4)

    def finish(i, _):
        rows = pl.ds(pl.multiple_of(i * ROWS, ROWS), ROWS)
        square = jnp.zeros((ROWS, 1), F32)
        for h in range(tiles):
            for part, st in ((0, st_re), (1, st_im)):
                v = st[h, rows, :]
                g = proj[rows, lanes((2 + part) * half, h)]
                at = lanes(part * half, h)
                unit[rows, at] = (v * gain[0:1, at] * (g * sig(g))).astype(LOW)
                square = square + jnp.sum(v * v, axis=1, keepdims=True)
        squares[rows, :] = jnp.broadcast_to(square, (ROWS, LANES))
        return 0

    lax.fori_loop(0, total // ROWS, finish, 0)


def back_kernel(
    half, length, grad_mid, st_re, st_im, proj, gain, scale, d_re, d_im,
    gs_re, gs_im, gate_low, mid, gain_grad, summ, acc,
):
    total = d_re.shape[1]
    blocks = total // length
    tiles = half // LANES
    acc[...] = jnp.zeros_like(acc)

    def terms(i, _):
        rows = pl.ds(pl.multiple_of(i * ROWS, ROWS), ROWS)
        r = scale[rows, 0:1]
        q = scale[rows, 1:2]
        for h in range(tiles):
            for part, st, gs in ((0, st_re, gs_re), (1, st_im, gs_im)):
                at = lanes(part * half, h)
                g = proj[rows, lanes((2 + part) * half, h)]
                v = st[h, rows, :]
                gv = gain[0:1, at]
                dm = grad_mid[rows, at]
                sg = sig(g)
                silu = g * sg
                du = dm * silu
                normed = v * r
                scaled = normed * gv
                mid[rows, at] = (scaled * silu).astype(LOW)
                gate_low[rows, at] = (dm * scaled * (sg * (1.0 + g * (1.0 - sg)))).astype(LOW)
                gs[h, rows, :] = du * gv * r - v * q
                acc[:, at] = acc[:, at] + fold_rows(du * normed)
        return 0

    lax.fori_loop(0, total // ROWS, terms, 0)
    gain_grad[...] = acc[...]

    def step(i, carry):
        rows = pl.ds(length - 1 - i, blocks, stride=length)
        out = []
        for h in range(tiles):
            a_re = gs_re[h, rows, :] + carry[2 * h]
            a_im = gs_im[h, rows, :] + carry[2 * h + 1]
            dr, di = d_re[h, rows, :], d_im[h, rows, :]
            out += [dr * a_re + di * a_im, dr * a_im - di * a_re]
        return tuple(out)

    zero = jnp.zeros((blocks, LANES), F32)
    ends = lax.fori_loop(0, length, step, (zero, zero) * tiles, unroll=4)
    for j in range(blocks):
        summ[j, 2:8, :] = jnp.zeros((6, half), F32)
        for h in range(tiles):
            for k in range(2):
                summ[j, k : k + 1, lanes(0, h)] = ends[2 * h + k][j : j + 1, :]


def adjoint_kernel(
    half, length, n, ints, summ, back, gs_re, gs_im, d_re, d_im, be_re, be_im, proj, keep, par, gate_low,
    grads, lower_grad, angle_grad, ad_re, ad_im, acc,
):
    total = d_re.shape[1]
    blocks = total // length
    tiles = half // LANES

    def step(i, carry):
        rows = pl.ds(length - 1 - i, blocks, stride=length)
        out = []
        for h in range(tiles):
            a_re = gs_re[h, rows, :] + carry[2 * h]
            a_im = gs_im[h, rows, :] + carry[2 * h + 1]
            ad_re[h, rows, :] = a_re
            ad_im[h, rows, :] = a_im
            dr, di = d_re[h, rows, :], d_im[h, rows, :]
            out += [dr * a_re + di * a_im, dr * a_im - di * a_re]
        return tuple(out)

    entry = chain_blocks(half, n, blocks, ints, summ, back)
    lax.fori_loop(0, length, step, entry, unroll=4)
    acc[...] = jnp.zeros_like(acc)

    def terms(i, _):
        rows = pl.ds(pl.multiple_of(i * ROWS, ROWS), ROWS)
        kept = keep[rows, :]
        for h in range(tiles):
            at = slice(h * LANES, (h + 1) * LANES)
            lower, cos, sin = par[0:1, at], par[1:2, at], par[2:3, at]
            sf = sig(proj[rows, lanes(4 * half, h)])
            magnitude = lower + (1.0 - lower) * sf
            rest = 1.0 - magnitude
            a = proj[rows, lanes(0, h)]
            b = proj[rows, lanes(half, h)]
            sa, sb = sig(a), sig(b)
            ar, ai = ad_re[h, rows, :], ad_im[h, rows, :]
            br, bi = be_re[h, rows, :], be_im[h, rows, :]
            g_re = ar * br + ai * bi
            g_im = ai * br - ar * bi
            g_mag = kept * (g_re * cos + g_im * sin) - (ar * (a * sa) + ai * (b * sb))
            acc[0:8, at] = acc[0:8, at] + fold_rows(g_mag * (1.0 - sf))
            acc[8:16, at] = acc[8:16, at] + fold_rows(kept * magnitude * (g_im * cos - g_re * sin))
            grads[rows, lanes(0, h)] = (ar * rest * (sa * (1.0 + a * (1.0 - sa)))).astype(LOW)
            grads[rows, lanes(half, h)] = (ai * rest * (sb * (1.0 + b * (1.0 - sb)))).astype(LOW)
            grads[rows, lanes(4 * half, h)] = (g_mag * (1.0 - lower) * sf * (1.0 - sf)).astype(LOW)
        grads[rows, 2 * half : 4 * half] = gate_low[rows, :]
        return 0

    lax.fori_loop(0, total // ROWS, terms, 0)
    lower_grad[...] = acc[0:8, :]
    angle_grad[...] = acc[8:16, :]


VMEM = pl.BlockSpec(memory_space=pltpu.VMEM)
SMEM = pl.BlockSpec(memory_space=pltpu.SMEM)


def plain_call(body, outs, n_in, smem=0, scratch=(), name=None):
    return pl.pallas_call(
        body,
        out_shape=tuple(jax.ShapeDtypeStruct(s, d) for s, d in outs),
        in_specs=[SMEM] * smem + [VMEM] * (n_in - smem),
        out_specs=tuple(VMEM for _ in outs),
        scratch_shapes=list(scratch),
        compiler_params=pltpu.CompilerParams(vmem_limit_bytes=48 << 20),
        cost_estimate=estimate(7),
        name=name,
    )


def local(
    n,
    tokens,
    cotangent,
    seq_lengths,
    block_deal,
    in_proj,
    forget_proj,
    gate_proj,
    out_proj,
    ffn_gate,
    ffn_up,
    ffn_down,
    gain_mix,
    gain_out,
    gain_ffn,
    lower_bound,
    rotation,
):
    lay = Layout(n)
    Y = lay.Y
    W = n // 4
    me = lax.axis_index("dp")
    zhi, zlo, y, x, c = lay.parts(me)
    mine_t = zlo * 2 + x
    length, width = tokens.shape
    half = width // 8
    total = 4 * length
    r_in, r_f = in_proj.shape[0], forget_proj.shape[0]

    indices = jnp.arange(n, dtype=jnp.int32)
    order = jnp.sum(jnp.where(block_deal[None, :] == indices[:, None], indices[None, :], 0), axis=1)
    t_devices = jnp.stack([lay.flip(me, m) for m in lay.tmasks])
    t_places = jnp.sum(
        jnp.where(t_devices[:, None] == indices[None, :], block_deal[None, :], 0), axis=1
    )
    o_parts = lay.parts(order)
    t_rel = ((o_parts[1] + zlo) % 2) * 2 + (o_parts[3] + x) % 2
    ints = jnp.concatenate([w_slot(lay, order) * 4 + t_rel, t_places]).astype(jnp.int32)
    offsets = jnp.cumsum(seq_lengths) - seq_lengths
    positions = (
        t_places[:, None] * length + jnp.arange(length, dtype=jnp.int32)[None, :]
    ).reshape(-1)
    starts = jnp.any(positions[:, None] == offsets[None, :], axis=1)
    keep = jnp.where(starts, 0.0, 1.0).astype(F32)[:, None]

    packed = jnp.concatenate([gain_mix, gain_ffn, gain_out, lower_bound, rotation])
    pack_rows = -(-packed.shape[0] // 128)
    packed = jnp.pad(packed, (0, 8 * 128 - packed.shape[0])).reshape(8, 128)
    out_cols = out_proj.astype(LOW).reshape(r_in, 2, 2, Y, 2, 2 * r_in)
    out_cols = out_cols.transpose(2, 4, 0, 1, 3, 5).reshape(4, r_in, 2 * half)
    units = r_in // r_f
    r_ffn = ffn_gate.shape[0]
    cuts = row_cuts("up", r_ffn)
    f_gate = ffn_gate.astype(LOW)
    tok_all, w_mix, _, _, w_out, gate_za, every = net_call(
        partial(start_kernel, lay, units),
        lay,
        (
            tokens,
            in_proj.astype(LOW).reshape(units, r_f, width),
            gate_proj.astype(LOW).reshape(units, r_f, width),
            forget_proj.astype(LOW).reshape(1, r_f, width),
            out_cols,
            f_gate,
            packed,
        ),
        [
            ((4, length, width), LOW),
            ((W * (2 * units + 1), r_f, width), LOW),
            ((1, r_f, width), LOW),
            ((4, r_in, 2 * half), LOW),
            ((W, 4, r_in, 2 * half), LOW),
            ((cuts[0][1], width), LOW),
            ((n, 8, 128), F32),
        ],
        4 * (W - 1) + 9 + n - 1,
        24,
        0,
        "start",
        60,
        [
            pltpu.VMEM((units, r_f, width), LOW),
            pltpu.VMEM((units, r_f, width), LOW),
            pltpu.VMEM((length, width), LOW),
            pltpu.VMEM((1, r_f, width), LOW),
            pltpu.VMEM((4, r_in, 2 * half), LOW),
        ],
    )
    f_up, f_down = ffn_up.astype(LOW), ffn_down.astype(LOW)
    gate_z = [gate_za]
    if len(cuts) > 1:
        gate_z.append(lay.send(tie(ffn_gate[cuts[1][0] :].astype(LOW), tok_all), lay.ZH))
    tok_all = tok_all.reshape(total, width)
    w_mix = w_mix.reshape(5 * half, width)
    w_out = w_out.reshape(2, Y, 2, 2, 2, r_in, 2 * half).transpose(0, 3, 1, 4, 2, 5, 6)
    w_out = w_out.reshape(width, 2 * half)
    every = every[:, :pack_rows, :].reshape(n, pack_rows * 128)
    g_mix = every[:, 0:r_in].reshape(1, width)
    g_ffn = every[:, r_in : 2 * r_in].reshape(1, width)
    g_out = every[:, 2 * r_in : 3 * r_in].reshape(2, 2, Y, 2, 2 * r_in)
    g_out = lax.dynamic_index_in_dim(g_out, zlo, 1, keepdims=False)
    g_out = lax.dynamic_index_in_dim(g_out, x, 2, keepdims=False).reshape(1, 2 * half)

    def channels(vector):
        vector = vector.reshape(2, Y, 2, half // Y)
        vector = lax.dynamic_index_in_dim(vector, zlo, 0, keepdims=False)
        return lax.dynamic_index_in_dim(vector, x, 1, keepdims=False).reshape(1, half)

    lower = channels(every[:, 3 * r_in : 3 * r_in + r_f])
    angle = channels(every[:, 3 * r_in + r_f : 3 * r_in + 2 * r_f])
    par = jnp.concatenate(
        [lower, jnp.cos(angle), jnp.sin(angle), jnp.zeros((5, half), F32)], axis=0
    )

    inputs = tokens.astype(F32)
    r_tok = lax.rsqrt(jnp.mean(inputs * inputs, axis=-1, keepdims=True) + EPS)
    all32 = tok_all.astype(F32)
    r_all = lax.rsqrt(jnp.mean(all32 * all32, axis=-1, keepdims=True) + EPS)
    normed = (all32 * r_all * g_mix).astype(LOW)
    proj = contract(normed, w_mix)
    wide = ((half // LANES, total, LANES), F32)
    d_re, d_im, v_re, v_im, summ = plain_call(
        partial(forward_kernel, half, length),
        [wide] * 4 + [((4, 8, half), F32)],
        3,
        name="gates",
    )(proj, keep, par)
    summ = tie(summ, gate_z[-1])
    summ_all = small_gather(lay, summ, lay.wmasks, partial(w_slot, lay), W, 1)
    cot_blocks = lay.gather_t(tie(cotangent, summ_all))
    up_z = [lay.send(tie(ffn_up[: cuts[0][1]].astype(LOW), summ_all), lay.ZH)]
    st_re, st_im, be_re, be_im, unit, squares = plain_call(
        partial(state_kernel, half, length, n),
        [wide] * 4 + [((total, 2 * half), LOW), ((total, LANES), F32)],
        8,
        smem=1,
        name="states",
    )(ints, summ_all, d_re, d_im, v_re, v_im, proj, g_out)
    branch_low = tie(contract(unit, w_out).astype(LOW), up_z[0])

    def t_blocks(value):
        return [value[j * length : (j + 1) * length] for j in range(4)]

    branch_x, branch_z, got_squares, w_ffn_gate, down_y, down_z, *up_zb = net_call(
        partial(branch_kernel, lay, cuts),
        lay,
        (
            branch_low.reshape(4, length, width),
            squares.reshape(4, length, LANES),
            f_gate,
            f_up,
            f_down,
            *gate_z,
        ),
        [
            ((length, width), LOW),
            ((length, width), LOW),
            ((3, length, LANES), F32),
            ((W, r_ffn, width), LOW),
            ((r_ffn, width), LOW),
            ((cuts[0][1], width), LOW),
        ]
        + [((rows, width), LOW) for _, rows in cuts[1:]],
        2 * W + 10,
        12,
        4,
        "branch",
        40,
        [pltpu.VMEM((length, width), LOW)] * 2
        + [pltpu.VMEM((rows, width), LOW) for _, rows in cuts for _ in range(2)],
    )
    w_ffn_gate = w_ffn_gate.reshape(W * r_ffn, width)

    def own_sum(whole, arrived_parts):
        value = whole[:length].astype(F32)
        for part in arrived_parts:
            value = value + part.astype(F32)
        return value

    square = own_sum(squares, [got_squares[j] for j in range(3)])[:, 0:1]
    branch = own_sum(branch_low, (branch_x, branch_z))
    r_state = lax.rsqrt(square / width + EPS)
    residual = inputs + r_state * branch
    r_res = lax.rsqrt(jnp.mean(residual * residual, axis=-1, keepdims=True) + EPS)
    ffn_low = (residual * r_res * g_ffn).astype(LOW)

    tok_room = pltpu.VMEM((length, width), LOW)
    rooms = [pltpu.VMEM((rows, width), LOW) for _, rows in cuts]
    last = len(cuts) - 1
    down_rooms = [[room] * (3 if i == 0 else 2) for i, room in enumerate(rooms)]
    ffn_all, w_ffn_up, w_down, cot_all = net_call(
        partial(ffn_kernel, lay, cuts),
        lay,
        (ffn_low, f_up, f_down, down_y, down_z, *up_z, *up_zb, *cot_blocks),
        [
            ((4, length, width), LOW),
            ((W, r_ffn, width), LOW),
            ((W, r_ffn, width), LOW),
            ((4, length, width), LOW),
        ],
        4 * W + 8,
        32,
        5,
        "ffn_in",
        40,
        down_rooms[last]
        + [tok_room]
        + [room for i in range(last) for room in down_rooms[i]]
        + [room for room in rooms for _ in range(2)]
        + [tok_room] * 4,
    )
    ffn_all = ffn_all.reshape(total, width)
    w_ffn_up = w_ffn_up.reshape(W * r_ffn, width)
    w_down = w_down.reshape(W * r_ffn, width)
    cot_all = cot_all.reshape(total, width)
    gate_value = contract(ffn_all, w_ffn_gate)
    up_value = contract(ffn_all, w_ffn_up)
    s_gate = jax.nn.sigmoid(gate_value)
    silu_gate = gate_value * s_gate
    hidden_low = (silu_gate * up_value).astype(LOW)
    grad_hidden = contract(cot_all, w_down)
    grad_gate = (grad_hidden * up_value * s_gate * (1.0 + gate_value * (1.0 - s_gate))).astype(LOW)
    grad_up = (grad_hidden * silu_gate).astype(LOW)
    du_low = (
        jnp.dot(grad_gate, w_ffn_gate, preferred_element_type=F32)
        + jnp.dot(grad_up, w_ffn_up, preferred_element_type=F32)
    ).astype(LOW)
    du_blocks = t_blocks(du_low)
    du_got = [lay.send(b, m) for b, m in zip(du_blocks[1:], lay.tmasks[1:])]
    du = du_blocks[0].astype(F32)
    for got in du_got:
        du = du + got.astype(F32)

    def join(kept, got):
        return kept.astype(F32) + got.astype(F32)

    def split_sum(kept, got):
        rows = kept.shape[0] // 2
        return join(kept[:rows], got[:rows]).astype(LOW), join(kept[rows:], got[rows:]).astype(LOW)

    def over_y(kept, away):
        for bit in lay.ybits:
            kept, away = split_sum(kept, lay.send(away, bit))
        return kept, away

    left_gate, left_up, left_hidden, *_ = lax.optimization_barrier(
        (grad_gate, grad_up, hidden_low, *du_blocks)
    )
    gate_part = outer_rows(left_gate, ffn_all).astype(LOW)
    up_part = outer_rows(left_up, ffn_all).astype(LOW)
    down_part = outer_rows(left_hidden, cot_all).astype(LOW)
    mixed_low = jnp.dot(tie(left_hidden, du_got[0]), w_down, preferred_element_type=F32).astype(LOW)

    du_gain = du * g_ffn
    grad_residual = (
        cotangent.astype(F32)
        + r_res * du_gain
        - residual * (r_res * r_res * r_res) * jnp.mean(residual * du_gain, axis=-1, keepdims=True)
    )
    ffn_gain_part = jnp.sum(du * residual * r_res, axis=0)
    grad_low = tie(grad_residual.astype(LOW), mixed_low)
    inner = jnp.sum(grad_low.astype(F32) * branch, axis=-1, keepdims=True) / width
    scale = jnp.where(
        jnp.arange(LANES)[None, :] == 0, r_state, r_state * r_state * r_state * inner
    )

    split = (2,) * len(lay.wbits)
    block = (r_ffn, width)
    grad_all, scale_all, gate_kept, gate_away, up_kept, up_away, down_kept, down_away = net_call(
        partial(grad_kernel, lay),
        lay,
        (grad_low, scale, *[part.reshape(split + block) for part in (gate_part, up_part, down_part)]),
        [((4, length, width), LOW), ((4, length, LANES), F32)] + [(split[2:] + block, LOW)] * 6,
        10,
        13,
        6,
        "grad_in",
        27,
        [pltpu.VMEM((length, width), LOW), pltpu.VMEM((length, LANES), F32)]
        + [pltpu.VMEM(split[1:] + block, LOW)] * 6,
    )
    gate_kept, gate_away = over_y(gate_kept.reshape(-1, width), gate_away.reshape(-1, width))
    grad_all = grad_all.reshape(total, width)
    scale_all = scale_all.reshape(total, LANES)
    grad_mid = jnp.dot(grad_all, w_out, preferred_element_type=F32)
    gs_re, gs_im, gate_low, mid, out_gain_part, back = plain_call(
        partial(back_kernel, half, length),
        [wide] * 2
        + [((total, 2 * half), LOW)] * 2
        + [((8, 2 * half), F32), ((4, 8, half), F32)],
        8,
        scratch=[pltpu.VMEM((8, 2 * half), F32)],
        name="back_gates",
    )(grad_mid, st_re, st_im, proj, g_out, scale_all, d_re, d_im)
    back_all = tie(small_gather(lay, back, lay.wmasks, partial(w_slot, lay), W, 2), gate_away)
    grads, lower_part, angle_part = plain_call(
        partial(adjoint_kernel, half, length, n),
        [((total, 5 * half), LOW), ((8, half), F32), ((8, half), F32)],
        13,
        smem=1,
        scratch=[pltpu.VMEM((half // LANES, total, LANES), F32)] * 2 + [pltpu.VMEM((16, half), F32)],
        name="adjoints",
    )(ints, summ_all, back_all, gs_re, gs_im, d_re, d_im, be_re, be_im, proj, keep, par, gate_low)
    du_mix_low = jnp.dot(grads, w_mix, preferred_element_type=F32).astype(LOW)
    mix_gain_part = jnp.sum(
        du_mix_low.astype(F32) * (all32 * r_all), axis=0
    )

    t_hot = ((jnp.arange(2)[:, None] == zlo) & (jnp.arange(2)[None, :] == x)).astype(F32)
    out_gain_part = jnp.sum(out_gain_part, axis=0).reshape(2, 1, Y, 1, 2 * r_in)
    out_gain_part = (out_gain_part * t_hot[None, :, None, :, None]).reshape(n, r_in)

    def spread(vector):
        vector = jnp.sum(vector, axis=0).reshape(1, Y, 1, half // Y)
        return (vector * t_hot[:, None, :, None]).reshape(n, r_f)

    to_owner = jnp.concatenate(
        [
            mix_gain_part.reshape(n, r_in),
            ffn_gain_part.reshape(n, r_in),
            out_gain_part,
            spread(lower_part),
            spread(angle_part),
        ],
        axis=1,
    )
    to_owner = jnp.pad(to_owner, ((0, 0), (0, 1024 - to_owner.shape[1]))).reshape(n, 8, 128)

    grad_w_out = outer_rows(grad_all, mid).astype(LOW).reshape(2, 2, Y, 2, 2, r_in, 2 * half)
    grad_w_out = grad_w_out.transpose(0, 2, 4, 1, 3, 5, 6).reshape(W, 4 * r_in, 2 * half)
    gate_got = lay.send(tie(gate_away, back_all), lay.ZH)
    up_came = lay.send(tie(up_away, gate_away, back_all), lay.ybits[0])
    du_mix_low = tie(du_mix_low, gate_got)
    part_of = {
        "forget": outer_rows(grads[:, 4 * half :], normed).astype(LOW).reshape(split + (r_f, width)),
        "out": grad_w_out.reshape(split + (4 * r_in, 2 * half)),
        "up": up_kept,
        "down": down_kept,
        "gate": outer_rows(tie(gate_low, up_came), normed).astype(LOW).reshape(split + (r_in, width)),
        "in": outer_rows(grads[:, : 2 * half], normed).astype(LOW).reshape(split + (r_in, width)),
    }
    out_of = {name: (part.shape[-2:], F32) for name, part in part_of.items()}
    out_of["out"] = ((4, r_in, 2 * half), F32)
    parts = [part_of[name] for name in PARTS]
    scratch, copies, local_copies = [pltpu.VMEM((length, width), LOW)] * 4, 6 + 3 + n, 8
    for name, part in zip(PARTS, parts):
        for _, rows in row_cuts(name, part.shape[-2]):
            shape, skip = (rows, part.shape[-1]), first_stage(name)
            scratch.append(pltpu.VMEM(split[1 + skip :] + shape, LOW))
            for k in range(skip, len(split)):
                scratch.append(pltpu.VMEM(split[1 + k :] + shape, LOW))
            scratch.append(pltpu.VMEM(shape, F32))
            copies += len(split)
            local_copies += 3
    *sums, du_x, du_z, mixed_x, mixed_z, owned = net_call(
        partial(reduce_kernel, lay),
        lay,
        (
            *parts,
            up_came,
            down_away,
            du_mix_low.reshape(4, length, width),
            mixed_low.reshape(4, length, width),
            to_owner,
        ),
        [
            *[out_of[name] for name in PARTS],
            *[((length, width), LOW)] * 4,
            ((n, 8, 128), F32),
        ],
        copies,
        local_copies,
        3,
        "reduce",
        120,
        scratch,
    )
    ffn_gate_grad = join(gate_kept, gate_got)
    sum_of = dict(zip(PARTS, sums))
    out_proj_grad = (
        sum_of["out"].reshape(2, 2, r_in, 2, Y, 2 * r_in)
        .transpose(2, 3, 0, 4, 1, 5)
        .reshape(r_in, width)
    )
    owned = jnp.sum(owned, axis=0).reshape(-1)
    mixed_out = (residual + own_sum(mixed_low, (mixed_x, mixed_z))).astype(LOW)
    du_mix = own_sum(du_mix_low, (du_x, du_z))
    dg_mix = du_mix * g_mix
    tokens_grad = (
        grad_residual
        + r_tok * dg_mix
        - inputs * (r_tok * r_tok * r_tok) * jnp.mean(inputs * dg_mix, axis=-1, keepdims=True)
    ).astype(LOW)
    return (
        mixed_out,
        tokens_grad,
        sum_of["in"],
        sum_of["forget"],
        sum_of["gate"],
        out_proj_grad,
        ffn_gate_grad,
        sum_of["up"],
        sum_of["down"],
        owned[0:r_in],
        owned[2 * r_in : 3 * r_in],
        owned[r_in : 2 * r_in],
        owned[3 * r_in : 3 * r_in + r_f],
        owned[3 * r_in + r_f : 3 * r_in + 2 * r_f],
    )


def solution(mesh):
    rows, vector = P("dp", None), P("dp")
    in_specs = (rows, rows, P(), P()) + (rows,) * 7 + (vector,) * 5
    out_specs = (rows,) * 9 + (vector,) * 5
    return jax.shard_map(
        partial(local, mesh.shape["dp"]),
        mesh=mesh,
        in_specs=in_specs,
        out_specs=out_specs,
        check_vma=False,
    )
```

```python
from functools import partial

import jax
import jax.numpy as jnp
from jax import lax
from jax.experimental import pallas as pl
from jax.experimental.pallas import tpu as pltpu
from jax.sharding import PartitionSpec as P


EPS = 1e-06
LOW = jnp.bfloat16
F32 = jnp.float32
MESH = pl.DeviceIdType.MESH
ROWS = 32
LANES = 128


def contract(left_rows, right_rows):
    return lax.dot_general(
        left_rows, right_rows, (((1,), (1,)), ((), ())), preferred_element_type=F32
    )


def outer_rows(left_rows, right_rows):
    return lax.dot_general(
        left_rows, right_rows, (((0,), (0,)), ((), ())), preferred_element_type=F32
    )


def tie(value, *others):
    return lax.optimization_barrier((value,) + others)[0]


class Layout:
    def __init__(self, n):
        self.n = n
        self.Y = n // 16
        self.C, self.X, self.ZL, self.ZH = 1, 2, 4 * self.Y, 8 * self.Y
        self.ybits = []
        bit = 4
        while bit < self.ZL:
            self.ybits.append(bit)
            bit *= 2
        self.wbits = [self.ZH] + self.ybits + [self.C]
        self.rbits = [self.C] + self.ybits + [self.ZH]
        self.tmasks = [0, self.X, self.ZL, self.ZL | self.X]
        self.wmasks = [0]
        for bit in self.wbits:
            self.wmasks = self.wmasks + [m | bit for m in self.wmasks]
        self.bits = [1 << k for k in range(n.bit_length() - 1)]

    def rel_slot(self, mask):
        return ((mask % 2) * self.Y + (mask // 4) % self.Y) * 2 + mask // self.ZH

    def flip(self, device, mask):
        for bit in self.bits:
            if mask & bit:
                device = device + bit * (1 - 2 * ((device // bit) % 2))
        return device

    def parts(self, device):
        c = device % 2
        x = (device // self.X) % 2
        y = (device // 4) % self.Y
        zlo = (device // self.ZL) % 2
        zhi = device // self.ZH
        return zhi, zlo, y, x, c

    def send(self, value, mask):
        return lax.ppermute(value, "dp", [(i, i ^ mask) for i in range(self.n)])

    def gather_t(self, value):
        return [value] + [self.send(value, m) for m in self.tmasks[1:]]

    def scatter_t(self, blocks):
        got = [self.send(b, m) for b, m in zip(blocks[1:], self.tmasks[1:])]
        total = blocks[0].astype(F32)
        for g in got:
            total = total + g.astype(F32)
        return total

    def gather_w(self, value):
        pieces = [value]
        for bit in self.wbits:
            pieces = pieces + [self.send(v, bit) for v in pieces]
        return pieces


def gather_kernel(lay, masks, slot_of, in_ref, out_ref, send_sems, recv_sems):
    me = lax.axis_index("dp")
    peers = [lay.flip(me, m) for m in masks]
    barrier = pltpu.get_barrier_semaphore()
    for peer in peers:
        pl.semaphore_signal(barrier, inc=1, device_id=(peer,), device_id_type=MESH)
    pl.semaphore_wait(barrier, len(peers))
    slot = slot_of(me)
    copies = []
    for i, peer in enumerate(peers):
        copy = pltpu.make_async_remote_copy(
            src_ref=in_ref,
            dst_ref=out_ref.at[pl.ds(slot * in_ref.shape[0], in_ref.shape[0])],
            send_sem=send_sems.at[i],
            recv_sem=recv_sems.at[i],
            device_id=(peer,),
            device_id_type=MESH,
        )
        copy.start()
        copies.append(copy)
    out_ref[pl.ds(slot * in_ref.shape[0], in_ref.shape[0])] = in_ref[...]
    for copy in copies:
        copy.wait()


def small_gather(lay, value, masks, slot_of, slots, collective_id):
    masks = [m for m in masks if m]
    vmem = pl.BlockSpec(memory_space=pltpu.VMEM)
    return pl.pallas_call(
        partial(gather_kernel, lay, masks, slot_of),
        out_shape=jax.ShapeDtypeStruct((slots * value.shape[0],) + value.shape[1:], value.dtype),
        in_specs=[vmem],
        out_specs=vmem,
        scratch_shapes=[
            pltpu.SemaphoreType.DMA((len(masks),)),
            pltpu.SemaphoreType.DMA((len(masks),)),
        ],
        compiler_params=pltpu.CompilerParams(collective_id=collective_id, has_side_effects=True),
        cost_estimate=estimate(10),
    )(value)


class Net:
    def __init__(self, lay, peers, send_sems, recv_sems, local_sems, rooms=()):
        self.lay, self.send_sems, self.recv_sems, self.local_sems = lay, send_sems, recv_sems, local_sems
        self.rooms, self.moving = list(rooms), []
        self.me = lax.axis_index("dp")
        self.used, self.used_local, self.open, self.local = 0, 0, [], []
        barrier = pltpu.get_barrier_semaphore()
        for mask in peers:
            pl.semaphore_signal(
                barrier, inc=1, device_id=(lay.flip(self.me, mask),), device_id_type=MESH
            )
        pl.semaphore_wait(barrier, len(peers))

    def put(self, src, dst, mask):
        copy = pltpu.make_async_remote_copy(
            src_ref=src,
            dst_ref=dst,
            send_sem=self.send_sems.at[self.used],
            recv_sem=self.recv_sems.at[self.used],
            device_id=(self.lay.flip(self.me, mask),),
            device_id_type=MESH,
        )
        copy.start()
        self.used += 1
        self.open.append(copy)
        return copy

    def load(self, src, dst):
        copy = pltpu.make_async_copy(src, dst, self.local_sems.at[self.used_local])
        copy.start()
        self.used_local += 1
        return copy

    def keep(self, src, dst):
        self.local.append(self.load(src, dst))

    def move(self, src, dst):
        room = self.rooms.pop(0)
        self.moving.append((self.load(src, room), room, dst))

    def settle(self):
        for copy, room, dst in self.moving:
            copy.wait()
            self.keep(room, dst)
        self.moving = []

    def finish(self):
        for copy in self.open:
            copy.wait_send()
        for copy in self.local:
            copy.wait()


class WeightGather:
    def __init__(self, net, own, place, early=None):
        self.net, self.own, self.place, self.early = net, own, place, early or {}
        self.bits = net.lay.wbits
        self.pending = {}

    def start(self):
        me = self.net.me
        for bit in self.bits:
            if bit not in self.early:
                self.pending[bit] = self.net.put(self.own, self.place(me, bit), bit)
        self.net.move(self.own, self.place(me, 0))
        for bit, block in self.early.items():
            self.pass_on(bit, block)
            self.net.move(block, self.place(self.net.lay.flip(me, bit), bit))

    def masks(self):
        out = [0]
        for bit in self.bits[:-1]:
            out = out + [m | bit for m in out]
        out = sorted(out[1:], key=lambda m: (bin(m).count("1"), -m))
        return [m for m in out if m not in self.early]

    def pass_on(self, mask, block):
        last = max(i for i, bit in enumerate(self.bits) if mask & bit)
        source = self.net.lay.flip(self.net.me, mask)
        for bit in self.bits[last + 1 :]:
            self.pending[mask | bit] = self.net.put(block, self.place(source, mask | bit), bit)

    def forward(self, mask):
        self.pending[mask].wait_recv()
        self.pass_on(mask, self.place(self.net.lay.flip(self.net.me, mask), mask))

    def end(self):
        for mask, copy in self.pending.items():
            if mask & self.bits[-1]:
                copy.wait_recv()


def token_start(net, own, out):
    lay = net.lay
    first = [net.put(own, out.at[1], lay.X), net.put(own, out.at[2], lay.ZL)]
    net.move(own, out.at[0])
    return first


def token_finish(net, first, out):
    lay, half = net.lay, out.shape[1] // 2
    top, low = pl.ds(0, half), pl.ds(half, half)
    arrived(first[:1])
    copies = [net.put(out.at[1, top], out.at[3, top], lay.ZL)]
    arrived(first[1:])
    return copies + [net.put(out.at[2, low], out.at[3, low], lay.X)]


def token_scatter(net, blocks, out):
    return [net.put(blocks.at[j], out.at[j - 1], m) for j, m in enumerate(net.lay.tmasks) if j]


def arrived(copies):
    for copy in copies:
        copy.wait_recv()


SCALE = 10_000_000


def estimate(micros):
    return pl.CostEstimate(flops=micros * SCALE, bytes_accessed=0, transcendentals=0)


def net_call(body, lay, values, outs, copies, local, collective_id, name, micros, scratch=()):
    hbm = pl.BlockSpec(memory_space=pl.ANY)
    return pl.pallas_call(
        body,
        out_shape=tuple(jax.ShapeDtypeStruct(s, d) for s, d in outs),
        in_specs=[hbm] * len(values),
        out_specs=tuple(hbm for _ in outs),
        scratch_shapes=[
            *scratch,
            pltpu.SemaphoreType.DMA((copies,)),
            pltpu.SemaphoreType.DMA((copies,)),
            pltpu.SemaphoreType.DMA((local,)),
        ],
        compiler_params=pltpu.CompilerParams(
            collective_id=collective_id,
            has_side_effects=True,
            vmem_limit_bytes=60 << 20,
        ),
        cost_estimate=estimate(micros),
        name=name,
    )(*values)


def w_slot(lay, device):
    zhi, _, y, _, c = lay.parts(device)
    return (zhi * lay.Y + y) * 2 + c


def f_slot(lay, device):
    zhi, _, y, _, c = lay.parts(device)
    return (y * 2 + c) * 2 + zhi


def t_slot(lay, device):
    _, zlo, _, x, _ = lay.parts(device)
    return zlo * 2 + x


class Turn:
    def __init__(self, net, target, src, dst):
        self.remote = target != net.me
        self.away = pltpu.make_async_remote_copy(
            src_ref=src,
            dst_ref=dst,
            send_sem=net.send_sems.at[net.used],
            recv_sem=net.recv_sems.at[net.used],
            device_id=(target,),
            device_id_type=MESH,
        )
        self.here = pltpu.make_async_copy(src, dst, net.local_sems.at[net.used_local])
        net.used += 1
        net.used_local += 1

        @pl.when(self.remote)
        def _():
            self.away.start()

        @pl.when(jnp.logical_not(self.remote))
        def _():
            self.here.start()

    def wait(self):
        @pl.when(self.remote)
        def _():
            self.away.wait()

        @pl.when(jnp.logical_not(self.remote))
        def _():
            self.here.wait()


def forget_to(lay, device):
    return (device % 2) * (lay.n // 2) + device // 2


def forget_from(lay, device):
    return 2 * (device % (lay.n // 2)) + device // (lay.n // 2)


def start_kernel(
    lay, units, cuts, tok, w_in, w_gate, w_forget, w_out, pack, wide_0, wide_1, wide_2,
    tok_all, mix_all, forget_own, out_own, out_all, f_gate_z, every, low_0, low_1, low_2, up_a, *rest,
):
    n, W = lay.n, lay.n // 4
    gate_b, rest = rest[: len(cuts) - 1], rest[len(cuts) - 1 :]
    wide_rooms, low_rooms, rest = rest[:3], rest[3:6], rest[6:]
    *rooms, send_sems, recv_sems, local_sems = rest
    net = Net(lay, list(range(1, n)), send_sems, recv_sems, local_sems, rooms)
    me = net.me

    def region(base):
        return lambda d, m: mix_all.at[pl.ds(base + w_slot(lay, d) * units, units)]

    g_in = WeightGather(net, w_in, region(0))
    g_gate = WeightGather(net, w_gate, region(W * units))
    g_forget = WeightGather(
        net, forget_own, lambda d, m: mix_all.at[pl.ds(2 * W * units + f_slot(lay, d), 1)]
    )

    def out_place(d, m):
        zhi, _, y, _, c = lay.parts(d)
        return out_all.at[zhi, :, y, :, c]

    g_out = WeightGather(net, out_own, out_place)
    turn = Turn(net, forget_to(lay, me), w_forget, forget_own)
    g_in.start()
    g_gate.start()
    def square(d):
        _, zlo, _, x, _ = lay.parts(d)
        return zlo, x

    mine = square(me)
    own = net.load(w_out.at[mine], out_own.at[mine])
    out_in = [net.put(w_out.at[square(lay.flip(me, m))], out_own.at[mine], m) for m in lay.tmasks[1:]]
    first = token_start(net, tok, tok_all)
    all_in = [net.put(pack, every.at[me], m) for m in range(1, n)]
    net.keep(pack, every.at[me])
    turn.wait()
    g_forget.start()
    own.wait()
    arrived(out_in)
    g_out.start()
    net.settle()
    wide = [net.load(w, room) for w, room in zip((wide_0, wide_1, wide_2), wide_rooms)]
    for copy, src, room, low in zip(wide, wide_rooms, low_rooms, (low_0, low_1, low_2)):
        copy.wait()
        cast_rows(room, src)
        if low is low_0:
            gate_in = net.put(room.at[pl.ds(*cuts[0])], f_gate_z, lay.ZH)
            for cut, out in zip(cuts[1:], gate_b):
                net.keep(room.at[pl.ds(*cut)], out)
        if low is low_1:
            net.keep(room.at[pl.ds(*cuts[0])], up_a)
        net.keep(room, low)
    for mask in g_in.masks():
        g_in.forward(mask)
        g_gate.forward(mask)
    rest = token_finish(net, first, tok_all)
    for mask in g_forget.masks():
        g_forget.forward(mask)
        g_out.forward(mask)
    for gather in (g_in, g_gate, g_forget, g_out):
        gather.end()
    arrived(rest + [gate_in])
    arrived(all_in)
    net.finish()


def group_peers(lay):
    return lay.tmasks[1:] + lay.wbits


def rel_gather(net, own, early, out, cut):
    rows = pl.ds(*cut)
    early = {bit: block if block.shape[0] == cut[1] else block.at[rows] for bit, block in early.items()}
    return WeightGather(net, own.at[rows], lambda d, m: out.at[net.lay.rel_slot(m), rows], early)


def branch_kernel(lay, cuts, blocks, small, gate, up, down, *rest):
    pieces = len(cuts)
    gate_z, rest = rest[:pieces], rest[pieces:]
    (got_x, got_z, got_small, gate_all, down_y, down_z), rest = rest[:6], rest[6:]
    up_z, rest = rest[: pieces - 1], rest[pieces - 1 :]
    token_rooms, rest = rest[:2], rest[2:]
    *rooms, send_sems, recv_sems, local_sems = rest
    net = Net(lay, group_peers(lay), send_sems, recv_sems, local_sems, rooms)
    gathers = [rel_gather(net, gate, {lay.ZH: z}, gate_all, cut) for cut, z in zip(cuts, gate_z)]
    for gather in gathers:
        gather.start()
    tokens = TokenReduce(net, blocks, got_x, got_z, *token_rooms)
    waits = [net.put(up.at[pl.ds(*cut)], z, lay.ZH) for cut, z in zip(cuts[1:], up_z)]
    waits += token_scatter(net, small, got_small)
    net.settle()
    arrived(waits[: pieces - 1])
    waits = waits[pieces - 1 :]
    waits.append(net.put(down.at[pl.ds(*cuts[0])], down_z, lay.ZH))
    for gather in gathers:
        for mask in gather.masks():
            gather.forward(mask)
    waits.append(net.put(down, down_y, lay.ybits[0]))
    tokens.pass_on()
    for gather in gathers:
        gather.end()
    tokens.end()
    arrived(waits)
    net.finish()


def ffn_kernel(lay, cuts, own, up, down, down_y, down_z, *rest):
    pieces = len(cuts)
    up_z, rest = rest[:pieces], rest[pieces:]
    cot_blocks, (own_all, up_all, down_all, cot_all), rest = rest[:4], rest[4:8], rest[8:]
    *rooms, send_sems, recv_sems, local_sems = rest
    net = Net(lay, group_peers(lay), send_sems, recv_sems, local_sems, rooms)
    gathers = []
    for i, cut in enumerate(cuts):
        early = {lay.ybits[0]: down_y}
        if i == 0:
            early[lay.ZH] = down_z
        gathers.append(rel_gather(net, down, early, down_all, cut))
    for cut, z in zip(cuts, up_z):
        gathers.append(rel_gather(net, up, {lay.ZH: z}, up_all, cut))
    gathers[pieces - 1].start()
    first = token_start(net, own, own_all)
    for i, gather in enumerate(gathers):
        if i != pieces - 1:
            gather.start()
    for j, block in enumerate(cot_blocks):
        net.move(block, cot_all.at[j])
    net.settle()
    rest = token_finish(net, first, own_all)
    for gather in gathers[pieces:] + gathers[:pieces]:
        for mask in gather.masks():
            gather.forward(mask)
    for gather in gathers:
        gather.end()
    arrived(rest)
    net.finish()


def add_rows(out, left, right):
    rows = left.shape[0]
    tile = 16 if rows % 16 == 0 else rows

    def body(i, _):
        at = pl.ds(pl.multiple_of(i * tile, tile), tile)
        out[at, :] = (left[at, :].astype(F32) + right[at, :].astype(F32)).astype(out.dtype)
        return 0

    lax.fori_loop(0, rows // tile, body, 0)


class WeightReduce:
    def __init__(self, net, part, rows, dims, local, stages, total, relative, leaves=None, came=None):
        self.net, self.part, self.rows, self.relative = net, part, rows, relative
        self.local, self.stages, self.total = local, stages, total
        self.leaves, self.came = leaves, came
        self.first = 0 if leaves is None and came is None else 1
        self.bits = net.lay.rbits[self.first :]
        self.dims = [[d for d in dims if d in self.bits]]
        for bit in self.bits:
            self.dims.append([d for d in self.dims[-1] if d != bit])
        self.copy, self.waited = None, -1

    def side(self, k):
        return 0 if self.relative else (self.net.me // self.bits[k]) % 2

    def cut(self, k, away):
        index = [slice(None)] * len(self.dims[k])
        index[self.dims[k].index(self.bits[k])] = 1 - self.side(k) if away else self.side(k)
        if k:
            return self.stages[k - 1].at[tuple(index)]
        return self.part.at[tuple(index) + self.rows]

    def start(self):
        if self.first == 0:
            self.copy = self.net.put(self.cut(0, True), self.stages[0], self.bits[0])
            self.loaded = self.net.load(self.cut(0, False), self.local)
            return
        index = (slice(None),) * len(self.dims[1]) + self.rows
        self.loaded = self.net.load(self.part.at[index] if self.rows else self.part, self.local)
        if self.came is None:
            block = self.leaves.at[index] if self.rows else self.leaves
            self.copy = self.net.put(block, self.stages[0], self.bits[0])
        else:
            block = self.came.at[index] if self.rows else self.came
            self.copy = self.net.load(block, self.stages[0])

    def wait(self, k):
        if self.waited < k:
            if k == 0 and self.came is not None:
                self.copy.wait()
            else:
                self.copy.wait_recv()
            self.waited = k

    def add(self, k, away):
        if k == 0 and away:
            self.loaded.wait()
        stage = self.stages[k]
        old = self.cut(k, False) if k else self.local
        if k + 1 == len(self.bits):
            if away:
                add_rows(self.total, stage, old)
            return
        dims = self.dims[k + 1]
        place = dims.index(self.bits[k + 1])
        side = 1 - self.side(k + 1) if away else self.side(k + 1)
        for number in range(1 << (len(dims) - 1)):
            index = [(number >> j) & 1 for j in range(len(dims) - 1)]
            index = tuple(index[:place] + [side] + index[place:])
            add_rows(stage.at[index], stage.at[index], old.at[index])

    def send(self, k):
        self.copy = self.net.put(self.cut(k, True), self.stages[k], self.bits[k])


def grad_kernel(lay, own, small, gate, up, down, own_all, small_all, *rest):
    outs, (room, small_room, *scratch), (send_sems, recv_sems, local_sems) = rest[:6], rest[6:-3], rest[-3:]
    net = Net(lay, lay.tmasks[1:] + [lay.C], send_sems, recv_sems, local_sems, [room, small_room])
    first = token_start(net, own, own_all)
    waits = [net.put(small, small_all.at[j], m) for j, m in enumerate(lay.tmasks) if j]
    net.move(small, small_all.at[0])
    dims = part_dims(lay, "up")
    jobs = []
    for j, part in enumerate((gate, up, down)):
        local, stage = scratch[2 * j : 2 * j + 2]
        jobs.append(WeightReduce(net, part, (), dims, local, [stage], None, True))
        jobs[-1].start()
    net.settle()
    for j, job in enumerate(jobs):
        job.wait(0)
        job.add(0, True)
        net.keep(job.cut(1, True), outs[2 * j + 1])
        job.add(0, False)
        net.keep(job.cut(1, False), outs[2 * j])
        if j == 0:
            waits += token_finish(net, first, own_all)
    arrived(waits)
    net.finish()


def row_cuts(name, rows):
    if name not in ("up", "down") or rows % 16 or rows < 128:
        return [(0, rows)]
    first = rows // 32 * 16
    return [(0, first), (first, rows - first)]


PARTS = ("up", "forget", "out", "down", "gate", "in")


def cast_rows(out, src):
    rows = src.shape[0]
    tile = 16 if rows % 16 == 0 else rows

    def body(i, _):
        at = pl.ds(pl.multiple_of(i * tile, tile), tile)
        out[at, :] = src[at, :].astype(out.dtype)
        return 0

    lax.fori_loop(0, rows // tile, body, 0)


class TokenReduce:
    def __init__(self, net, blocks, got_x, got_z, room, other):
        lay = net.lay
        self.net, self.room, self.other, self.got_z = net, room, other, got_z
        self.first = [net.put(blocks.at[3], other, lay.X), net.put(blocks.at[1], got_x, lay.X)]
        self.loaded = net.load(blocks.at[2], room)

    def pass_on(self):
        self.first[0].wait_recv()
        self.loaded.wait()
        add_rows(self.room, self.room, self.other)
        self.last = self.net.put(self.room, self.got_z, self.net.lay.ZL)

    def end(self):
        arrived([self.first[1], self.last])


def first_stage(name):
    return 1 if name in ("up", "down") else 0


def part_dims(lay, name):
    y_bits = list(reversed(lay.ybits))
    if name == "forget":
        return y_bits + [lay.C, lay.ZH]
    if name in ("up", "down"):
        return [lay.C] + y_bits + [lay.ZH]
    return [lay.ZH] + y_bits + [lay.C]


LAG = 2


def reduce_kernel(lay, *refs):
    count = len(PARTS)
    parts, refs = refs[:count], refs[count:]
    (up_came, down_leaves, du, mixed, vectors), refs = refs[:5], refs[5:]
    outs, refs = refs[:count], refs[count:]
    (du_x, du_z, mixed_x, mixed_z, all_vectors), refs = refs[:5], refs[5:]
    token_rooms, refs = refs[:4], refs[4:]
    scratch, (send_sems, recv_sems, local_sems) = list(refs[:-3]), refs[-3:]
    net = Net(lay, list(range(1, lay.n)), send_sems, recv_sems, local_sems)
    me = net.me
    jobs, places, turns, waits = [], [], [], []
    for name, part, out in zip(PARTS, parts, outs):
        for first, rows in row_cuts(name, part.shape[-2]):
            local = scratch.pop(0)
            stages = [scratch.pop(0) for _ in lay.rbits[first_stage(name) :]]
            whole = rows == part.shape[-2]
            at = () if whole else (pl.ds(first, rows),)
            relative = name in ("up", "down")
            dims = part_dims(lay, name)
            jobs.append(
                WeightReduce(
                    net,
                    part,
                    at,
                    dims,
                    local,
                    stages,
                    scratch.pop(0),
                    relative,
                    down_leaves if name == "down" else None,
                    up_came if name == "up" else None,
                )
            )
            places.append((name, out if whole else out.at[pl.ds(first, rows)]))
    flows = [[] for _ in lay.rbits]
    late = []
    for job, (name, _) in zip(jobs, places):
        if name in ("gate", "in"):
            late.append(job)
        else:
            job.start()
            if name == "down":
                flows[1].append(job)
    du_sum = TokenReduce(net, du, du_x, du_z, *token_rooms[:2])

    def finish(i):
        total = jobs[i].total
        name, out = places[i]
        if name == "forget":
            turns.append(Turn(net, forget_from(lay, me), total, out))
        elif name == "out":
            rows = total.shape[0] // 4
            mine = t_slot(lay, me)

            def cut(slot):
                return total.at[pl.ds(pl.multiple_of(slot * rows, rows), rows)]

            net.keep(cut(mine), out.at[mine])
            for m in lay.tmasks[1:]:
                waits.append(net.put(cut(t_slot(lay, lay.flip(me, m))), out.at[mine], m))
        else:
            net.keep(total, out)

    depth = len(lay.rbits)
    for tick in range(len(jobs) + depth):
        for k in range(depth + 1):
            i = tick - k
            if not 0 <= i < len(jobs):
                continue
            job = jobs[i]
            last = depth - 1 - job.first
            if k < last:
                job.wait(k)
                job.add(k, True)
                flow = k + 1 + job.first
                if len(flows[flow]) >= LAG:
                    behind = flows[flow][-LAG]
                    behind.wait(flow - behind.first)
                job.send(k + 1)
                flows[flow].append(job)
                job.add(k, False)
            elif k == last + 1:
                job.wait(last)
                job.add(last, True)
                finish(i)
        if tick == 0:
            for job in late:
                job.start()
        if tick == 1:
            waits += [
                net.put(vectors.at[lay.flip(me, m)], all_vectors.at[me], m) for m in range(1, lay.n)
            ]
            net.keep(vectors.at[me], all_vectors.at[me])
            mixed_sum = TokenReduce(net, mixed, mixed_x, mixed_z, *token_rooms[2:])
        if tick == 3:
            du_sum.pass_on()
        if tick == 5:
            mixed_sum.pass_on()
    du_sum.end()
    mixed_sum.end()
    arrived(waits)
    for turn in turns:
        turn.wait()
    net.finish()


def sig(v):
    return 1.0 / (1.0 + jnp.exp(-v))


def lanes(base, h):
    return slice(base + h * LANES, base + (h + 1) * LANES)


def fold_rows(v):
    return jnp.sum(v.reshape(v.shape[0] // 8, 8, v.shape[1]), axis=0)


def forward_kernel(half, length, proj, keep, par, d_re, d_im, v_re, v_im, summ):
    total = d_re.shape[1]
    blocks = total // length
    tiles = half // LANES

    def terms(i, _):
        rows = pl.ds(pl.multiple_of(i * ROWS, ROWS), ROWS)
        kept = keep[rows, :]
        for h in range(tiles):
            at = slice(h * LANES, (h + 1) * LANES)
            lower = par[0:1, at]
            magnitude = lower + (1.0 - lower) * sig(proj[rows, lanes(4 * half, h)])
            rest = 1.0 - magnitude
            d_re[h, rows, :] = kept * magnitude * par[1:2, at]
            d_im[h, rows, :] = kept * magnitude * par[2:3, at]
            a = proj[rows, lanes(0, h)]
            b = proj[rows, lanes(half, h)]
            v_re[h, rows, :] = a * sig(a) * rest
            v_im[h, rows, :] = b * sig(b) * rest
        return 0

    lax.fori_loop(0, total // ROWS, terms, 0)

    def step(t, carry):
        rows = pl.ds(t, blocks, stride=length)
        out = []
        for h in range(tiles):
            p_re, p_im, s_re, s_im = carry[4 * h : 4 * h + 4]
            dr, di = d_re[h, rows, :], d_im[h, rows, :]
            out += [
                dr * p_re - di * p_im,
                dr * p_im + di * p_re,
                dr * s_re - di * s_im + v_re[h, rows, :],
                dr * s_im + di * s_re + v_im[h, rows, :],
            ]
        return tuple(out)

    zero = jnp.zeros((blocks, LANES), F32)
    ends = lax.fori_loop(0, length, step, (zero + 1.0, zero, zero, zero) * tiles, unroll=4)
    for j in range(blocks):
        summ[j, 4:8, :] = jnp.zeros((4, half), F32)
        for h in range(tiles):
            for k in range(4):
                summ[j, k : k + 1, lanes(0, h)] = ends[4 * h + k][j : j + 1, :]


def chain_blocks(half, n, blocks, ints, summ, back):
    tiles = half // LANES

    def chain(i, carry):
        p = i if back is None else n - 1 - i
        tile = summ[ints[p]]
        shift = tile[2:4, :] if back is None else back[ints[p]]
        out = []
        for h in range(tiles):
            at = slice(h * LANES, (h + 1) * LANES)
            old = carry[h * (2 + 2 * blocks) : (h + 1) * (2 + 2 * blocks)]
            c_re, c_im = old[0], old[1]
            a_re = tile[0:1, at]
            a_im = tile[1:2, at] if back is None else -tile[1:2, at]
            out.append(a_re * c_re - a_im * c_im + shift[0:1, at])
            out.append(a_re * c_im + a_im * c_re + shift[1:2, at])
            for j in range(blocks):
                here = ints[n + j] == p
                out.append(jnp.where(here, c_re, old[2 + 2 * j]))
                out.append(jnp.where(here, c_im, old[3 + 2 * j]))
        return tuple(out)

    first = summ[0]
    zero = first[0:1, 0:LANES] - first[0:1, 0:LANES]
    res = lax.fori_loop(0, n, chain, (zero,) * (tiles * (2 + 2 * blocks)))
    entry = []
    for h in range(tiles):
        old = res[h * (2 + 2 * blocks) : (h + 1) * (2 + 2 * blocks)]
        entry.append(jnp.concatenate([old[2 + 2 * j] for j in range(blocks)], axis=0))
        entry.append(jnp.concatenate([old[3 + 2 * j] for j in range(blocks)], axis=0))
    return tuple(entry)


def state_kernel(
    half, length, n, ints, summ, d_re, d_im, v_re, v_im, proj, gain,
    st_re, st_im, be_re, be_im, unit, squares,
):
    total = d_re.shape[1]
    blocks = total // length
    tiles = half // LANES

    def step(t, carry):
        rows = pl.ds(t, blocks, stride=length)
        out = []
        for h in range(tiles):
            s_re, s_im = carry[2 * h], carry[2 * h + 1]
            be_re[h, rows, :] = s_re
            be_im[h, rows, :] = s_im
            dr, di = d_re[h, rows, :], d_im[h, rows, :]
            n_re = dr * s_re - di * s_im + v_re[h, rows, :]
            n_im = dr * s_im + di * s_re + v_im[h, rows, :]
            st_re[h, rows, :] = n_re
            st_im[h, rows, :] = n_im
            out += [n_re, n_im]
        return tuple(out)

    entry = chain_blocks(half, n, blocks, ints, summ, None)
    lax.fori_loop(0, length, step, entry, unroll=4)

    def finish(i, _):
        rows = pl.ds(pl.multiple_of(i * ROWS, ROWS), ROWS)
        square = jnp.zeros((ROWS, 1), F32)
        for h in range(tiles):
            for part, st in ((0, st_re), (1, st_im)):
                v = st[h, rows, :]
                g = proj[rows, lanes((2 + part) * half, h)]
                at = lanes(part * half, h)
                unit[rows, at] = (v * gain[0:1, at] * (g * sig(g))).astype(LOW)
                square = square + jnp.sum(v * v, axis=1, keepdims=True)
        squares[rows, :] = jnp.broadcast_to(square, (ROWS, LANES))
        return 0

    lax.fori_loop(0, total // ROWS, finish, 0)


def back_kernel(
    half, length, grad_mid, st_re, st_im, proj, gain, scale, d_re, d_im,
    gs_re, gs_im, gate_low, mid, gain_grad, summ, acc,
):
    total = d_re.shape[1]
    blocks = total // length
    tiles = half // LANES
    acc[...] = jnp.zeros_like(acc)

    def terms(i, _):
        rows = pl.ds(pl.multiple_of(i * ROWS, ROWS), ROWS)
        r = scale[rows, 0:1]
        q = scale[rows, 1:2]
        for h in range(tiles):
            for part, st, gs in ((0, st_re, gs_re), (1, st_im, gs_im)):
                at = lanes(part * half, h)
                g = proj[rows, lanes((2 + part) * half, h)]
                v = st[h, rows, :]
                gv = gain[0:1, at]
                dm = grad_mid[rows, at]
                sg = sig(g)
                silu = g * sg
                du = dm * silu
                normed = v * r
                scaled = normed * gv
                mid[rows, at] = (scaled * silu).astype(LOW)
                gate_low[rows, at] = (dm * scaled * (sg * (1.0 + g * (1.0 - sg)))).astype(LOW)
                gs[h, rows, :] = du * gv * r - v * q
                acc[:, at] = acc[:, at] + fold_rows(du * normed)
        return 0

    lax.fori_loop(0, total // ROWS, terms, 0)
    gain_grad[...] = acc[...]

    def step(i, carry):
        rows = pl.ds(length - 1 - i, blocks, stride=length)
        out = []
        for h in range(tiles):
            a_re = gs_re[h, rows, :] + carry[2 * h]
            a_im = gs_im[h, rows, :] + carry[2 * h + 1]
            dr, di = d_re[h, rows, :], d_im[h, rows, :]
            out += [dr * a_re + di * a_im, dr * a_im - di * a_re]
        return tuple(out)

    zero = jnp.zeros((blocks, LANES), F32)
    ends = lax.fori_loop(0, length, step, (zero, zero) * tiles, unroll=4)
    for j in range(blocks):
        summ[j, 2:8, :] = jnp.zeros((6, half), F32)
        for h in range(tiles):
            for k in range(2):
                summ[j, k : k + 1, lanes(0, h)] = ends[2 * h + k][j : j + 1, :]


def adjoint_kernel(
    half, length, n, ints, summ, back, gs_re, gs_im, d_re, d_im, be_re, be_im, proj, keep, par, gate_low,
    grads, lower_grad, angle_grad, ad_re, ad_im, acc,
):
    total = d_re.shape[1]
    blocks = total // length
    tiles = half // LANES

    def step(i, carry):
        rows = pl.ds(length - 1 - i, blocks, stride=length)
        out = []
        for h in range(tiles):
            a_re = gs_re[h, rows, :] + carry[2 * h]
            a_im = gs_im[h, rows, :] + carry[2 * h + 1]
            ad_re[h, rows, :] = a_re
            ad_im[h, rows, :] = a_im
            dr, di = d_re[h, rows, :], d_im[h, rows, :]
            out += [dr * a_re + di * a_im, dr * a_im - di * a_re]
        return tuple(out)

    entry = chain_blocks(half, n, blocks, ints, summ, back)
    lax.fori_loop(0, length, step, entry, unroll=4)
    acc[...] = jnp.zeros_like(acc)

    def terms(i, _):
        rows = pl.ds(pl.multiple_of(i * ROWS, ROWS), ROWS)
        kept = keep[rows, :]
        for h in range(tiles):
            at = slice(h * LANES, (h + 1) * LANES)
            lower, cos, sin = par[0:1, at], par[1:2, at], par[2:3, at]
            sf = sig(proj[rows, lanes(4 * half, h)])
            magnitude = lower + (1.0 - lower) * sf
            rest = 1.0 - magnitude
            a = proj[rows, lanes(0, h)]
            b = proj[rows, lanes(half, h)]
            sa, sb = sig(a), sig(b)
            ar, ai = ad_re[h, rows, :], ad_im[h, rows, :]
            br, bi = be_re[h, rows, :], be_im[h, rows, :]
            g_re = ar * br + ai * bi
            g_im = ai * br - ar * bi
            g_mag = kept * (g_re * cos + g_im * sin) - (ar * (a * sa) + ai * (b * sb))
            acc[0:8, at] = acc[0:8, at] + fold_rows(g_mag * (1.0 - sf))
            acc[8:16, at] = acc[8:16, at] + fold_rows(kept * magnitude * (g_im * cos - g_re * sin))
            grads[rows, lanes(0, h)] = (ar * rest * (sa * (1.0 + a * (1.0 - sa)))).astype(LOW)
            grads[rows, lanes(half, h)] = (ai * rest * (sb * (1.0 + b * (1.0 - sb)))).astype(LOW)
            grads[rows, lanes(4 * half, h)] = (g_mag * (1.0 - lower) * sf * (1.0 - sf)).astype(LOW)
        grads[rows, 2 * half : 4 * half] = gate_low[rows, :]
        return 0

    lax.fori_loop(0, total // ROWS, terms, 0)
    lower_grad[...] = acc[0:8, :]
    angle_grad[...] = acc[8:16, :]


VMEM = pl.BlockSpec(memory_space=pltpu.VMEM)
SMEM = pl.BlockSpec(memory_space=pltpu.SMEM)


def plain_call(body, outs, n_in, smem=0, scratch=(), name=None):
    return pl.pallas_call(
        body,
        out_shape=tuple(jax.ShapeDtypeStruct(s, d) for s, d in outs),
        in_specs=[SMEM] * smem + [VMEM] * (n_in - smem),
        out_specs=tuple(VMEM for _ in outs),
        scratch_shapes=list(scratch),
        compiler_params=pltpu.CompilerParams(vmem_limit_bytes=48 << 20),
        cost_estimate=estimate(7),
        name=name,
    )


def local(
    n,
    tokens,
    cotangent,
    seq_lengths,
    block_deal,
    in_proj,
    forget_proj,
    gate_proj,
    out_proj,
    ffn_gate,
    ffn_up,
    ffn_down,
    gain_mix,
    gain_out,
    gain_ffn,
    lower_bound,
    rotation,
):
    lay = Layout(n)
    Y = lay.Y
    W = n // 4
    me = lax.axis_index("dp")
    zhi, zlo, y, x, c = lay.parts(me)
    mine_t = zlo * 2 + x
    length, width = tokens.shape
    half = width // 8
    total = 4 * length
    r_in, r_f = in_proj.shape[0], forget_proj.shape[0]

    indices = jnp.arange(n, dtype=jnp.int32)
    order = jnp.sum(jnp.where(block_deal[None, :] == indices[:, None], indices[None, :], 0), axis=1)
    t_devices = jnp.stack([lay.flip(me, m) for m in lay.tmasks])
    t_places = jnp.sum(
        jnp.where(t_devices[:, None] == indices[None, :], block_deal[None, :], 0), axis=1
    )
    o_parts = lay.parts(order)
    t_rel = ((o_parts[1] + zlo) % 2) * 2 + (o_parts[3] + x) % 2
    ints = jnp.concatenate([w_slot(lay, order) * 4 + t_rel, t_places]).astype(jnp.int32)
    offsets = jnp.cumsum(seq_lengths) - seq_lengths
    positions = (
        t_places[:, None] * length + jnp.arange(length, dtype=jnp.int32)[None, :]
    ).reshape(-1)
    starts = jnp.any(positions[:, None] == offsets[None, :], axis=1)
    keep = jnp.where(starts, 0.0, 1.0).astype(F32)[:, None]

    packed = jnp.concatenate([gain_mix, gain_ffn, gain_out, lower_bound, rotation])
    pack_rows = -(-packed.shape[0] // 128)
    packed = jnp.pad(packed, (0, 8 * 128 - packed.shape[0])).reshape(8, 128)
    out_cols = out_proj.astype(LOW).reshape(r_in, 2, 2, Y, 2, 2 * r_in)
    out_cols = out_cols.transpose(2, 4, 0, 1, 3, 5).reshape(2, 2, r_in, 2 * half)
    units = r_in // r_f
    r_ffn = ffn_gate.shape[0]
    cuts = row_cuts("up", r_ffn)
    tok_all, w_mix, _, _, w_out, gate_za, every, f_gate, f_up, f_down, up_a, *gate_b = net_call(
        partial(start_kernel, lay, units, cuts),
        lay,
        (
            tokens,
            in_proj.astype(LOW).reshape(units, r_f, width),
            gate_proj.astype(LOW).reshape(units, r_f, width),
            forget_proj.astype(LOW).reshape(1, r_f, width),
            out_cols,
            packed,
            ffn_gate,
            ffn_up,
            ffn_down,
        ),
        [
            ((4, length, width), LOW),
            ((W * (2 * units + 1), r_f, width), LOW),
            ((1, r_f, width), LOW),
            ((2, 2, r_in, 2 * half), LOW),
            ((2, 2, Y, 2, 2, r_in, 2 * half), LOW),
            ((cuts[0][1], width), LOW),
            ((n, 8, 128), F32),
            *[((r_ffn, width), LOW)] * 3,
            *[((rows, width), LOW) for _, rows in cuts],
        ],
        4 * (W - 1) + 9 + n - 1,
        32,
        0,
        "start",
        60,
        [
            *[pltpu.VMEM((r_ffn, width), F32)] * 3,
            *[pltpu.VMEM((r_ffn, width), LOW)] * 3,
            pltpu.VMEM((units, r_f, width), LOW),
            pltpu.VMEM((units, r_f, width), LOW),
            pltpu.VMEM((length, width), LOW),
            pltpu.VMEM((1, r_f, width), LOW),
            pltpu.VMEM((2, 2, r_in, 2 * half), LOW),
        ],
    )
    cot_own = tie(cotangent, tok_all)
    cot_x, cot_z = lay.send(cot_own, lay.X), lay.send(cot_own, lay.ZL)
    gate_z = [gate_za]
    if len(cuts) > 1:
        gate_z.append(lay.send(gate_b[0], lay.ZH))
    tok_all = tok_all.reshape(total, width)
    w_mix = w_mix.reshape(5 * half, width)
    w_out = w_out.reshape(width, 2 * half)
    every = every[:, :pack_rows, :].reshape(n, pack_rows * 128)
    g_mix = every[:, 0:r_in].reshape(1, width)
    g_ffn = every[:, r_in : 2 * r_in].reshape(1, width)
    g_out = every[:, 2 * r_in : 3 * r_in].reshape(2, 2, Y, 2, 2 * r_in)
    g_out = lax.dynamic_index_in_dim(g_out, zlo, 1, keepdims=False)
    g_out = lax.dynamic_index_in_dim(g_out, x, 2, keepdims=False).reshape(1, 2 * half)

    def channels(vector):
        vector = vector.reshape(2, Y, 2, half // Y)
        vector = lax.dynamic_index_in_dim(vector, zlo, 0, keepdims=False)
        return lax.dynamic_index_in_dim(vector, x, 1, keepdims=False).reshape(1, half)

    lower = channels(every[:, 3 * r_in : 3 * r_in + r_f])
    angle = channels(every[:, 3 * r_in + r_f : 3 * r_in + 2 * r_f])
    par = jnp.concatenate(
        [lower, jnp.cos(angle), jnp.sin(angle), jnp.zeros((5, half), F32)], axis=0
    )

    inputs = tokens.astype(F32)
    r_tok = lax.rsqrt(jnp.mean(inputs * inputs, axis=-1, keepdims=True) + EPS)
    all32 = tok_all.astype(F32)
    r_all = lax.rsqrt(jnp.mean(all32 * all32, axis=-1, keepdims=True) + EPS)
    normed = (all32 * r_all * g_mix).astype(LOW)
    proj = contract(normed, w_mix)
    wide = ((half // LANES, total, LANES), F32)
    d_re, d_im, v_re, v_im, summ = plain_call(
        partial(forward_kernel, half, length),
        [wide] * 4 + [((4, 8, half), F32)],
        3,
        name="gates",
    )(proj, keep, par)
    summ = tie(summ, gate_z[-1], cot_x, cot_z)
    summ_all = small_gather(lay, summ, lay.wmasks, partial(w_slot, lay), W, 1)
    cot_blocks = [cotangent, cot_x, cot_z, lay.send(tie(cot_z, summ_all), lay.X)]
    up_z = [lay.send(tie(up_a, summ_all), lay.ZH)]
    st_re, st_im, be_re, be_im, unit, squares = plain_call(
        partial(state_kernel, half, length, n),
        [wide] * 4 + [((total, 2 * half), LOW), ((total, LANES), F32)],
        8,
        smem=1,
        name="states",
    )(ints, summ_all, d_re, d_im, v_re, v_im, proj, g_out)
    branch_low = tie(contract(unit, w_out).astype(LOW), up_z[0])

    def t_blocks(value):
        return [value[j * length : (j + 1) * length] for j in range(4)]

    branch_x, branch_z, got_squares, w_ffn_gate, down_y, down_z, *up_zb = net_call(
        partial(branch_kernel, lay, cuts),
        lay,
        (
            branch_low.reshape(4, length, width),
            squares.reshape(4, length, LANES),
            f_gate,
            f_up,
            f_down,
            *gate_z,
        ),
        [
            ((length, width), LOW),
            ((length, width), LOW),
            ((3, length, LANES), F32),
            ((W, r_ffn, width), LOW),
            ((r_ffn, width), LOW),
            ((cuts[0][1], width), LOW),
        ]
        + [((rows, width), LOW) for _, rows in cuts[1:]],
        2 * W + 10,
        12,
        4,
        "branch",
        40,
        [pltpu.VMEM((length, width), LOW)] * 2
        + [pltpu.VMEM((rows, width), LOW) for _, rows in cuts for _ in range(2)],
    )
    w_ffn_gate = w_ffn_gate.reshape(W * r_ffn, width)

    def own_sum(whole, arrived_parts):
        value = whole[:length].astype(F32)
        for part in arrived_parts:
            value = value + part.astype(F32)
        return value

    square = own_sum(squares, [got_squares[j] for j in range(3)])[:, 0:1]
    branch = own_sum(branch_low, (branch_x, branch_z))
    r_state = lax.rsqrt(square / width + EPS)
    residual = inputs + r_state * branch
    r_res = lax.rsqrt(jnp.mean(residual * residual, axis=-1, keepdims=True) + EPS)
    ffn_low = (residual * r_res * g_ffn).astype(LOW)

    tok_room = pltpu.VMEM((length, width), LOW)
    rooms = [pltpu.VMEM((rows, width), LOW) for _, rows in cuts]
    last = len(cuts) - 1
    down_rooms = [[room] * (3 if i == 0 else 2) for i, room in enumerate(rooms)]
    ffn_all, w_ffn_up, w_down, cot_all = net_call(
        partial(ffn_kernel, lay, cuts),
        lay,
        (ffn_low, f_up, f_down, down_y, down_z, *up_z, *up_zb, *cot_blocks),
        [
            ((4, length, width), LOW),
            ((W, r_ffn, width), LOW),
            ((W, r_ffn, width), LOW),
            ((4, length, width), LOW),
        ],
        4 * W + 8,
        32,
        5,
        "ffn_in",
        40,
        down_rooms[last]
        + [tok_room]
        + [room for i in range(last) for room in down_rooms[i]]
        + [room for room in rooms for _ in range(2)]
        + [tok_room] * 4,
    )
    ffn_all = ffn_all.reshape(total, width)
    w_ffn_up = w_ffn_up.reshape(W * r_ffn, width)
    w_down = w_down.reshape(W * r_ffn, width)
    cot_all = cot_all.reshape(total, width)
    gate_value = contract(ffn_all, w_ffn_gate)
    up_value = contract(ffn_all, w_ffn_up)
    s_gate = jax.nn.sigmoid(gate_value)
    silu_gate = gate_value * s_gate
    hidden_low = (silu_gate * up_value).astype(LOW)
    grad_hidden = contract(cot_all, w_down)
    grad_gate = (grad_hidden * up_value * s_gate * (1.0 + gate_value * (1.0 - s_gate))).astype(LOW)
    grad_up = (grad_hidden * silu_gate).astype(LOW)
    du_low = (
        jnp.dot(grad_gate, w_ffn_gate, preferred_element_type=F32)
        + jnp.dot(grad_up, w_ffn_up, preferred_element_type=F32)
    ).astype(LOW)
    du_blocks = t_blocks(du_low)
    du_got = [lay.send(b, m) for b, m in zip(du_blocks[1:], lay.tmasks[1:])]
    du = du_blocks[0].astype(F32)
    for got in du_got:
        du = du + got.astype(F32)

    def join(kept, got):
        return kept.astype(F32) + got.astype(F32)

    def split_sum(kept, got):
        rows = kept.shape[0] // 2
        return join(kept[:rows], got[:rows]).astype(LOW), join(kept[rows:], got[rows:]).astype(LOW)

    def over_y(kept, away):
        for bit in lay.ybits:
            kept, away = split_sum(kept, lay.send(away, bit))
        return kept, away

    left_gate, left_up, left_hidden, *_ = lax.optimization_barrier(
        (grad_gate, grad_up, hidden_low, *du_blocks)
    )
    gate_part = outer_rows(left_gate, ffn_all).astype(LOW)
    up_part = outer_rows(left_up, ffn_all).astype(LOW)
    down_part = outer_rows(left_hidden, cot_all).astype(LOW)
    mixed_low = jnp.dot(tie(left_hidden, du_got[0]), w_down, preferred_element_type=F32).astype(LOW)

    du_gain = du * g_ffn
    grad_residual = (
        cotangent.astype(F32)
        + r_res * du_gain
        - residual * (r_res * r_res * r_res) * jnp.mean(residual * du_gain, axis=-1, keepdims=True)
    )
    ffn_gain_part = jnp.sum(du * residual * r_res, axis=0)
    grad_low = tie(grad_residual.astype(LOW), mixed_low)
    inner = jnp.sum(grad_low.astype(F32) * branch, axis=-1, keepdims=True) / width
    scale = jnp.where(
        jnp.arange(LANES)[None, :] == 0, r_state, r_state * r_state * r_state * inner
    )

    split = (2,) * len(lay.wbits)
    block = (r_ffn, width)
    grad_all, scale_all, gate_kept, gate_away, up_kept, up_away, down_kept, down_away = net_call(
        partial(grad_kernel, lay),
        lay,
        (grad_low, scale, *[part.reshape(split + block) for part in (gate_part, up_part, down_part)]),
        [((4, length, width), LOW), ((4, length, LANES), F32)] + [(split[2:] + block, LOW)] * 6,
        10,
        13,
        6,
        "grad_in",
        27,
        [pltpu.VMEM((length, width), LOW), pltpu.VMEM((length, LANES), F32)]
        + [pltpu.VMEM(split[1:] + block, LOW)] * 6,
    )
    gate_kept, gate_away = over_y(gate_kept.reshape(-1, width), gate_away.reshape(-1, width))
    grad_all = grad_all.reshape(total, width)
    scale_all = scale_all.reshape(total, LANES)
    grad_mid = jnp.dot(grad_all, w_out, preferred_element_type=F32)
    gs_re, gs_im, gate_low, mid, out_gain_part, back = plain_call(
        partial(back_kernel, half, length),
        [wide] * 2
        + [((total, 2 * half), LOW)] * 2
        + [((8, 2 * half), F32), ((4, 8, half), F32)],
        8,
        scratch=[pltpu.VMEM((8, 2 * half), F32)],
        name="back_gates",
    )(grad_mid, st_re, st_im, proj, g_out, scale_all, d_re, d_im)
    back_all = tie(small_gather(lay, back, lay.wmasks, partial(w_slot, lay), W, 2), gate_away)
    grads, lower_part, angle_part = plain_call(
        partial(adjoint_kernel, half, length, n),
        [((total, 5 * half), LOW), ((8, half), F32), ((8, half), F32)],
        13,
        smem=1,
        scratch=[pltpu.VMEM((half // LANES, total, LANES), F32)] * 2 + [pltpu.VMEM((16, half), F32)],
        name="adjoints",
    )(ints, summ_all, back_all, gs_re, gs_im, d_re, d_im, be_re, be_im, proj, keep, par, gate_low)
    du_mix_low = jnp.dot(grads, w_mix, preferred_element_type=F32).astype(LOW)
    mix_gain_part = jnp.sum(
        du_mix_low.astype(F32) * (all32 * r_all), axis=0
    )

    t_hot = ((jnp.arange(2)[:, None] == zlo) & (jnp.arange(2)[None, :] == x)).astype(F32)
    out_gain_part = jnp.sum(out_gain_part, axis=0).reshape(2, 1, Y, 1, 2 * r_in)
    out_gain_part = (out_gain_part * t_hot[None, :, None, :, None]).reshape(n, r_in)

    def spread(vector):
        vector = jnp.sum(vector, axis=0).reshape(1, Y, 1, half // Y)
        return (vector * t_hot[:, None, :, None]).reshape(n, r_f)

    to_owner = jnp.concatenate(
        [
            mix_gain_part.reshape(n, r_in),
            ffn_gain_part.reshape(n, r_in),
            out_gain_part,
            spread(lower_part),
            spread(angle_part),
        ],
        axis=1,
    )
    to_owner = jnp.pad(to_owner, ((0, 0), (0, 1024 - to_owner.shape[1]))).reshape(n, 8, 128)

    grad_w_out = outer_rows(grad_all, mid).astype(LOW).reshape(2, 2, Y, 2, 2, r_in, 2 * half)
    grad_w_out = grad_w_out.transpose(0, 2, 4, 1, 3, 5, 6).reshape(W, 4 * r_in, 2 * half)
    gate_got = lay.send(tie(gate_away, back_all), lay.ZH)
    up_came = lay.send(tie(up_away, gate_away, back_all), lay.ybits[0])
    du_mix_low = tie(du_mix_low, gate_got)
    part_of = {
        "forget": outer_rows(grads[:, 4 * half :], normed).astype(LOW).reshape(split + (r_f, width)),
        "out": grad_w_out.reshape(split + (4 * r_in, 2 * half)),
        "up": up_kept,
        "down": down_kept,
        "gate": outer_rows(gate_low, normed).astype(LOW).reshape(split + (r_in, width)),
        "in": outer_rows(grads[:, : 2 * half], normed).astype(LOW).reshape(split + (r_in, width)),
    }
    out_of = {name: (part.shape[-2:], F32) for name, part in part_of.items()}
    out_of["out"] = ((4, r_in, 2 * half), F32)
    parts = [part_of[name] for name in PARTS]
    scratch, copies, local_copies = [pltpu.VMEM((length, width), LOW)] * 4, 6 + 3 + n, 8
    for name, part in zip(PARTS, parts):
        for _, rows in row_cuts(name, part.shape[-2]):
            shape, skip = (rows, part.shape[-1]), first_stage(name)
            scratch.append(pltpu.VMEM(split[1 + skip :] + shape, LOW))
            for k in range(skip, len(split)):
                scratch.append(pltpu.VMEM(split[1 + k :] + shape, LOW))
            scratch.append(pltpu.VMEM(shape, F32))
            copies += len(split)
            local_copies += 3
    *sums, du_x, du_z, mixed_x, mixed_z, owned = net_call(
        partial(reduce_kernel, lay),
        lay,
        (
            *parts,
            up_came,
            down_away,
            du_mix_low.reshape(4, length, width),
            mixed_low.reshape(4, length, width),
            to_owner,
        ),
        [
            *[out_of[name] for name in PARTS],
            *[((length, width), LOW)] * 4,
            ((n, 8, 128), F32),
        ],
        copies,
        local_copies,
        3,
        "reduce",
        120,
        scratch,
    )
    ffn_gate_grad = join(gate_kept, gate_got)
    sum_of = dict(zip(PARTS, sums))
    out_proj_grad = (
        sum_of["out"].reshape(2, 2, r_in, 2, Y, 2 * r_in)
        .transpose(2, 3, 0, 4, 1, 5)
        .reshape(r_in, width)
    )
    owned = jnp.sum(owned, axis=0).reshape(-1)
    mixed_out = (residual + own_sum(mixed_low, (mixed_x, mixed_z))).astype(LOW)
    du_mix = own_sum(du_mix_low, (du_x, du_z))
    dg_mix = du_mix * g_mix
    tokens_grad = (
        grad_residual
        + r_tok * dg_mix
        - inputs * (r_tok * r_tok * r_tok) * jnp.mean(inputs * dg_mix, axis=-1, keepdims=True)
    ).astype(LOW)
    return (
        mixed_out,
        tokens_grad,
        sum_of["in"],
        sum_of["forget"],
        sum_of["gate"],
        out_proj_grad,
        ffn_gate_grad,
        sum_of["up"],
        sum_of["down"],
        owned[0:r_in],
        owned[2 * r_in : 3 * r_in],
        owned[r_in : 2 * r_in],
        owned[3 * r_in : 3 * r_in + r_f],
        owned[3 * r_in + r_f : 3 * r_in + 2 * r_f],
    )


def solution(mesh):
    rows, vector = P("dp", None), P("dp")
    in_specs = (rows, rows, P(), P()) + (rows,) * 7 + (vector,) * 5
    out_specs = (rows,) * 9 + (vector,) * 5
    return jax.shard_map(
        partial(local, mesh.shape["dp"]),
        mesh=mesh,
        in_specs=in_specs,
        out_specs=out_specs,
        check_vma=False,
    )
```

```python
from functools import partial

import jax
import jax.numpy as jnp
from jax import lax
from jax.experimental import pallas as pl
from jax.experimental.pallas import tpu as pltpu
from jax.sharding import PartitionSpec as P


EPS = 1e-06
LOW = jnp.bfloat16
F32 = jnp.float32
MESH = pl.DeviceIdType.MESH
ROWS = 32
LANES = 128


def contract(left_rows, right_rows):
    return lax.dot_general(
        left_rows, right_rows, (((1,), (1,)), ((), ())), preferred_element_type=F32
    )


def outer_rows(left_rows, right_rows):
    return lax.dot_general(
        left_rows, right_rows, (((0,), (0,)), ((), ())), preferred_element_type=F32
    )


def tie(value, *others):
    return lax.optimization_barrier((value,) + others)[0]


class Layout:
    def __init__(self, n):
        self.n = n
        self.Y = n // 16
        self.C, self.X, self.ZL, self.ZH = 1, 2, 4 * self.Y, 8 * self.Y
        self.ybits = []
        bit = 4
        while bit < self.ZL:
            self.ybits.append(bit)
            bit *= 2
        self.wbits = [self.ZH] + self.ybits + [self.C]
        self.rbits = [self.C] + self.ybits + [self.ZH]
        self.tmasks = [0, self.X, self.ZL, self.ZL | self.X]
        self.wmasks = [0]
        for bit in self.wbits:
            self.wmasks = self.wmasks + [m | bit for m in self.wmasks]
        self.bits = [1 << k for k in range(n.bit_length() - 1)]

    def rel_slot(self, mask):
        return ((mask % 2) * self.Y + (mask // 4) % self.Y) * 2 + mask // self.ZH

    def flip(self, device, mask):
        for bit in self.bits:
            if mask & bit:
                device = device + bit * (1 - 2 * ((device // bit) % 2))
        return device

    def parts(self, device):
        c = device % 2
        x = (device // self.X) % 2
        y = (device // 4) % self.Y
        zlo = (device // self.ZL) % 2
        zhi = device // self.ZH
        return zhi, zlo, y, x, c

    def send(self, value, mask):
        return lax.ppermute(value, "dp", [(i, i ^ mask) for i in range(self.n)])

    def gather_t(self, value):
        return [value] + [self.send(value, m) for m in self.tmasks[1:]]

    def scatter_t(self, blocks):
        got = [self.send(b, m) for b, m in zip(blocks[1:], self.tmasks[1:])]
        total = blocks[0].astype(F32)
        for g in got:
            total = total + g.astype(F32)
        return total

    def gather_w(self, value):
        pieces = [value]
        for bit in self.wbits:
            pieces = pieces + [self.send(v, bit) for v in pieces]
        return pieces


def gather_kernel(lay, masks, slot_of, in_ref, out_ref, send_sems, recv_sems):
    me = lax.axis_index("dp")
    peers = [lay.flip(me, m) for m in masks]
    barrier = pltpu.get_barrier_semaphore()
    for peer in peers:
        pl.semaphore_signal(barrier, inc=1, device_id=(peer,), device_id_type=MESH)
    pl.semaphore_wait(barrier, len(peers))
    slot = slot_of(me)
    copies = []
    for i, peer in enumerate(peers):
        copy = pltpu.make_async_remote_copy(
            src_ref=in_ref,
            dst_ref=out_ref.at[pl.ds(slot * in_ref.shape[0], in_ref.shape[0])],
            send_sem=send_sems.at[i],
            recv_sem=recv_sems.at[i],
            device_id=(peer,),
            device_id_type=MESH,
        )
        copy.start()
        copies.append(copy)
    out_ref[pl.ds(slot * in_ref.shape[0], in_ref.shape[0])] = in_ref[...]
    for copy in copies:
        copy.wait()


def small_gather(lay, value, masks, slot_of, slots, collective_id):
    masks = [m for m in masks if m]
    vmem = pl.BlockSpec(memory_space=pltpu.VMEM)
    return pl.pallas_call(
        partial(gather_kernel, lay, masks, slot_of),
        out_shape=jax.ShapeDtypeStruct((slots * value.shape[0],) + value.shape[1:], value.dtype),
        in_specs=[vmem],
        out_specs=vmem,
        scratch_shapes=[
            pltpu.SemaphoreType.DMA((len(masks),)),
            pltpu.SemaphoreType.DMA((len(masks),)),
        ],
        compiler_params=pltpu.CompilerParams(collective_id=collective_id, has_side_effects=True),
        cost_estimate=estimate(10),
    )(value)


class Net:
    def __init__(self, lay, peers, send_sems, recv_sems, local_sems, rooms=()):
        self.lay, self.send_sems, self.recv_sems, self.local_sems = lay, send_sems, recv_sems, local_sems
        self.rooms, self.moving = list(rooms), []
        self.me = lax.axis_index("dp")
        self.used, self.used_local, self.open, self.local = 0, 0, [], []
        barrier = pltpu.get_barrier_semaphore()
        for mask in peers:
            pl.semaphore_signal(
                barrier, inc=1, device_id=(lay.flip(self.me, mask),), device_id_type=MESH
            )
        pl.semaphore_wait(barrier, len(peers))

    def put(self, src, dst, mask):
        copy = pltpu.make_async_remote_copy(
            src_ref=src,
            dst_ref=dst,
            send_sem=self.send_sems.at[self.used],
            recv_sem=self.recv_sems.at[self.used],
            device_id=(self.lay.flip(self.me, mask),),
            device_id_type=MESH,
        )
        copy.start()
        self.used += 1
        self.open.append(copy)
        return copy

    def load(self, src, dst):
        copy = pltpu.make_async_copy(src, dst, self.local_sems.at[self.used_local])
        copy.start()
        self.used_local += 1
        return copy

    def keep(self, src, dst):
        self.local.append(self.load(src, dst))

    def move(self, src, dst):
        room = self.rooms.pop(0)
        self.moving.append((self.load(src, room), room, dst))

    def settle(self):
        for copy, room, dst in self.moving:
            copy.wait()
            self.keep(room, dst)
        self.moving = []

    def finish(self):
        for copy in self.open:
            copy.wait_send()
        for copy in self.local:
            copy.wait()


class WeightGather:
    def __init__(self, net, own, place, early=None):
        self.net, self.own, self.place, self.early = net, own, place, early or {}
        self.bits = net.lay.wbits
        self.pending = {}

    def start(self):
        me = self.net.me
        for bit in self.bits:
            if bit not in self.early:
                self.pending[bit] = self.net.put(self.own, self.place(me, bit), bit)
        self.net.move(self.own, self.place(me, 0))
        for bit, block in self.early.items():
            self.pass_on(bit, block)
            self.net.move(block, self.place(self.net.lay.flip(me, bit), bit))

    def masks(self):
        out = [0]
        for bit in self.bits[:-1]:
            out = out + [m | bit for m in out]
        out = sorted(out[1:], key=lambda m: (bin(m).count("1"), -m))
        return [m for m in out if m not in self.early]

    def pass_on(self, mask, block):
        last = max(i for i, bit in enumerate(self.bits) if mask & bit)
        source = self.net.lay.flip(self.net.me, mask)
        for bit in self.bits[last + 1 :]:
            self.pending[mask | bit] = self.net.put(block, self.place(source, mask | bit), bit)

    def forward(self, mask):
        self.pending[mask].wait_recv()
        self.pass_on(mask, self.place(self.net.lay.flip(self.net.me, mask), mask))

    def end(self):
        for mask, copy in self.pending.items():
            if mask & self.bits[-1]:
                copy.wait_recv()


def token_start(net, own, out):
    lay = net.lay
    first = [net.put(own, out.at[1], lay.X), net.put(own, out.at[2], lay.ZL)]
    net.move(own, out.at[0])
    return first


def token_finish(net, first, out):
    lay, half = net.lay, out.shape[1] // 2
    top, low = pl.ds(0, half), pl.ds(half, half)
    arrived(first[:1])
    copies = [net.put(out.at[1, top], out.at[3, top], lay.ZL)]
    arrived(first[1:])
    return copies + [net.put(out.at[2, low], out.at[3, low], lay.X)]


def token_scatter(net, blocks, out):
    return [net.put(blocks.at[j], out.at[j - 1], m) for j, m in enumerate(net.lay.tmasks) if j]


def arrived(copies):
    for copy in copies:
        copy.wait_recv()


SCALE = 10_000_000


def estimate(micros):
    return pl.CostEstimate(flops=micros * SCALE, bytes_accessed=0, transcendentals=0)


def net_call(body, lay, values, outs, copies, local, collective_id, name, micros, scratch=()):
    hbm = pl.BlockSpec(memory_space=pl.ANY)
    return pl.pallas_call(
        body,
        out_shape=tuple(jax.ShapeDtypeStruct(s, d) for s, d in outs),
        in_specs=[hbm] * len(values),
        out_specs=tuple(hbm for _ in outs),
        scratch_shapes=[
            *scratch,
            pltpu.SemaphoreType.DMA((copies,)),
            pltpu.SemaphoreType.DMA((copies,)),
            pltpu.SemaphoreType.DMA((local,)),
        ],
        compiler_params=pltpu.CompilerParams(
            collective_id=collective_id,
            has_side_effects=True,
            vmem_limit_bytes=60 << 20,
        ),
        cost_estimate=estimate(micros),
        name=name,
    )(*values)


def w_slot(lay, device):
    zhi, _, y, _, c = lay.parts(device)
    return (zhi * lay.Y + y) * 2 + c


def f_slot(lay, device):
    zhi, _, y, _, c = lay.parts(device)
    return (y * 2 + c) * 2 + zhi


def t_slot(lay, device):
    _, zlo, _, x, _ = lay.parts(device)
    return zlo * 2 + x


class Turn:
    def __init__(self, net, target, src, dst):
        self.remote = target != net.me
        self.away = pltpu.make_async_remote_copy(
            src_ref=src,
            dst_ref=dst,
            send_sem=net.send_sems.at[net.used],
            recv_sem=net.recv_sems.at[net.used],
            device_id=(target,),
            device_id_type=MESH,
        )
        self.here = pltpu.make_async_copy(src, dst, net.local_sems.at[net.used_local])
        net.used += 1
        net.used_local += 1

        @pl.when(self.remote)
        def _():
            self.away.start()

        @pl.when(jnp.logical_not(self.remote))
        def _():
            self.here.start()

    def wait(self):
        @pl.when(self.remote)
        def _():
            self.away.wait()

        @pl.when(jnp.logical_not(self.remote))
        def _():
            self.here.wait()


def forget_to(lay, device):
    return (device % 2) * (lay.n // 2) + device // 2


def forget_from(lay, device):
    return 2 * (device % (lay.n // 2)) + device // (lay.n // 2)


def start_kernel(
    lay, units, cuts, tok, w_in, w_gate, w_forget, w_out, pack, wide_0, wide_1, wide_2,
    tok_all, mix_all, forget_own, out_own, out_all, f_gate_z, every, low_0, low_1, low_2, up_a, *rest,
):
    n, W = lay.n, lay.n // 4
    gate_b, rest = rest[: len(cuts) - 1], rest[len(cuts) - 1 :]
    wide_rooms, low_rooms, rest = rest[:3], rest[3:6], rest[6:]
    *rooms, send_sems, recv_sems, local_sems = rest
    net = Net(lay, list(range(1, n)), send_sems, recv_sems, local_sems, rooms)
    me = net.me

    def region(base):
        return lambda d, m: mix_all.at[pl.ds(base + w_slot(lay, d) * units, units)]

    g_in = WeightGather(net, w_in, region(0))
    g_gate = WeightGather(net, w_gate, region(W * units))
    g_forget = WeightGather(
        net, forget_own, lambda d, m: mix_all.at[pl.ds(2 * W * units + f_slot(lay, d), 1)]
    )

    def out_place(d, m):
        zhi, _, y, _, c = lay.parts(d)
        return out_all.at[zhi, :, y, :, c]

    g_out = WeightGather(net, out_own, out_place)
    turn = Turn(net, forget_to(lay, me), w_forget, forget_own)
    g_in.start()
    g_gate.start()
    def square(d):
        _, zlo, _, x, _ = lay.parts(d)
        return zlo, x

    mine = square(me)
    own = net.load(w_out.at[mine], out_own.at[mine])
    out_in = [net.put(w_out.at[square(lay.flip(me, m))], out_own.at[mine], m) for m in lay.tmasks[1:]]
    first = token_start(net, tok, tok_all)
    all_in = [net.put(pack, every.at[me], m) for m in range(1, n)]
    net.keep(pack, every.at[me])
    turn.wait()
    g_forget.start()
    own.wait()
    arrived(out_in)
    g_out.start()
    net.settle()
    wide = [net.load(w, room) for w, room in zip((wide_0, wide_1, wide_2), wide_rooms)]
    for copy, src, room, low in zip(wide, wide_rooms, low_rooms, (low_0, low_1, low_2)):
        copy.wait()
        cast_rows(room, src)
        if low is low_0:
            gate_in = net.put(room.at[pl.ds(*cuts[0])], f_gate_z, lay.ZH)
            for cut, out in zip(cuts[1:], gate_b):
                net.keep(room.at[pl.ds(*cut)], out)
        if low is low_1:
            net.keep(room.at[pl.ds(*cuts[0])], up_a)
        net.keep(room, low)
    for mask in g_in.masks():
        g_in.forward(mask)
        g_gate.forward(mask)
    rest = token_finish(net, first, tok_all)
    for mask in g_forget.masks():
        g_forget.forward(mask)
        g_out.forward(mask)
    for gather in (g_in, g_gate, g_forget, g_out):
        gather.end()
    arrived(rest + [gate_in])
    arrived(all_in)
    net.finish()


def group_peers(lay):
    return lay.tmasks[1:] + lay.wbits


def rel_gather(net, own, early, out, cut):
    rows = pl.ds(*cut)
    early = {bit: block if block.shape[0] == cut[1] else block.at[rows] for bit, block in early.items()}
    return WeightGather(net, own.at[rows], lambda d, m: out.at[net.lay.rel_slot(m), rows], early)


def branch_kernel(lay, cuts, blocks, small, gate, up, down, *rest):
    pieces = len(cuts)
    gate_z, rest = rest[:pieces], rest[pieces:]
    (got_x, got_z, got_small, gate_all, down_y, down_z), rest = rest[:6], rest[6:]
    up_z, rest = rest[: pieces - 1], rest[pieces - 1 :]
    token_rooms, rest = rest[:2], rest[2:]
    *rooms, send_sems, recv_sems, local_sems = rest
    net = Net(lay, group_peers(lay), send_sems, recv_sems, local_sems, rooms)
    gathers = [rel_gather(net, gate, {lay.ZH: z}, gate_all, cut) for cut, z in zip(cuts, gate_z)]
    for gather in gathers:
        gather.start()
    tokens = TokenReduce(net, blocks, got_x, got_z, *token_rooms)
    waits = [net.put(up.at[pl.ds(*cut)], z, lay.ZH) for cut, z in zip(cuts[1:], up_z)]
    waits += token_scatter(net, small, got_small)
    net.settle()
    arrived(waits[: pieces - 1])
    waits = waits[pieces - 1 :]
    waits.append(net.put(down.at[pl.ds(*cuts[0])], down_z, lay.ZH))
    for gather in gathers:
        for mask in gather.masks():
            gather.forward(mask)
    waits.append(net.put(down, down_y, lay.ybits[0]))
    tokens.pass_on()
    for gather in gathers:
        gather.end()
    tokens.end()
    arrived(waits)
    net.finish()


def ffn_kernel(lay, cuts, own, up, down, down_y, down_z, *rest):
    pieces = len(cuts)
    up_z, rest = rest[:pieces], rest[pieces:]
    cot_blocks, (own_all, up_all, down_all, cot_all), rest = rest[:4], rest[4:8], rest[8:]
    *rooms, send_sems, recv_sems, local_sems = rest
    net = Net(lay, group_peers(lay), send_sems, recv_sems, local_sems, rooms)
    gathers = []
    for i, cut in enumerate(cuts):
        early = {lay.ybits[0]: down_y}
        if i == 0:
            early[lay.ZH] = down_z
        gathers.append(rel_gather(net, down, early, down_all, cut))
    for cut, z in zip(cuts, up_z):
        gathers.append(rel_gather(net, up, {lay.ZH: z}, up_all, cut))
    gathers[pieces - 1].start()
    first = token_start(net, own, own_all)
    for i, gather in enumerate(gathers):
        if i != pieces - 1:
            gather.start()
    for j, block in enumerate(cot_blocks):
        net.move(block, cot_all.at[j])
    net.settle()
    rest = token_finish(net, first, own_all)
    for gather in gathers[pieces:] + gathers[:pieces]:
        for mask in gather.masks():
            gather.forward(mask)
    for gather in gathers:
        gather.end()
    arrived(rest)
    net.finish()


def add_rows(out, left, right):
    rows = left.shape[0]
    tile = 16 if rows % 16 == 0 else rows

    def body(i, _):
        at = pl.ds(pl.multiple_of(i * tile, tile), tile)
        out[at, :] = (left[at, :].astype(F32) + right[at, :].astype(F32)).astype(out.dtype)
        return 0

    lax.fori_loop(0, rows // tile, body, 0)


class WeightReduce:
    def __init__(self, net, part, rows, dims, local, stages, total, relative, leaves=None, came=None):
        self.net, self.part, self.rows, self.relative = net, part, rows, relative
        self.local, self.stages, self.total = local, stages, total
        self.leaves, self.came = leaves, came
        self.first = 0 if leaves is None and came is None else 1
        self.bits = net.lay.rbits[self.first :]
        self.dims = [[d for d in dims if d in self.bits]]
        for bit in self.bits:
            self.dims.append([d for d in self.dims[-1] if d != bit])
        self.copy, self.waited = None, -1

    def side(self, k):
        return 0 if self.relative else (self.net.me // self.bits[k]) % 2

    def cut(self, k, away):
        index = [slice(None)] * len(self.dims[k])
        index[self.dims[k].index(self.bits[k])] = 1 - self.side(k) if away else self.side(k)
        if k:
            return self.stages[k - 1].at[tuple(index)]
        return self.part.at[tuple(index) + self.rows]

    def start(self):
        if self.first == 0:
            self.copy = self.net.put(self.cut(0, True), self.stages[0], self.bits[0])
            self.loaded = self.net.load(self.cut(0, False), self.local)
            return
        index = (slice(None),) * len(self.dims[1]) + self.rows
        self.loaded = self.net.load(self.part.at[index] if self.rows else self.part, self.local)
        if self.came is None:
            block = self.leaves.at[index] if self.rows else self.leaves
            self.copy = self.net.put(block, self.stages[0], self.bits[0])
        else:
            block = self.came.at[index] if self.rows else self.came
            self.copy = self.net.load(block, self.stages[0])

    def wait(self, k):
        if self.waited < k:
            if k == 0 and self.came is not None:
                self.copy.wait()
            else:
                self.copy.wait_recv()
            self.waited = k

    def add(self, k, away):
        if k == 0 and away:
            self.loaded.wait()
        stage = self.stages[k]
        old = self.cut(k, False) if k else self.local
        if k + 1 == len(self.bits):
            if away:
                add_rows(self.total, stage, old)
            return
        dims = self.dims[k + 1]
        place = dims.index(self.bits[k + 1])
        side = 1 - self.side(k + 1) if away else self.side(k + 1)
        for number in range(1 << (len(dims) - 1)):
            index = [(number >> j) & 1 for j in range(len(dims) - 1)]
            index = tuple(index[:place] + [side] + index[place:])
            add_rows(stage.at[index], stage.at[index], old.at[index])

    def send(self, k):
        self.copy = self.net.put(self.cut(k, True), self.stages[k], self.bits[k])


def grad_kernel(lay, own, small, gate, up, down, own_all, small_all, *rest):
    outs, (room, small_room, *scratch), (send_sems, recv_sems, local_sems) = rest[:6], rest[6:-3], rest[-3:]
    net = Net(lay, lay.tmasks[1:] + [lay.C], send_sems, recv_sems, local_sems, [room, small_room])
    first = token_start(net, own, own_all)
    waits = [net.put(small, small_all.at[j], m) for j, m in enumerate(lay.tmasks) if j]
    net.move(small, small_all.at[0])
    dims = part_dims(lay, "up")
    jobs = []
    for j, part in enumerate((gate, up, down)):
        local, stage = scratch[2 * j : 2 * j + 2]
        jobs.append(WeightReduce(net, part, (), dims, local, [stage], None, True))
        jobs[-1].start()
    net.settle()
    for j, job in enumerate(jobs):
        job.wait(0)
        job.add(0, True)
        net.keep(job.cut(1, True), outs[2 * j + 1])
        job.add(0, False)
        net.keep(job.cut(1, False), outs[2 * j])
        if j == 0:
            waits += token_finish(net, first, own_all)
    arrived(waits)
    net.finish()


def row_cuts(name, rows):
    if name not in ("up", "down") or rows % 16 or rows < 128:
        return [(0, rows)]
    first = rows // 32 * 16
    return [(0, first), (first, rows - first)]


PARTS = ("up", "forget", "out", "down", "gate", "in")


def cast_rows(out, src):
    rows = src.shape[0]
    tile = 16 if rows % 16 == 0 else rows

    def body(i, _):
        at = pl.ds(pl.multiple_of(i * tile, tile), tile)
        out[at, :] = src[at, :].astype(out.dtype)
        return 0

    lax.fori_loop(0, rows // tile, body, 0)


class TokenReduce:
    def __init__(self, net, blocks, got_x, got_z, room, other):
        lay = net.lay
        self.net, self.room, self.other, self.got_z = net, room, other, got_z
        self.first = [net.put(blocks.at[3], other, lay.X), net.put(blocks.at[1], got_x, lay.X)]
        self.loaded = net.load(blocks.at[2], room)

    def pass_on(self):
        self.first[0].wait_recv()
        self.loaded.wait()
        add_rows(self.room, self.room, self.other)
        self.last = self.net.put(self.room, self.got_z, self.net.lay.ZL)

    def end(self):
        arrived([self.first[1], self.last])


def first_stage(name):
    return 1 if name in ("up", "down") else 0


def part_dims(lay, name):
    y_bits = list(reversed(lay.ybits))
    if name == "forget":
        return y_bits + [lay.C, lay.ZH]
    if name in ("up", "down"):
        return [lay.C] + y_bits + [lay.ZH]
    return [lay.ZH] + y_bits + [lay.C]


LAG = 2


def reduce_kernel(lay, *refs):
    count = len(PARTS)
    parts, refs = refs[:count], refs[count:]
    (up_came, down_leaves, du, mixed, vectors), refs = refs[:5], refs[5:]
    outs, refs = refs[:count], refs[count:]
    (du_x, du_z, mixed_x, mixed_z, all_vectors), refs = refs[:5], refs[5:]
    token_rooms, refs = refs[:4], refs[4:]
    scratch, (send_sems, recv_sems, local_sems) = list(refs[:-3]), refs[-3:]
    net = Net(lay, list(range(1, lay.n)), send_sems, recv_sems, local_sems)
    me = net.me
    jobs, places, turns, waits = [], [], [], []
    for name, part, out in zip(PARTS, parts, outs):
        for first, rows in row_cuts(name, part.shape[-2]):
            local = scratch.pop(0)
            stages = [scratch.pop(0) for _ in lay.rbits[first_stage(name) :]]
            whole = rows == part.shape[-2]
            at = () if whole else (pl.ds(first, rows),)
            relative = name in ("up", "down")
            dims = part_dims(lay, name)
            jobs.append(
                WeightReduce(
                    net,
                    part,
                    at,
                    dims,
                    local,
                    stages,
                    scratch.pop(0),
                    relative,
                    down_leaves if name == "down" else None,
                    up_came if name == "up" else None,
                )
            )
            places.append((name, out if whole else out.at[pl.ds(first, rows)]))
    flows = [[] for _ in lay.rbits]
    late = []
    for job, (name, _) in zip(jobs, places):
        if name in ("gate", "in"):
            late.append(job)
        else:
            job.start()
            if name == "down":
                flows[1].append(job)
    du_sum = TokenReduce(net, du, du_x, du_z, *token_rooms[:2])

    def finish(i):
        total = jobs[i].total
        name, out = places[i]
        if name == "forget":
            turns.append(Turn(net, forget_from(lay, me), total, out))
        elif name == "out":
            rows = total.shape[0] // 4
            mine = t_slot(lay, me)

            def cut(slot):
                return total.at[pl.ds(pl.multiple_of(slot * rows, rows), rows)]

            run = total.shape[1] // (2 * lay.Y)
            if run % LANES:
                net.keep(cut(mine), out.at[mine])
                for m in lay.tmasks[1:]:
                    waits.append(net.put(cut(t_slot(lay, lay.flip(me, m))), out.at[mine], m))
                return
            for block in range(2 * lay.Y):
                zhi, y = block // lay.Y, block % lay.Y
                start = (((zhi * 2 + mine // 2) * lay.Y + y) * 2 + mine % 2) * run
                there = out.at[:, pl.ds(pl.multiple_of(start, LANES), run)]
                lanes_here = pl.ds(block * run, run)

                def piece(slot):
                    return total.at[pl.ds(pl.multiple_of(slot * rows, rows), rows), lanes_here]

                net.keep(piece(mine), there)
                for m in lay.tmasks[1:]:
                    waits.append(net.put(piece(t_slot(lay, lay.flip(me, m))), there, m))
        else:
            net.keep(total, out)

    depth = len(lay.rbits)
    for tick in range(len(jobs) + depth):
        for k in range(depth + 1):
            i = tick - k
            if not 0 <= i < len(jobs):
                continue
            job = jobs[i]
            last = depth - 1 - job.first
            if k < last:
                job.wait(k)
                job.add(k, True)
                flow = k + 1 + job.first
                if len(flows[flow]) >= LAG:
                    behind = flows[flow][-LAG]
                    behind.wait(flow - behind.first)
                job.send(k + 1)
                flows[flow].append(job)
                job.add(k, False)
            elif k == last + 1:
                job.wait(last)
                job.add(last, True)
                finish(i)
        if tick == 0:
            for job in late:
                job.start()
        if tick == 1:
            waits += [
                net.put(vectors.at[lay.flip(me, m)], all_vectors.at[me], m) for m in range(1, lay.n)
            ]
            net.keep(vectors.at[me], all_vectors.at[me])
            mixed_sum = TokenReduce(net, mixed, mixed_x, mixed_z, *token_rooms[2:])
        if tick == 3:
            du_sum.pass_on()
        if tick == 5:
            mixed_sum.pass_on()
    du_sum.end()
    mixed_sum.end()
    arrived(waits)
    for turn in turns:
        turn.wait()
    net.finish()


def sig(v):
    return 1.0 / (1.0 + jnp.exp(-v))


def lanes(base, h):
    return slice(base + h * LANES, base + (h + 1) * LANES)


def fold_rows(v):
    return jnp.sum(v.reshape(v.shape[0] // 8, 8, v.shape[1]), axis=0)


def forward_kernel(half, length, proj, keep, par, d_re, d_im, v_re, v_im, summ):
    total = d_re.shape[1]
    blocks = total // length
    tiles = half // LANES

    def terms(i, _):
        rows = pl.ds(pl.multiple_of(i * ROWS, ROWS), ROWS)
        kept = keep[rows, :]
        for h in range(tiles):
            at = slice(h * LANES, (h + 1) * LANES)
            lower = par[0:1, at]
            magnitude = lower + (1.0 - lower) * sig(proj[rows, lanes(4 * half, h)])
            rest = 1.0 - magnitude
            d_re[h, rows, :] = kept * magnitude * par[1:2, at]
            d_im[h, rows, :] = kept * magnitude * par[2:3, at]
            a = proj[rows, lanes(0, h)]
            b = proj[rows, lanes(half, h)]
            v_re[h, rows, :] = a * sig(a) * rest
            v_im[h, rows, :] = b * sig(b) * rest
        return 0

    lax.fori_loop(0, total // ROWS, terms, 0)

    def step(t, carry):
        rows = pl.ds(t, blocks, stride=length)
        out = []
        for h in range(tiles):
            p_re, p_im, s_re, s_im = carry[4 * h : 4 * h + 4]
            dr, di = d_re[h, rows, :], d_im[h, rows, :]
            out += [
                dr * p_re - di * p_im,
                dr * p_im + di * p_re,
                dr * s_re - di * s_im + v_re[h, rows, :],
                dr * s_im + di * s_re + v_im[h, rows, :],
            ]
        return tuple(out)

    zero = jnp.zeros((blocks, LANES), F32)
    ends = lax.fori_loop(0, length, step, (zero + 1.0, zero, zero, zero) * tiles, unroll=4)
    for j in range(blocks):
        summ[j, 4:8, :] = jnp.zeros((4, half), F32)
        for h in range(tiles):
            for k in range(4):
                summ[j, k : k + 1, lanes(0, h)] = ends[4 * h + k][j : j + 1, :]


def chain_blocks(half, n, blocks, ints, summ, back):
    tiles = half // LANES

    def chain(i, carry):
        p = i if back is None else n - 1 - i
        tile = summ[ints[p]]
        shift = tile[2:4, :] if back is None else back[ints[p]]
        out = []
        for h in range(tiles):
            at = slice(h * LANES, (h + 1) * LANES)
            old = carry[h * (2 + 2 * blocks) : (h + 1) * (2 + 2 * blocks)]
            c_re, c_im = old[0], old[1]
            a_re = tile[0:1, at]
            a_im = tile[1:2, at] if back is None else -tile[1:2, at]
            out.append(a_re * c_re - a_im * c_im + shift[0:1, at])
            out.append(a_re * c_im + a_im * c_re + shift[1:2, at])
            for j in range(blocks):
                here = ints[n + j] == p
                out.append(jnp.where(here, c_re, old[2 + 2 * j]))
                out.append(jnp.where(here, c_im, old[3 + 2 * j]))
        return tuple(out)

    first = summ[0]
    zero = first[0:1, 0:LANES] - first[0:1, 0:LANES]
    res = lax.fori_loop(0, n, chain, (zero,) * (tiles * (2 + 2 * blocks)))
    entry = []
    for h in range(tiles):
        old = res[h * (2 + 2 * blocks) : (h + 1) * (2 + 2 * blocks)]
        entry.append(jnp.concatenate([old[2 + 2 * j] for j in range(blocks)], axis=0))
        entry.append(jnp.concatenate([old[3 + 2 * j] for j in range(blocks)], axis=0))
    return tuple(entry)


def state_kernel(
    half, length, n, ints, summ, d_re, d_im, v_re, v_im, proj, gain,
    st_re, st_im, be_re, be_im, unit, squares,
):
    total = d_re.shape[1]
    blocks = total // length
    tiles = half // LANES

    def step(t, carry):
        rows = pl.ds(t, blocks, stride=length)
        out = []
        for h in range(tiles):
            s_re, s_im = carry[2 * h], carry[2 * h + 1]
            be_re[h, rows, :] = s_re
            be_im[h, rows, :] = s_im
            dr, di = d_re[h, rows, :], d_im[h, rows, :]
            n_re = dr * s_re - di * s_im + v_re[h, rows, :]
            n_im = dr * s_im + di * s_re + v_im[h, rows, :]
            st_re[h, rows, :] = n_re
            st_im[h, rows, :] = n_im
            out += [n_re, n_im]
        return tuple(out)

    entry = chain_blocks(half, n, blocks, ints, summ, None)
    lax.fori_loop(0, length, step, entry, unroll=4)

    def finish(i, _):
        rows = pl.ds(pl.multiple_of(i * ROWS, ROWS), ROWS)
        square = jnp.zeros((ROWS, 1), F32)
        for h in range(tiles):
            for part, st in ((0, st_re), (1, st_im)):
                v = st[h, rows, :]
                g = proj[rows, lanes((2 + part) * half, h)]
                at = lanes(part * half, h)
                unit[rows, at] = (v * gain[0:1, at] * (g * sig(g))).astype(LOW)
                square = square + jnp.sum(v * v, axis=1, keepdims=True)
        squares[rows, :] = jnp.broadcast_to(square, (ROWS, LANES))
        return 0

    lax.fori_loop(0, total // ROWS, finish, 0)


def back_kernel(
    half, length, grad_mid, st_re, st_im, proj, gain, scale, d_re, d_im,
    gs_re, gs_im, gate_low, mid, gain_grad, summ, acc,
):
    total = d_re.shape[1]
    blocks = total // length
    tiles = half // LANES
    acc[...] = jnp.zeros_like(acc)

    def terms(i, _):
        rows = pl.ds(pl.multiple_of(i * ROWS, ROWS), ROWS)
        r = scale[rows, 0:1]
        q = scale[rows, 1:2]
        for h in range(tiles):
            for part, st, gs in ((0, st_re, gs_re), (1, st_im, gs_im)):
                at = lanes(part * half, h)
                g = proj[rows, lanes((2 + part) * half, h)]
                v = st[h, rows, :]
                gv = gain[0:1, at]
                dm = grad_mid[rows, at]
                sg = sig(g)
                silu = g * sg
                du = dm * silu
                normed = v * r
                scaled = normed * gv
                mid[rows, at] = (scaled * silu).astype(LOW)
                gate_low[rows, at] = (dm * scaled * (sg * (1.0 + g * (1.0 - sg)))).astype(LOW)
                gs[h, rows, :] = du * gv * r - v * q
                acc[:, at] = acc[:, at] + fold_rows(du * normed)
        return 0

    lax.fori_loop(0, total // ROWS, terms, 0)
    gain_grad[...] = acc[...]

    def step(i, carry):
        rows = pl.ds(length - 1 - i, blocks, stride=length)
        out = []
        for h in range(tiles):
            a_re = gs_re[h, rows, :] + carry[2 * h]
            a_im = gs_im[h, rows, :] + carry[2 * h + 1]
            dr, di = d_re[h, rows, :], d_im[h, rows, :]
            out += [dr * a_re + di * a_im, dr * a_im - di * a_re]
        return tuple(out)

    zero = jnp.zeros((blocks, LANES), F32)
    ends = lax.fori_loop(0, length, step, (zero, zero) * tiles, unroll=4)
    for j in range(blocks):
        summ[j, 2:8, :] = jnp.zeros((6, half), F32)
        for h in range(tiles):
            for k in range(2):
                summ[j, k : k + 1, lanes(0, h)] = ends[2 * h + k][j : j + 1, :]


def adjoint_kernel(
    half, length, n, ints, summ, back, gs_re, gs_im, d_re, d_im, be_re, be_im, proj, keep, par, gate_low,
    grads, lower_grad, angle_grad, ad_re, ad_im, acc,
):
    total = d_re.shape[1]
    blocks = total // length
    tiles = half // LANES

    def step(i, carry):
        rows = pl.ds(length - 1 - i, blocks, stride=length)
        out = []
        for h in range(tiles):
            a_re = gs_re[h, rows, :] + carry[2 * h]
            a_im = gs_im[h, rows, :] + carry[2 * h + 1]
            ad_re[h, rows, :] = a_re
            ad_im[h, rows, :] = a_im
            dr, di = d_re[h, rows, :], d_im[h, rows, :]
            out += [dr * a_re + di * a_im, dr * a_im - di * a_re]
        return tuple(out)

    entry = chain_blocks(half, n, blocks, ints, summ, back)
    lax.fori_loop(0, length, step, entry, unroll=4)
    acc[...] = jnp.zeros_like(acc)

    def terms(i, _):
        rows = pl.ds(pl.multiple_of(i * ROWS, ROWS), ROWS)
        kept = keep[rows, :]
        for h in range(tiles):
            at = slice(h * LANES, (h + 1) * LANES)
            lower, cos, sin = par[0:1, at], par[1:2, at], par[2:3, at]
            sf = sig(proj[rows, lanes(4 * half, h)])
            magnitude = lower + (1.0 - lower) * sf
            rest = 1.0 - magnitude
            a = proj[rows, lanes(0, h)]
            b = proj[rows, lanes(half, h)]
            sa, sb = sig(a), sig(b)
            ar, ai = ad_re[h, rows, :], ad_im[h, rows, :]
            br, bi = be_re[h, rows, :], be_im[h, rows, :]
            g_re = ar * br + ai * bi
            g_im = ai * br - ar * bi
            g_mag = kept * (g_re * cos + g_im * sin) - (ar * (a * sa) + ai * (b * sb))
            acc[0:8, at] = acc[0:8, at] + fold_rows(g_mag * (1.0 - sf))
            acc[8:16, at] = acc[8:16, at] + fold_rows(kept * magnitude * (g_im * cos - g_re * sin))
            grads[rows, lanes(0, h)] = (ar * rest * (sa * (1.0 + a * (1.0 - sa)))).astype(LOW)
            grads[rows, lanes(half, h)] = (ai * rest * (sb * (1.0 + b * (1.0 - sb)))).astype(LOW)
            grads[rows, lanes(4 * half, h)] = (g_mag * (1.0 - lower) * sf * (1.0 - sf)).astype(LOW)
        grads[rows, 2 * half : 4 * half] = gate_low[rows, :]
        return 0

    lax.fori_loop(0, total // ROWS, terms, 0)
    lower_grad[...] = acc[0:8, :]
    angle_grad[...] = acc[8:16, :]


VMEM = pl.BlockSpec(memory_space=pltpu.VMEM)
SMEM = pl.BlockSpec(memory_space=pltpu.SMEM)


def plain_call(body, outs, n_in, smem=0, scratch=(), name=None):
    return pl.pallas_call(
        body,
        out_shape=tuple(jax.ShapeDtypeStruct(s, d) for s, d in outs),
        in_specs=[SMEM] * smem + [VMEM] * (n_in - smem),
        out_specs=tuple(VMEM for _ in outs),
        scratch_shapes=list(scratch),
        compiler_params=pltpu.CompilerParams(vmem_limit_bytes=48 << 20),
        cost_estimate=estimate(7),
        name=name,
    )


def local(
    n,
    tokens,
    cotangent,
    seq_lengths,
    block_deal,
    in_proj,
    forget_proj,
    gate_proj,
    out_proj,
    ffn_gate,
    ffn_up,
    ffn_down,
    gain_mix,
    gain_out,
    gain_ffn,
    lower_bound,
    rotation,
):
    lay = Layout(n)
    Y = lay.Y
    W = n // 4
    me = lax.axis_index("dp")
    zhi, zlo, y, x, c = lay.parts(me)
    mine_t = zlo * 2 + x
    length, width = tokens.shape
    half = width // 8
    total = 4 * length
    r_in, r_f = in_proj.shape[0], forget_proj.shape[0]

    indices = jnp.arange(n, dtype=jnp.int32)
    order = jnp.sum(jnp.where(block_deal[None, :] == indices[:, None], indices[None, :], 0), axis=1)
    t_devices = jnp.stack([lay.flip(me, m) for m in lay.tmasks])
    t_places = jnp.sum(
        jnp.where(t_devices[:, None] == indices[None, :], block_deal[None, :], 0), axis=1
    )
    o_parts = lay.parts(order)
    t_rel = ((o_parts[1] + zlo) % 2) * 2 + (o_parts[3] + x) % 2
    ints = jnp.concatenate([w_slot(lay, order) * 4 + t_rel, t_places]).astype(jnp.int32)
    offsets = jnp.cumsum(seq_lengths) - seq_lengths
    positions = (
        t_places[:, None] * length + jnp.arange(length, dtype=jnp.int32)[None, :]
    ).reshape(-1)
    starts = jnp.any(positions[:, None] == offsets[None, :], axis=1)
    keep = jnp.where(starts, 0.0, 1.0).astype(F32)[:, None]

    packed = jnp.concatenate([gain_mix, gain_ffn, gain_out, lower_bound, rotation])
    pack_rows = -(-packed.shape[0] // 128)
    packed = jnp.pad(packed, (0, 8 * 128 - packed.shape[0])).reshape(8, 128)
    out_cols = out_proj.astype(LOW).reshape(r_in, 2, 2, Y, 2, 2 * r_in)
    out_cols = out_cols.transpose(2, 4, 0, 1, 3, 5).reshape(2, 2, r_in, 2 * half)
    units = r_in // r_f
    r_ffn = ffn_gate.shape[0]
    cuts = row_cuts("up", r_ffn)
    tok_all, w_mix, _, _, w_out, gate_za, every, f_gate, f_up, f_down, up_a, *gate_b = net_call(
        partial(start_kernel, lay, units, cuts),
        lay,
        (
            tokens,
            in_proj.astype(LOW).reshape(units, r_f, width),
            gate_proj.astype(LOW).reshape(units, r_f, width),
            forget_proj.astype(LOW).reshape(1, r_f, width),
            out_cols,
            packed,
            ffn_gate,
            ffn_up,
            ffn_down,
        ),
        [
            ((4, length, width), LOW),
            ((W * (2 * units + 1), r_f, width), LOW),
            ((1, r_f, width), LOW),
            ((2, 2, r_in, 2 * half), LOW),
            ((2, 2, Y, 2, 2, r_in, 2 * half), LOW),
            ((cuts[0][1], width), LOW),
            ((n, 8, 128), F32),
            *[((r_ffn, width), LOW)] * 3,
            *[((rows, width), LOW) for _, rows in cuts],
        ],
        4 * (W - 1) + 9 + n - 1,
        32,
        0,
        "start",
        60,
        [
            *[pltpu.VMEM((r_ffn, width), F32)] * 3,
            *[pltpu.VMEM((r_ffn, width), LOW)] * 3,
            pltpu.VMEM((units, r_f, width), LOW),
            pltpu.VMEM((units, r_f, width), LOW),
            pltpu.VMEM((length, width), LOW),
            pltpu.VMEM((1, r_f, width), LOW),
            pltpu.VMEM((2, 2, r_in, 2 * half), LOW),
        ],
    )
    cot_own = tie(cotangent, tok_all)
    cot_x, cot_z = lay.send(cot_own, lay.X), lay.send(cot_own, lay.ZL)
    gate_z = [gate_za]
    if len(cuts) > 1:
        gate_z.append(lay.send(gate_b[0], lay.ZH))
    tok_all = tok_all.reshape(total, width)
    w_mix = w_mix.reshape(5 * half, width)
    w_out = w_out.reshape(width, 2 * half)
    every = every[:, :pack_rows, :].reshape(n, pack_rows * 128)
    g_mix = every[:, 0:r_in].reshape(1, width)
    g_ffn = every[:, r_in : 2 * r_in].reshape(1, width)
    g_out = every[:, 2 * r_in : 3 * r_in].reshape(2, 2, Y, 2, 2 * r_in)
    g_out = lax.dynamic_index_in_dim(g_out, zlo, 1, keepdims=False)
    g_out = lax.dynamic_index_in_dim(g_out, x, 2, keepdims=False).reshape(1, 2 * half)

    def channels(vector):
        vector = vector.reshape(2, Y, 2, half // Y)
        vector = lax.dynamic_index_in_dim(vector, zlo, 0, keepdims=False)
        return lax.dynamic_index_in_dim(vector, x, 1, keepdims=False).reshape(1, half)

    lower = channels(every[:, 3 * r_in : 3 * r_in + r_f])
    angle = channels(every[:, 3 * r_in + r_f : 3 * r_in + 2 * r_f])
    par = jnp.concatenate(
        [lower, jnp.cos(angle), jnp.sin(angle), jnp.zeros((5, half), F32)], axis=0
    )

    inputs = tokens.astype(F32)
    r_tok = lax.rsqrt(jnp.mean(inputs * inputs, axis=-1, keepdims=True) + EPS)
    all32 = tok_all.astype(F32)
    r_all = lax.rsqrt(jnp.mean(all32 * all32, axis=-1, keepdims=True) + EPS)
    normed = (all32 * r_all * g_mix).astype(LOW)
    proj = contract(normed, w_mix)
    wide = ((half // LANES, total, LANES), F32)
    d_re, d_im, v_re, v_im, summ = plain_call(
        partial(forward_kernel, half, length),
        [wide] * 4 + [((4, 8, half), F32)],
        3,
        name="gates",
    )(proj, keep, par)
    summ = tie(summ, gate_z[-1], cot_x, cot_z)
    summ_all = small_gather(lay, summ, lay.wmasks, partial(w_slot, lay), W, 1)
    cot_blocks = [cotangent, cot_x, cot_z, lay.send(tie(cot_z, summ_all), lay.X)]
    up_z = [lay.send(tie(up_a, summ_all), lay.ZH)]
    st_re, st_im, be_re, be_im, unit, squares = plain_call(
        partial(state_kernel, half, length, n),
        [wide] * 4 + [((total, 2 * half), LOW), ((total, LANES), F32)],
        8,
        smem=1,
        name="states",
    )(ints, summ_all, d_re, d_im, v_re, v_im, proj, g_out)
    branch_low = tie(contract(unit, w_out).astype(LOW), up_z[0])

    def t_blocks(value):
        return [value[j * length : (j + 1) * length] for j in range(4)]

    branch_x, branch_z, got_squares, w_ffn_gate, down_y, down_z, *up_zb = net_call(
        partial(branch_kernel, lay, cuts),
        lay,
        (
            branch_low.reshape(4, length, width),
            squares.reshape(4, length, LANES),
            f_gate,
            f_up,
            f_down,
            *gate_z,
        ),
        [
            ((length, width), LOW),
            ((length, width), LOW),
            ((3, length, LANES), F32),
            ((W, r_ffn, width), LOW),
            ((r_ffn, width), LOW),
            ((cuts[0][1], width), LOW),
        ]
        + [((rows, width), LOW) for _, rows in cuts[1:]],
        2 * W + 10,
        12,
        4,
        "branch",
        40,
        [pltpu.VMEM((length, width), LOW)] * 2
        + [pltpu.VMEM((rows, width), LOW) for _, rows in cuts for _ in range(2)],
    )
    w_ffn_gate = w_ffn_gate.reshape(W * r_ffn, width)

    def own_sum(whole, arrived_parts):
        value = whole[:length].astype(F32)
        for part in arrived_parts:
            value = value + part.astype(F32)
        return value

    square = own_sum(squares, [got_squares[j] for j in range(3)])[:, 0:1]
    branch = own_sum(branch_low, (branch_x, branch_z))
    r_state = lax.rsqrt(square / width + EPS)
    residual = inputs + r_state * branch
    r_res = lax.rsqrt(jnp.mean(residual * residual, axis=-1, keepdims=True) + EPS)
    ffn_low = (residual * r_res * g_ffn).astype(LOW)

    tok_room = pltpu.VMEM((length, width), LOW)
    rooms = [pltpu.VMEM((rows, width), LOW) for _, rows in cuts]
    last = len(cuts) - 1
    down_rooms = [[room] * (3 if i == 0 else 2) for i, room in enumerate(rooms)]
    ffn_all, w_ffn_up, w_down, cot_all = net_call(
        partial(ffn_kernel, lay, cuts),
        lay,
        (ffn_low, f_up, f_down, down_y, down_z, *up_z, *up_zb, *cot_blocks),
        [
            ((4, length, width), LOW),
            ((W, r_ffn, width), LOW),
            ((W, r_ffn, width), LOW),
            ((4, length, width), LOW),
        ],
        4 * W + 8,
        32,
        5,
        "ffn_in",
        40,
        down_rooms[last]
        + [tok_room]
        + [room for i in range(last) for room in down_rooms[i]]
        + [room for room in rooms for _ in range(2)]
        + [tok_room] * 4,
    )
    ffn_all = ffn_all.reshape(total, width)
    w_ffn_up = w_ffn_up.reshape(W * r_ffn, width)
    w_down = w_down.reshape(W * r_ffn, width)
    cot_all = cot_all.reshape(total, width)
    gate_value = contract(ffn_all, w_ffn_gate)
    up_value = contract(ffn_all, w_ffn_up)
    s_gate = jax.nn.sigmoid(gate_value)
    silu_gate = gate_value * s_gate
    hidden_low = (silu_gate * up_value).astype(LOW)
    grad_hidden = contract(cot_all, w_down)
    grad_gate = (grad_hidden * up_value * s_gate * (1.0 + gate_value * (1.0 - s_gate))).astype(LOW)
    grad_up = (grad_hidden * silu_gate).astype(LOW)
    du_low = (
        jnp.dot(grad_gate, w_ffn_gate, preferred_element_type=F32)
        + jnp.dot(grad_up, w_ffn_up, preferred_element_type=F32)
    ).astype(LOW)
    du_blocks = t_blocks(du_low)
    du_got = [lay.send(b, m) for b, m in zip(du_blocks[1:], lay.tmasks[1:])]
    du = du_blocks[0].astype(F32)
    for got in du_got:
        du = du + got.astype(F32)

    def join(kept, got):
        return kept.astype(F32) + got.astype(F32)

    def split_sum(kept, got):
        rows = kept.shape[0] // 2
        return join(kept[:rows], got[:rows]).astype(LOW), join(kept[rows:], got[rows:]).astype(LOW)

    def over_y(kept, away):
        for bit in lay.ybits:
            kept, away = split_sum(kept, lay.send(away, bit))
        return kept, away

    left_gate, left_up, left_hidden, *_ = lax.optimization_barrier(
        (grad_gate, grad_up, hidden_low, *du_blocks)
    )
    gate_part = outer_rows(left_gate, ffn_all).astype(LOW)
    up_part = outer_rows(left_up, ffn_all).astype(LOW)
    down_part = outer_rows(left_hidden, cot_all).astype(LOW)
    mixed_low = jnp.dot(tie(left_hidden, du_got[0]), w_down, preferred_element_type=F32).astype(LOW)

    du_gain = du * g_ffn
    grad_residual = (
        cotangent.astype(F32)
        + r_res * du_gain
        - residual * (r_res * r_res * r_res) * jnp.mean(residual * du_gain, axis=-1, keepdims=True)
    )
    ffn_gain_part = jnp.sum(du * residual * r_res, axis=0)
    grad_low = tie(grad_residual.astype(LOW), mixed_low)
    inner = jnp.sum(grad_low.astype(F32) * branch, axis=-1, keepdims=True) / width
    scale = jnp.where(
        jnp.arange(LANES)[None, :] == 0, r_state, r_state * r_state * r_state * inner
    )

    split = (2,) * len(lay.wbits)
    block = (r_ffn, width)
    grad_all, scale_all, gate_kept, gate_away, up_kept, up_away, down_kept, down_away = net_call(
        partial(grad_kernel, lay),
        lay,
        (grad_low, scale, *[part.reshape(split + block) for part in (gate_part, up_part, down_part)]),
        [((4, length, width), LOW), ((4, length, LANES), F32)] + [(split[2:] + block, LOW)] * 6,
        10,
        13,
        6,
        "grad_in",
        27,
        [pltpu.VMEM((length, width), LOW), pltpu.VMEM((length, LANES), F32)]
        + [pltpu.VMEM(split[1:] + block, LOW)] * 6,
    )
    gate_kept, gate_away = over_y(gate_kept.reshape(-1, width), gate_away.reshape(-1, width))
    grad_all = grad_all.reshape(total, width)
    scale_all = scale_all.reshape(total, LANES)
    grad_mid = jnp.dot(grad_all, w_out, preferred_element_type=F32)
    gs_re, gs_im, gate_low, mid, out_gain_part, back = plain_call(
        partial(back_kernel, half, length),
        [wide] * 2
        + [((total, 2 * half), LOW)] * 2
        + [((8, 2 * half), F32), ((4, 8, half), F32)],
        8,
        scratch=[pltpu.VMEM((8, 2 * half), F32)],
        name="back_gates",
    )(grad_mid, st_re, st_im, proj, g_out, scale_all, d_re, d_im)
    back_all = tie(small_gather(lay, back, lay.wmasks, partial(w_slot, lay), W, 2), gate_away)
    grads, lower_part, angle_part = plain_call(
        partial(adjoint_kernel, half, length, n),
        [((total, 5 * half), LOW), ((8, half), F32), ((8, half), F32)],
        13,
        smem=1,
        scratch=[pltpu.VMEM((half // LANES, total, LANES), F32)] * 2 + [pltpu.VMEM((16, half), F32)],
        name="adjoints",
    )(ints, summ_all, back_all, gs_re, gs_im, d_re, d_im, be_re, be_im, proj, keep, par, gate_low)
    du_mix_low = jnp.dot(grads, w_mix, preferred_element_type=F32).astype(LOW)
    mix_gain_part = jnp.sum(
        du_mix_low.astype(F32) * (all32 * r_all), axis=0
    )

    t_hot = ((jnp.arange(2)[:, None] == zlo) & (jnp.arange(2)[None, :] == x)).astype(F32)
    out_gain_part = jnp.sum(out_gain_part, axis=0).reshape(2, 1, Y, 1, 2 * r_in)
    out_gain_part = (out_gain_part * t_hot[None, :, None, :, None]).reshape(n, r_in)

    def spread(vector):
        vector = jnp.sum(vector, axis=0).reshape(1, Y, 1, half // Y)
        return (vector * t_hot[:, None, :, None]).reshape(n, r_f)

    to_owner = jnp.concatenate(
        [
            mix_gain_part.reshape(n, r_in),
            ffn_gain_part.reshape(n, r_in),
            out_gain_part,
            spread(lower_part),
            spread(angle_part),
        ],
        axis=1,
    )
    to_owner = jnp.pad(to_owner, ((0, 0), (0, 1024 - to_owner.shape[1]))).reshape(n, 8, 128)

    grad_w_out = outer_rows(grad_all, mid).astype(LOW).reshape(2, 2, Y, 2, 2, r_in, 2 * half)
    grad_w_out = grad_w_out.transpose(0, 2, 4, 1, 3, 5, 6).reshape(W, 4 * r_in, 2 * half)
    gate_got = lay.send(tie(gate_away, back_all), lay.ZH)
    up_came = lay.send(tie(up_away, gate_away, back_all), lay.ybits[0])
    du_mix_low = tie(du_mix_low, gate_got)
    part_of = {
        "forget": outer_rows(grads[:, 4 * half :], normed).astype(LOW).reshape(split + (r_f, width)),
        "out": grad_w_out.reshape(split + (4 * r_in, 2 * half)),
        "up": up_kept,
        "down": down_kept,
        "gate": outer_rows(gate_low, normed).astype(LOW).reshape(split + (r_in, width)),
        "in": outer_rows(grads[:, : 2 * half], normed).astype(LOW).reshape(split + (r_in, width)),
    }
    out_of = {name: (part.shape[-2:], F32) for name, part in part_of.items()}
    in_place = 2 * r_in % LANES == 0
    out_of["out"] = ((r_in, width) if in_place else (4, r_in, 2 * half), F32)
    parts = [part_of[name] for name in PARTS]
    scratch, copies, local_copies = [pltpu.VMEM((length, width), LOW)] * 4, 18 + n, 12
    for name, part in zip(PARTS, parts):
        for _, rows in row_cuts(name, part.shape[-2]):
            shape, skip = (rows, part.shape[-1]), first_stage(name)
            scratch.append(pltpu.VMEM(split[1 + skip :] + shape, LOW))
            for k in range(skip, len(split)):
                scratch.append(pltpu.VMEM(split[1 + k :] + shape, LOW))
            scratch.append(pltpu.VMEM(shape, F32))
            copies += len(split)
            local_copies += 3
    *sums, du_x, du_z, mixed_x, mixed_z, owned = net_call(
        partial(reduce_kernel, lay),
        lay,
        (
            *parts,
            up_came,
            down_away,
            du_mix_low.reshape(4, length, width),
            mixed_low.reshape(4, length, width),
            to_owner,
        ),
        [
            *[out_of[name] for name in PARTS],
            *[((length, width), LOW)] * 4,
            ((n, 8, 128), F32),
        ],
        copies,
        local_copies,
        3,
        "reduce",
        120,
        scratch,
    )
    ffn_gate_grad = join(gate_kept, gate_got)
    sum_of = dict(zip(PARTS, sums))
    out_proj_grad = sum_of["out"]
    if not in_place:
        out_proj_grad = out_proj_grad.reshape(2, 2, r_in, 2, Y, 2 * r_in)
        out_proj_grad = out_proj_grad.transpose(2, 3, 0, 4, 1, 5).reshape(r_in, width)
    owned = jnp.sum(owned, axis=0).reshape(-1)
    mixed_out = (residual + own_sum(mixed_low, (mixed_x, mixed_z))).astype(LOW)
    du_mix = own_sum(du_mix_low, (du_x, du_z))
    dg_mix = du_mix * g_mix
    tokens_grad = (
        grad_residual
        + r_tok * dg_mix
        - inputs * (r_tok * r_tok * r_tok) * jnp.mean(inputs * dg_mix, axis=-1, keepdims=True)
    ).astype(LOW)
    return (
        mixed_out,
        tokens_grad,
        sum_of["in"],
        sum_of["forget"],
        sum_of["gate"],
        out_proj_grad,
        ffn_gate_grad,
        sum_of["up"],
        sum_of["down"],
        owned[0:r_in],
        owned[2 * r_in : 3 * r_in],
        owned[r_in : 2 * r_in],
        owned[3 * r_in : 3 * r_in + r_f],
        owned[3 * r_in + r_f : 3 * r_in + 2 * r_f],
    )


def solution(mesh):
    rows, vector = P("dp", None), P("dp")
    in_specs = (rows, rows, P(), P()) + (rows,) * 7 + (vector,) * 5
    out_specs = (rows,) * 9 + (vector,) * 5
    return jax.shard_map(
        partial(local, mesh.shape["dp"]),
        mesh=mesh,
        in_specs=in_specs,
        out_specs=out_specs,
        check_vma=False,
    )
```
